32 devices in a mesh: rep: 8 (over y, x, core), shard: 4 (over z).
Axes of the slice: x: 2, y: 2, z: 4, core: 2. Of those that a mesh axis runs over, the one named last changes fastest.
Arguments:
- block_in: float32 [4096, 1024], P(('rep', 'shard')), may hold values from -6 to 6
- cotangent: float32 [4096, 1024], P(('rep', 'shard')), may hold values from -0.09375 to 0.09375
- segments: int32 [8, 512], P('rep'), may hold values from 0 to 3, never falling along the last dimension, each value on 1 to 224 neighbouring positions
- qkv_weight: float32 [1024, 3072], P(('rep', 'shard')), may hold values from -0.1875 to 0.1875
- out_weight: float32 [1024, 1024], P(('rep', 'shard')), may hold values from -0.75 to 0.75
- up_weight: float32 [1024, 4096], P(('rep', 'shard')), may hold values from -0.1875 to 0.1875
- down_weight: float32 [4096, 1024], P(('rep', 'shard')), may hold values from -0.09375 to 0.09375
- vectors: float32 [13, 1024], P(None, ('rep', 'shard')), may hold values from -0.9 to 1.5, as said below
- first_qkv: float32 [1024, 3072], P(('rep', 'shard')), may hold values from -1.8 to 1.8
- first_out: float32 [1024, 1024], P(('rep', 'shard')), may hold values from -1.8 to 1.8
- first_up: float32 [1024, 4096], P(('rep', 'shard')), may hold values from -1.8 to 1.8
- first_down: float32 [4096, 1024], P(('rep', 'shard')), may hold values from -1.8 to 1.8
- first_vec: float32 [13, 1024], P(None, ('rep', 'shard')), may hold values from -1.8 to 1.8
- second_qkv: float32 [1024, 3072], P(('rep', 'shard')), may hold values from 0.002 to 0.2
- second_out: float32 [1024, 1024], P(('rep', 'shard')), may hold values from 0.002 to 0.2
- second_up: float32 [1024, 4096], P(('rep', 'shard')), may hold values from 0.002 to 0.2
- second_down: float32 [4096, 1024], P(('rep', 'shard')), may hold values from 0.002 to 0.2
- second_vec: float32 [13, 1024], P(None, ('rep', 'shard')), may hold values from 0.002 to 0.2
Outputs:
- block_out: float32 [4096, 1024], P(('rep', 'shard'))
- grad_input: float32 [4096, 1024], P(('rep', 'shard'))
- grad_qkv: float32 [1024, 3072], P(('rep', 'shard'))
- grad_out: float32 [1024, 1024], P(('rep', 'shard'))
- grad_up: float32 [1024, 4096], P(('rep', 'shard'))
- grad_down: float32 [4096, 1024], P(('rep', 'shard'))
- grad_vec: float32 [13, 1024], P(None, ('rep', 'shard'))
- new_qkv: float32 [1024, 3072], P(('rep', 'shard'))
- new_out: float32 [1024, 1024], P(('rep', 'shard'))
- new_up: float32 [1024, 4096], P(('rep', 'shard'))
- new_down: float32 [4096, 1024], P(('rep', 'shard'))
- new_vec: float32 [13, 1024], P(None, ('rep', 'shard'))
- new_first_qkv: float32 [1024, 3072], P(('rep', 'shard'))
- new_first_out: float32 [1024, 1024], P(('rep', 'shard'))
- new_first_up: float32 [1024, 4096], P(('rep', 'shard'))
- new_first_down: float32 [4096, 1024], P(('rep', 'shard'))
- new_first_vec: float32 [13, 1024], P(None, ('rep', 'shard'))
- new_second_qkv: float32 [1024, 3072], P(('rep', 'shard'))
- new_second_out: float32 [1024, 1024], P(('rep', 'shard'))
- new_second_up: float32 [1024, 4096], P(('rep', 'shard'))
- new_second_down: float32 [4096, 1024], P(('rep', 'shard'))
- new_second_vec: float32 [13, 1024], P(None, ('rep', 'shard'))
The draws below stay inside these ranges and needn't reach their ends.
Inputs may be any that keep to these rules, and one draw needn't show every extreme that they name: `segments`: in every row the segment numbers never fall; each of the 4 numbers covers 1 to 224 consecutive positions and one covers exactly 224. `vectors`: rows 0 and 2 lie in 0.5 to 1.5.
All inputs are finite; a program needn't handle non-finite values.
Results may differ from the reference program's by a relative error of at most 0.019.
The reference program's roundings to bfloat16 on the way count: a program that leaves them out, or rounds other values in their place, can miss the bound.
Values may be sent and summed in bfloat16 or wider, within the bound.
No kernel may reach another device: no remote copies, remote signals or barrier semaphores. Data moves between devices by JAX's collectives and lax.ppermute only.
A program may use at most 320 MiB of HBM per device.

```python
import math
import jax
import jax.numpy as jnp
import numpy as np
from jax import lax

D = 1024
HEADS = 16
FF = 4096
ROT = 16
DOCS = 4
STEP = 10
SEQ = 512
TOKENS = 4096
DOC_MOST = 224
VROWS = 13
N_REP = 8


def draw_vectors(key, part):
    gain_key, shift_key = jax.random.split(jax.random.fold_in(key, 7))
    gains = jax.random.uniform(gain_key, (VROWS, D), jnp.float32, 0.5, 1.5)
    shifts = 0.3 * jax.random.truncated_normal(shift_key, -3.0, 3.0, (VROWS, D), jnp.float32)
    row_ids = jnp.arange(VROWS)[:, None]
    is_gain = (row_ids == 0) | (row_ids == 2)
    return jnp.where(is_gain, gains, shifts).astype(jnp.float32)


def block_levels(rng, extent, cuts, least, high):
    loudness = 1.0
    for dim, parts in cuts:
        draws = jax.random.uniform(jax.random.fold_in(jax.random.fold_in(rng, 6), dim), (parts,), jnp.float32, least / len(cuts), high / len(cuts))
        loudness = loudness * jnp.repeat(jnp.exp(draws), extent[dim] // parts).reshape((-1,) + (1,) * (len(extent) - 1 - dim))
    return loudness


def profile(count, total, limit, slope):
    loads = [(1 << 20) // math.isqrt(rank ** slope) + 1 for rank in range(2, count + 1)]
    surplus, holding = total - limit - (count - 1), [1] * (count - 1)
    while surplus > 0:
        candidates = [i for i in range(count - 1) if holding[i] < limit]
        mass, left = sum([loads[i] for i in candidates]), surplus
        for i in candidates:
            more = min(limit - holding[i], max(1, left * loads[i] // mass), surplus)
            holding[i] = holding[i] + more
            surplus = surplus - more
    return np.array([limit] + holding)


def ragged_sizes(rng, amount, total, limit, slope):
    if amount == 2:
        one = jax.random.randint(rng, (), max(1, total - limit), min(limit, total - 1) + 1)
        return jnp.stack([one, total - one])
    tallies = jnp.asarray(profile(amount, total, limit, slope), jnp.int32)
    twos = (amount - 1) // 2
    donor, sink = tallies[1:1 + 2 * twos:2], tallies[2:2 + 2 * twos:2]
    margin = jnp.minimum(donor - 1, limit - sink)
    passed = jax.random.randint(jax.random.fold_in(rng, 1), (twos,), 0, 1 << 20) % (margin + 1)
    tallies = tallies.at[1:1 + 2 * twos:2].set(donor - passed).at[2:2 + 2 * twos:2].set(sink + passed)
    return tallies[jax.random.permutation(jax.random.fold_in(rng, 2), amount)]


def centred(stream_key, dims, scale, limit, pieces=(), dtype=jnp.bfloat16):
    values = scale * jax.random.normal(stream_key, dims, jnp.float32)
    if pieces:
        values = values * block_levels(stream_key, dims, pieces, -0.22, 0.18)
    return jnp.clip(values, -limit, limit).astype(dtype)


def setup_inputs(seed: int = 0) -> dict:
    seeds = jax.random.split(jax.random.key(seed), 19)
    return {
        "block_in": centred(seeds[0], (TOKENS, D), 1.0, 6.0, ((0, 32),), jnp.float32),
        "cotangent": centred(seeds[1], (TOKENS, D), (1.0 / TOKENS ** 0.5), 0.09375, ((0, 32),), jnp.float32),
        "segments": jax.vmap(lambda own: jnp.searchsorted(jnp.cumsum(ragged_sizes(own, DOCS, SEQ, DOC_MOST, 0)), jnp.arange(SEQ), side="right"))(jax.random.split(seeds[2], N_REP)).reshape((N_REP, SEQ)).astype(jnp.int32),
        "qkv_weight": centred(seeds[3], (D, 3 * D), D ** -0.5, 0.1875, ((0, 32),), jnp.float32),
        "out_weight": centred(seeds[4], (D, D), (D // 16) ** -0.5, 0.75, ((0, 32),), jnp.float32),
        "up_weight": centred(seeds[5], (D, FF), D ** -0.5, 0.1875, ((0, 32),), jnp.float32),
        "down_weight": centred(seeds[6], (FF, D), FF ** -0.5, 0.09375, ((0, 32),), jnp.float32),
        "vectors": draw_vectors(jax.random.fold_in(seeds[18], 71), 0),
        "first_qkv": centred(seeds[8], (D, 3 * D), 0.3, 1.8, ((0, 32),), jnp.float32),
        "first_out": centred(seeds[9], (D, D), 0.3, 1.8, ((0, 32),), jnp.float32),
        "first_up": centred(seeds[10], (D, FF), 0.3, 1.8, ((0, 32),), jnp.float32),
        "first_down": centred(seeds[11], (FF, D), 0.3, 1.8, ((0, 32),), jnp.float32),
        "first_vec": centred(seeds[12], (VROWS, D), 0.3, 1.8, ((1, 32),), jnp.float32),
        "second_qkv": jnp.clip(jnp.exp(math.log(0.2) - 4.6051702 * jax.random.uniform(seeds[13], (D, 3 * D), jnp.float32) ** block_levels(seeds[13], (D, 3 * D), ((0, 32),), -0.2, 0.2)), 0.002, 0.2),
        "second_out": jnp.clip(jnp.exp(math.log(0.2) - 4.6051702 * jax.random.uniform(seeds[14], (D, D), jnp.float32) ** block_levels(seeds[14], (D, D), ((0, 32),), -0.2, 0.2)), 0.002, 0.2),
        "second_up": jnp.clip(jnp.exp(math.log(0.2) - 4.6051702 * jax.random.uniform(seeds[15], (D, FF), jnp.float32) ** block_levels(seeds[15], (D, FF), ((0, 32),), -0.2, 0.2)), 0.002, 0.2),
        "second_down": jnp.clip(jnp.exp(math.log(0.2) - 4.6051702 * jax.random.uniform(seeds[16], (FF, D), jnp.float32) ** block_levels(seeds[16], (FF, D), ((0, 32),), -0.2, 0.2)), 0.002, 0.2),
        "second_vec": jnp.clip(jnp.exp(math.log(0.2) - 4.6051702 * jax.random.uniform(seeds[17], (VROWS, D), jnp.float32) ** block_levels(seeds[17], (VROWS, D), ((1, 32),), -0.2, 0.2)), 0.002, 0.2),
    }


LN_EPS = 1e-05
BETA_ONE = 0.9
BETA_TWO = 0.95
ADAM_EPS = 1e-08
LR_MATRIX = 0.03
LR_VECTOR = 0.2
WEIGHT_DECAY = 0.01
ROPE_BASE = 10000.0
INV_ROOT_TWO = 0.7071067811865476
INV_ROOT_TAU = 0.3989422804014327

def layer_norm(values, gain, shift):
    center = values - lax.optimization_barrier(jnp.mean(values, axis=-1, keepdims=True))
    inv_std = lax.rsqrt(lax.optimization_barrier(jnp.mean(center * center, axis=-1, keepdims=True)) + LN_EPS)
    normed = center * inv_std
    return (normed * gain + shift, normed, inv_std)

def norm_backward(upstream, normed, inv_std, gain):
    scaled = upstream * gain
    result = inv_std * (scaled - lax.optimization_barrier(jnp.mean(scaled, axis=-1, keepdims=True)) - normed * lax.optimization_barrier(jnp.mean(scaled * normed, axis=-1, keepdims=True)))
    return (result, lax.optimization_barrier(jnp.sum(upstream * normed, axis=0)), lax.optimization_barrier(jnp.sum(upstream, axis=0)))

def rope_tables(positions):
    half_rot = ROT // 2
    freqs = ROPE_BASE ** (-(2.0 * jnp.arange(half_rot).astype(jnp.float32) / ROT))
    angles = positions.astype(jnp.float32)[:, None] * freqs[None, :]
    return (jnp.cos(angles)[:, None, :], jnp.sin(angles)[:, None, :])

def rotate(heads, cosines, sines):
    half_rot = ROT // 2
    lower = heads[..., :half_rot]
    upper = heads[..., half_rot:ROT]
    return jnp.concatenate([lower * cosines - upper * sines, upper * cosines + lower * sines, heads[..., ROT:]], axis=-1)

def unrotate(heads, cosines, sines):
    half_rot = ROT // 2
    lower = heads[..., :half_rot]
    upper = heads[..., half_rot:ROT]
    return jnp.concatenate([lower * cosines + upper * sines, upper * cosines - lower * sines, heads[..., ROT:]], axis=-1)

def gelu_value(inner):
    return 0.5 * inner * (1.0 + jax.scipy.special.erf(inner * INV_ROOT_TWO))

def gelu_slope(inner):
    return 0.5 * (1.0 + jax.scipy.special.erf(inner * INV_ROOT_TWO)) + inner * jnp.exp(-0.5 * inner * inner) * INV_ROOT_TAU

def adam_update(param, grad, first, second, rate, decay):
    first_new = BETA_ONE * first + (1.0 - BETA_ONE) * grad
    second_new = BETA_TWO * second + (1.0 - BETA_TWO) * grad * grad
    first_hat = first_new / (1.0 - BETA_ONE ** STEP)
    second_hat = second_new / (1.0 - BETA_TWO ** STEP)
    return (param - rate * (first_hat / (jnp.sqrt(second_hat) + ADAM_EPS) + decay * param), first_new, second_new)

def f32(values):
    return values.astype(jnp.float32)

def reference(block_in, cotangent, segments, qkv_weight, out_weight, up_weight, down_weight, vectors, first_qkv, first_out, first_up, first_down, first_vec, second_qkv, second_out, second_up, second_down, second_vec):
    bf16 = jnp.bfloat16
    per_row = FF // D
    head_dim = D // HEADS
    score_scale = head_dim ** (-0.5)
    gain_one, shift_one, gain_two, shift_two = (vectors[0], vectors[1], vectors[2], vectors[3])
    qkv_bias = vectors[4:7].reshape(3 * D)
    out_bias = vectors[7]
    up_bias = vectors[8:8 + per_row].reshape(FF)
    down_bias = vectors[8 + per_row]
    qkv_w16 = qkv_weight.astype(bf16)
    out_w16 = out_weight.astype(bf16)
    up_w16 = up_weight.astype(bf16)
    down_w16 = down_weight.astype(bf16)
    positions = jnp.arange(SEQ).astype(jnp.int32)
    cosines, sines = rope_tables(positions)

    def one_sequence(running, inputs):
        rows_in, rows_cot, seg_row = inputs
        ln_one, normed_one, inv_one = layer_norm(rows_in, gain_one, shift_one)
        ln_two, normed_two, inv_two = layer_norm(rows_in, gain_two, shift_two)
        h_one = ln_one.astype(bf16)
        h_two = ln_two.astype(bf16)
        qkv_lin = jnp.dot(h_one, qkv_w16, preferred_element_type=jnp.float32) + qkv_bias
        up_lin = jnp.dot(h_two, up_w16, preferred_element_type=jnp.float32) + up_bias
        query16 = rotate(qkv_lin[:, :D].reshape(SEQ, HEADS, head_dim), cosines, sines).astype(bf16)
        key16 = rotate(qkv_lin[:, D:2 * D].reshape(SEQ, HEADS, head_dim), cosines, sines).astype(bf16)
        value16 = qkv_lin[:, 2 * D:].reshape(SEQ, HEADS, head_dim).astype(bf16)
        allowed = (seg_row[:, None] == seg_row[None, :]) & (positions[None, :] <= positions[:, None])
        scores = jnp.where(allowed[None], jnp.einsum('qhd,khd->hqk', f32(query16), f32(key16)) * score_scale, -jnp.inf)
        row_max = lax.optimization_barrier(jnp.max(scores, axis=-1, keepdims=True))
        expo = jnp.exp(scores - row_max)
        row_sum = lax.optimization_barrier(jnp.sum(expo, axis=-1, keepdims=True))
        log_total = row_max + jnp.log(row_sum)
        probs16 = (expo / row_sum).astype(bf16)
        mixed16 = jnp.einsum('hqk,khd->qhd', f32(probs16), f32(value16)).reshape(SEQ, D).astype(bf16)
        act16 = gelu_value(up_lin).astype(bf16)
        attn_branch = jnp.dot(mixed16, out_w16, preferred_element_type=jnp.float32) + out_bias
        mlp_branch = jnp.dot(act16, down_w16, preferred_element_type=jnp.float32) + down_bias
        rows_out = rows_in + attn_branch + mlp_branch
        upstream16 = rows_cot.astype(bf16)
        g_down = jnp.dot(act16.T, upstream16, preferred_element_type=jnp.float32)
        g_out = jnp.dot(mixed16.T, upstream16, preferred_element_type=jnp.float32)
        d_act = jnp.dot(upstream16, down_w16.T, preferred_element_type=jnp.float32)
        d_mixed = jnp.dot(upstream16, out_w16.T, preferred_element_type=jnp.float32)
        d_up = d_act * gelu_slope(up_lin)
        d_up16 = d_up.astype(bf16)
        d_mixed16 = d_mixed.astype(bf16).reshape(SEQ, HEADS, head_dim)
        g_up = jnp.dot(h_two.T, d_up16, preferred_element_type=jnp.float32)
        d_two = jnp.dot(d_up16, up_w16.T, preferred_element_type=jnp.float32)
        row_delta = lax.optimization_barrier(jnp.sum(f32(d_mixed16) * f32(mixed16.reshape(SEQ, HEADS, head_dim)), axis=-1)).T[:, :, None]
        scores_again = jnp.where(allowed[None], jnp.einsum('qhd,khd->hqk', f32(query16), f32(key16)) * score_scale, -jnp.inf)
        probs_again = jnp.exp(scores_again - log_total)
        d_probs = jnp.einsum('qhd,khd->hqk', f32(d_mixed16), f32(value16))
        d_scores16 = (probs_again * (d_probs - row_delta) * score_scale).astype(bf16)
        probs_back16 = probs_again.astype(bf16)
        d_query = jnp.einsum('hqk,khd->qhd', f32(d_scores16), f32(key16))
        d_keys = jnp.einsum('hqk,qhd->khd', f32(d_scores16), f32(query16))
        d_values = jnp.einsum('hqk,qhd->khd', f32(probs_back16), f32(d_mixed16))
        d_qkv = jnp.concatenate([unrotate(d_query, cosines, sines).reshape(SEQ, D), unrotate(d_keys, cosines, sines).reshape(SEQ, D), d_values.reshape(SEQ, D)], axis=1)
        d_qkv16 = d_qkv.astype(bf16)
        g_qkv = jnp.dot(h_one.T, d_qkv16, preferred_element_type=jnp.float32)
        d_one = jnp.dot(d_qkv16, qkv_w16.T, preferred_element_type=jnp.float32)
        dx_one, dgain_one, dshift_one = norm_backward(d_one, normed_one, inv_one, gain_one)
        dx_two, dgain_two, dshift_two = norm_backward(d_two, normed_two, inv_two, gain_two)
        rows_grad = rows_cot + dx_one + dx_two
        cot_sum = lax.optimization_barrier(jnp.sum(rows_cot, axis=0))
        g_vec = jnp.concatenate([dgain_one[None], dshift_one[None], dgain_two[None], dshift_two[None], lax.optimization_barrier(jnp.sum(d_qkv, axis=0)).reshape(3, D), cot_sum[None], lax.optimization_barrier(jnp.sum(d_up, axis=0)).reshape(per_row, D), cot_sum[None]], axis=0)
        acc_qkv, acc_out, acc_up, acc_down, acc_vec = running
        return ((acc_qkv + g_qkv, acc_out + g_out, acc_up + g_up, acc_down + g_down, acc_vec + g_vec), (rows_out, rows_grad))
    start_acc = (jnp.zeros((D, 3 * D), jnp.float32), jnp.zeros((D, D), jnp.float32), jnp.zeros((D, FF), jnp.float32), jnp.zeros((FF, D), jnp.float32), jnp.zeros((VROWS, D), jnp.float32))
    inputs = (block_in.reshape(N_REP, SEQ, D), cotangent.reshape(N_REP, SEQ, D), segments)
    grads, outputs = lax.scan(one_sequence, start_acc, inputs)
    grad_qkv, grad_out, grad_up, grad_down, grad_vec = grads
    block_out = outputs[0].reshape(N_REP * SEQ, D)
    grad_input = outputs[1].reshape(N_REP * SEQ, D)
    new_qkv, new_first_qkv, new_second_qkv = adam_update(qkv_weight, grad_qkv, first_qkv, second_qkv, LR_MATRIX, WEIGHT_DECAY)
    new_out, new_first_out, new_second_out = adam_update(out_weight, grad_out, first_out, second_out, LR_MATRIX, WEIGHT_DECAY)
    new_up, new_first_up, new_second_up = adam_update(up_weight, grad_up, first_up, second_up, LR_MATRIX, WEIGHT_DECAY)
    new_down, new_first_down, new_second_down = adam_update(down_weight, grad_down, first_down, second_down, LR_MATRIX, WEIGHT_DECAY)
    new_vec, new_first_vec, new_second_vec = adam_update(vectors, grad_vec, first_vec, second_vec, LR_VECTOR, 0.0)
    return (block_out, grad_input, grad_qkv, grad_out, grad_up, grad_down, grad_vec, new_qkv, new_out, new_up, new_down, new_vec, new_first_qkv, new_first_out, new_first_up, new_first_down, new_first_vec, new_second_qkv, new_second_out, new_second_up, new_second_down, new_second_vec)
```

```python
import jax
import jax.numpy as jnp
from jax import lax
from jax.sharding import PartitionSpec as P

D = 1024
HEADS = 16
FF = 4096
ROT = 16
STEP = 10


LN_EPS = 1e-05
BETA_ONE = 0.9
BETA_TWO = 0.95
ADAM_EPS = 1e-08
LR_MATRIX = 0.03
LR_VECTOR = 0.2
WEIGHT_DECAY = 0.01
ROPE_BASE = 10000.0
INV_ROOT_TWO = 0.7071067811865476
INV_ROOT_TAU = 0.3989422804014327


def rope_tables(positions):
    half_rot = ROT // 2
    freqs = ROPE_BASE ** (-(2.0 * jnp.arange(half_rot).astype(jnp.float32) / ROT))
    angles = positions.astype(jnp.float32)[:, None] * freqs[None, :]
    return (jnp.cos(angles)[:, None, :], jnp.sin(angles)[:, None, :])


def rotate(heads, cosines, sines):
    half_rot = ROT // 2
    lower = heads[..., :half_rot]
    upper = heads[..., half_rot:ROT]
    return jnp.concatenate(
        [lower * cosines - upper * sines, upper * cosines + lower * sines, heads[..., ROT:]],
        axis=-1,
    )


def unrotate(heads, cosines, sines):
    half_rot = ROT // 2
    lower = heads[..., :half_rot]
    upper = heads[..., half_rot:ROT]
    return jnp.concatenate(
        [lower * cosines + upper * sines, upper * cosines - lower * sines, heads[..., ROT:]],
        axis=-1,
    )


def gelu_value(inner):
    return 0.5 * inner * (1.0 + jax.scipy.special.erf(inner * INV_ROOT_TWO))


def gelu_slope(inner):
    return (
        0.5 * (1.0 + jax.scipy.special.erf(inner * INV_ROOT_TWO))
        + inner * jnp.exp(-0.5 * inner * inner) * INV_ROOT_TAU
    )


def adam_update(param, grad, first, second, rate, decay):
    first_new = BETA_ONE * first + (1.0 - BETA_ONE) * grad
    second_new = BETA_TWO * second + (1.0 - BETA_TWO) * grad * grad
    first_hat = first_new / (1.0 - BETA_ONE**STEP)
    second_hat = second_new / (1.0 - BETA_TWO**STEP)
    return (
        param - rate * (first_hat / (jnp.sqrt(second_hat) + ADAM_EPS) + decay * param),
        first_new,
        second_new,
    )


def contract_rows(left, right):
    return lax.dot_general(
        left, right, (((0,), (0,)), ((), ())), preferred_element_type=jnp.float32
    )


def contract_cols(left, right):
    return lax.dot_general(
        left, right, (((1,), (1,)), ((), ())), preferred_element_type=jnp.float32
    )


def hop(value, axis, size, mask):
    return lax.ppermute(value, axis, [(i, i ^ mask) for i in range(size)])


def pick(blocks, index, axis=0):
    return lax.dynamic_index_in_dim(blocks, index, axis, keepdims=False)


def stages(size):
    bits = size.bit_length() - 1
    found = []
    while bits > 0:
        take = 2 if bits >= 2 else 1
        bits -= take
        found.append((bits, 1 << take))
    return found


def gather_axis(own, axis, me, size):
    if size > 16:
        return lax.all_gather(own, axis)
    pieces = {0: own}
    for shift, count in stages(size):
        more = dict(pieces)
        for k in range(1, count):
            for mask, piece in pieces.items():
                more[mask ^ (k << shift)] = hop(piece, axis, size, k << shift)
        pieces = more
    whole = jnp.zeros((size,) + own.shape, own.dtype)
    for mask in range(size):
        whole = lax.dynamic_update_index_in_dim(whole, pieces[mask], me ^ mask, 0)
    return whole


def exchange_axis(blocks, axis, me, size, wire):
    got = [(0, pick(blocks, me))]
    for mask in range(1, size):
        got.append((mask, hop(pick(blocks, me ^ mask).astype(wire), axis, size, mask)))
    return got


def reduce_axis(blocks, axis, me, size, wire):
    current = blocks
    for shift, count in reversed(stages(size)):
        left = current.shape[0] // count
        view = current.reshape((left, count) + current.shape[1:])
        digit = (me >> shift) & (count - 1)
        total = pick(view, digit, 1)
        for k in range(1, count):
            sent = pick(view, digit ^ k, 1).astype(wire)
            total = total + hop(sent, axis, size, k << shift).astype(jnp.float32)
        current = total
    return current[0]


def shards(
    block_in,
    cotangent,
    segments,
    qkv_weight,
    out_weight,
    up_weight,
    down_weight,
    vectors,
    first_qkv,
    first_out,
    first_up,
    first_down,
    first_vec,
    second_qkv,
    second_out,
    second_up,
    second_down,
    second_vec,
):
    bf16 = jnp.bfloat16
    f32 = jnp.float32
    tok_count = block_in.shape[0]
    n_rep = lax.axis_size("rep")
    n_shard = lax.axis_size("shard")
    rep = lax.axis_index("rep")
    shard = lax.axis_index("shard")
    seq_len = tok_count * n_shard
    head_dim = D // HEADS
    own_heads = HEADS // n_shard
    own_feats = own_heads * head_dim
    rows = qkv_weight.shape[0]
    units = down_weight.shape[0]
    own_units = units * n_rep
    cols = vectors.shape[1]
    score_scale = head_dim ** (-0.5)

    qkv_cols = qkv_weight.astype(bf16).reshape(rows, 3, own_heads, n_shard, head_dim)
    qkv_cols = qkv_cols.transpose(3, 0, 1, 2, 4).reshape(n_shard, rows, 3 * own_feats)
    up_cols = up_weight.astype(bf16).reshape(rows, n_rep, n_shard, units)
    up_cols = up_cols.transpose(2, 0, 1, 3).reshape(n_shard, rows, own_units)
    in_cols = jnp.concatenate([qkv_cols, up_cols], axis=2)
    in_rows = jnp.zeros_like(in_cols)
    for mask, piece in exchange_axis(in_cols, "shard", shard, n_shard, bf16):
        in_rows = lax.dynamic_update_index_in_dim(in_rows, piece, shard ^ mask, 0)
    in_rows = in_rows.reshape(n_shard * rows, 3 * own_feats + own_units)

    center = block_in - jnp.mean(block_in, axis=-1, keepdims=True)
    inv_std = lax.rsqrt(jnp.mean(center * center, axis=-1, keepdims=True) + LN_EPS)
    normed = center * inv_std
    normed_seq = gather_axis(normed.astype(bf16), "shard", shard, n_shard).reshape(seq_len, D)
    normed_seq = normed_seq.astype(f32)

    vec_some = gather_axis(vectors, "shard", shard, n_shard)
    vec_all = gather_axis(vec_some, "rep", rep, n_rep)
    vec_all = vec_all.transpose(2, 0, 1, 3).reshape(vectors.shape[0], D)

    in_whole = gather_axis(in_rows, "rep", rep, n_rep).reshape(D, 3 * own_feats + own_units)
    upstream16 = gather_axis(cotangent.astype(bf16), "shard", shard, n_shard).reshape(seq_len, D)
    down_whole = gather_axis(down_weight.astype(bf16), "rep", rep, n_rep).reshape(own_units, D)
    share = head_dim // rows
    moves = []
    for device in range(n_rep * n_shard):
        head, part = device // share, device % share
        moves.append((device, ((head // n_shard) * share + part) * n_shard + head % n_shard))
    out_rows = lax.ppermute(out_weight.astype(bf16), ("rep", "shard"), moves)
    out_whole = gather_axis(out_rows, "rep", rep, n_rep).reshape(own_feats, D)

    per_row = FF // D
    gain_one, shift_one, gain_two, shift_two = (vec_all[0], vec_all[1], vec_all[2], vec_all[3])
    qkv_bias = pick(vec_all[4:7].reshape(3, own_heads, n_shard, head_dim), shard, 2).reshape(
        3 * own_feats
    )
    up_bias = pick(vec_all[8 : 8 + per_row].reshape(n_rep, n_shard, units), shard, 1).reshape(
        own_units
    )
    out_bias = vec_all[7]
    down_bias = vec_all[8 + per_row]

    h_one = (normed_seq * gain_one + shift_one).astype(bf16)
    h_two = (normed_seq * gain_two + shift_two).astype(bf16)
    qkv_whole = in_whole[:, : 3 * own_feats]
    up_whole = in_whole[:, 3 * own_feats :]
    qkv_lin = jnp.dot(h_one, qkv_whole, preferred_element_type=f32) + qkv_bias
    up_lin = jnp.dot(h_two, up_whole, preferred_element_type=f32) + up_bias

    positions = jnp.arange(seq_len)
    cosines, sines = rope_tables(positions)

    def heads_of(values):
        return values.reshape(seq_len, own_heads, head_dim)

    query16 = rotate(heads_of(qkv_lin[:, :own_feats]), cosines, sines).astype(bf16)
    key16 = rotate(heads_of(qkv_lin[:, own_feats : 2 * own_feats]), cosines, sines).astype(bf16)
    value16 = heads_of(qkv_lin[:, 2 * own_feats :]).astype(bf16)
    seg_row = segments[0]
    allowed = (seg_row[:, None] == seg_row[None, :]) & (positions[None, :] <= positions[:, None])
    scores = jnp.where(
        allowed[None],
        jnp.einsum("qhd,khd->hqk", query16, key16, preferred_element_type=f32) * score_scale,
        -jnp.inf,
    )
    row_max = jnp.max(scores, axis=-1, keepdims=True)
    expo = jnp.exp(scores - row_max)
    row_sum = jnp.sum(expo, axis=-1, keepdims=True)
    log_total = row_max + jnp.log(row_sum)
    probs16 = (expo / row_sum).astype(bf16)
    mixed16 = (
        jnp.einsum("hqk,khd->qhd", probs16, value16, preferred_element_type=f32)
        .reshape(seq_len, own_feats)
        .astype(bf16)
    )
    act16 = gelu_value(up_lin).astype(bf16)
    branches = jnp.dot(mixed16, out_whole, preferred_element_type=f32)
    branches = branches + jnp.dot(act16, down_whole, preferred_element_type=f32)
    branches = reduce_axis(
        branches.reshape(n_shard, tok_count, D), "shard", shard, n_shard, bf16
    )
    block_out = block_in + branches + out_bias + down_bias

    term_down = contract_rows(act16, upstream16)
    sum_down = reduce_axis(term_down.reshape(n_rep, units, D), "rep", rep, n_rep, bf16)
    term_out = contract_rows(mixed16, upstream16)
    sum_out = reduce_axis(term_out.reshape(n_rep, rows, D), "rep", rep, n_rep, bf16)
    grad_out = lax.ppermute(sum_out, ("rep", "shard"), [(b, a) for a, b in moves])
    grad_down = sum_down
    d_act = contract_cols(upstream16, down_whole)
    d_mixed16 = heads_of(contract_cols(upstream16, out_whole)).astype(bf16)
    d_up = d_act * gelu_slope(up_lin)
    d_up16 = d_up.astype(bf16)
    term_up = contract_rows(h_two, d_up16)
    sum_up = reduce_axis(
        term_up.reshape(n_rep, n_shard * rows, own_units), "rep", rep, n_rep, bf16
    )

    def back_rows(sums, width):
        whole = jnp.zeros((n_shard, rows, width), f32)
        blocks = sums.reshape(n_shard, rows, width)
        for mask, piece in exchange_axis(blocks, "shard", shard, n_shard, bf16):
            whole = lax.dynamic_update_index_in_dim(whole, piece.astype(f32), shard ^ mask, 0)
        return whole

    grad_up = back_rows(sum_up, own_units).reshape(n_shard, rows, n_rep, units)
    grad_up = grad_up.transpose(1, 2, 0, 3).reshape(rows, FF)

    row_delta = jnp.sum(
        d_mixed16.astype(f32) * heads_of(mixed16).astype(f32),
        axis=-1,
    ).T[:, :, None]
    probs_again = jnp.exp(scores - log_total)
    d_probs = jnp.einsum("qhd,khd->hqk", d_mixed16, value16, preferred_element_type=f32)
    d_scores16 = (probs_again * (d_probs - row_delta) * score_scale).astype(bf16)
    probs_back16 = probs_again.astype(bf16)
    d_query = jnp.einsum("hqk,khd->qhd", d_scores16, key16, preferred_element_type=f32)
    d_keys = jnp.einsum("hqk,qhd->khd", d_scores16, query16, preferred_element_type=f32)
    d_values = jnp.einsum("hqk,qhd->khd", probs_back16, d_mixed16, preferred_element_type=f32)
    d_qkv = jnp.concatenate(
        [
            unrotate(d_query, cosines, sines).reshape(seq_len, own_feats),
            unrotate(d_keys, cosines, sines).reshape(seq_len, own_feats),
            d_values.reshape(seq_len, own_feats),
        ],
        axis=1,
    )
    d_qkv16 = d_qkv.astype(bf16)
    term_qkv = contract_rows(h_one, d_qkv16)
    sum_qkv = reduce_axis(
        term_qkv.reshape(n_rep, n_shard * rows, 3 * own_feats), "rep", rep, n_rep, bf16
    )
    grad_qkv = back_rows(sum_qkv, 3 * own_feats)
    grad_qkv = grad_qkv.reshape(n_shard, rows, 3, own_heads, head_dim)
    grad_qkv = grad_qkv.transpose(1, 2, 3, 0, 4).reshape(rows, 3 * D)

    d_one = contract_cols(d_qkv16, qkv_whole)
    d_two = contract_cols(d_up16, up_whole)
    scaled = d_one * gain_one + d_two * gain_two
    scaled = reduce_axis(scaled.reshape(n_shard, tok_count, D), "shard", shard, n_shard, bf16)
    grad_input = cotangent + inv_std * (
        scaled
        - jnp.mean(scaled, axis=-1, keepdims=True)
        - normed * jnp.mean(scaled * normed, axis=-1, keepdims=True)
    )

    mine = jnp.arange(n_shard) == shard
    cot_sum = jnp.sum(cotangent, axis=0)
    bias_qkv = jnp.where(
        mine[None, None, :, None],
        jnp.sum(d_qkv, axis=0).reshape(3, own_heads, 1, head_dim),
        0.0,
    ).reshape(3, D)
    bias_up = jnp.where(
        mine[None, :, None], jnp.sum(d_up, axis=0).reshape(n_rep, 1, units), 0.0
    ).reshape(per_row, D)
    vec_terms = jnp.concatenate(
        [
            jnp.sum(d_one * normed_seq, axis=0)[None],
            jnp.sum(d_one, axis=0)[None],
            jnp.sum(d_two * normed_seq, axis=0)[None],
            jnp.sum(d_two, axis=0)[None],
            bias_qkv,
            cot_sum[None],
            bias_up,
            cot_sum[None],
        ],
        axis=0,
    )
    vec_blocks = vec_terms.reshape(vectors.shape[0], n_rep, n_shard, cols).transpose(1, 2, 0, 3)
    grad_vec = reduce_axis(
        reduce_axis(vec_blocks, "rep", rep, n_rep, f32), "shard", shard, n_shard, f32
    )

    new_qkv, new_first_qkv, new_second_qkv = adam_update(
        qkv_weight, grad_qkv, first_qkv, second_qkv, LR_MATRIX, WEIGHT_DECAY
    )
    new_out, new_first_out, new_second_out = adam_update(
        out_weight, grad_out, first_out, second_out, LR_MATRIX, WEIGHT_DECAY
    )
    new_up, new_first_up, new_second_up = adam_update(
        up_weight, grad_up, first_up, second_up, LR_MATRIX, WEIGHT_DECAY
    )
    new_down, new_first_down, new_second_down = adam_update(
        down_weight, grad_down, first_down, second_down, LR_MATRIX, WEIGHT_DECAY
    )
    new_vec, new_first_vec, new_second_vec = adam_update(
        vectors, grad_vec, first_vec, second_vec, LR_VECTOR, 0.0
    )
    return (
        block_out,
        grad_input,
        grad_qkv,
        grad_out,
        grad_up,
        grad_down,
        grad_vec,
        new_qkv,
        new_out,
        new_up,
        new_down,
        new_vec,
        new_first_qkv,
        new_first_out,
        new_first_up,
        new_first_down,
        new_first_vec,
        new_second_qkv,
        new_second_out,
        new_second_up,
        new_second_down,
        new_second_vec,
    )


def solution(mesh):
    return jax.shard_map(
        shards,
        mesh=mesh,
        in_specs=(
            P(("rep", "shard"), None),
            P(("rep", "shard"), None),
            P("rep", None),
            P(("rep", "shard"), None),
            P(("rep", "shard"), None),
            P(("rep", "shard"), None),
            P(("rep", "shard"), None),
            P(None, ("rep", "shard")),
            P(("rep", "shard"), None),
            P(("rep", "shard"), None),
            P(("rep", "shard"), None),
            P(("rep", "shard"), None),
            P(None, ("rep", "shard")),
            P(("rep", "shard"), None),
            P(("rep", "shard"), None),
            P(("rep", "shard"), None),
            P(("rep", "shard"), None),
            P(None, ("rep", "shard")),
        ),
        out_specs=(
            P(("rep", "shard"), None),
            P(("rep", "shard"), None),
            P(("rep", "shard"), None),
            P(("rep", "shard"), None),
            P(("rep", "shard"), None),
            P(("rep", "shard"), None),
            P(None, ("rep", "shard")),
            P(("rep", "shard"), None),
            P(("rep", "shard"), None),
            P(("rep", "shard"), None),
            P(("rep", "shard"), None),
            P(None, ("rep", "shard")),
            P(("rep", "shard"), None),
            P(("rep", "shard"), None),
            P(("rep", "shard"), None),
            P(("rep", "shard"), None),
            P(None, ("rep", "shard")),
            P(("rep", "shard"), None),
            P(("rep", "shard"), None),
            P(("rep", "shard"), None),
            P(("rep", "shard"), None),
            P(None, ("rep", "shard")),
        ),
        check_vma=False,
    )
```

```python
import functools

import jax
import jax.numpy as jnp
import numpy as np
from jax import lax
from jax.experimental import pallas as pl
from jax.experimental.pallas import tpu as pltpu
from jax.sharding import PartitionSpec as P

D = 1024
HEADS = 16
HEAD = D // HEADS
FF = 4096
ROT = 16
STEP = 10
LANES = 128


LN_EPS = 1e-05
BETA_ONE = 0.9
BETA_TWO = 0.95
ADAM_EPS = 1e-08
LR_MATRIX = 0.03
LR_VECTOR = 0.2
WEIGHT_DECAY = 0.01
ROPE_BASE = 10000.0
INV_ROOT_TWO = 0.7071067811865476
INV_ROOT_TAU = 0.3989422804014327
HIDDEN = -1e30
bf16 = jnp.bfloat16
f32 = jnp.float32
TILE = 256


def adam_update(param, grad, first, second, rate, decay):
    first_new = BETA_ONE * first + (1.0 - BETA_ONE) * grad
    second_new = BETA_TWO * second + (1.0 - BETA_TWO) * grad * grad
    first_hat = first_new / (1.0 - BETA_ONE**STEP)
    second_hat = second_new / (1.0 - BETA_TWO**STEP)
    return (
        param - rate * (first_hat / (jnp.sqrt(second_hat) + ADAM_EPS) + decay * param),
        first_new,
        second_new,
    )


def contract_rows(left, right):
    return lax.dot_general(left, right, (((0,), (0,)), ((), ())), preferred_element_type=f32)


def contract_cols(left, right):
    return lax.dot_general(left, right, (((1,), (1,)), ((), ())), preferred_element_type=f32)


def plain_dot(left, right):
    return jnp.dot(left, right, preferred_element_type=f32)


def rope_lanes(seq_len):
    half = ROT // 2
    freqs = (ROPE_BASE ** (-(2.0 * np.arange(half, dtype=np.float32) / ROT))).astype(np.float32)
    angles = np.arange(seq_len, dtype=np.float32)[:, None] * freqs[None, :]
    cosines, sines = np.cos(angles), np.sin(angles)
    keep = np.ones((seq_len, HEAD), np.float32)
    up = np.zeros((seq_len, HEAD), np.float32)
    down = np.zeros((seq_len, HEAD), np.float32)
    keep[:, :half], keep[:, half:ROT] = cosines, cosines
    up[:, :half] = -sines
    down[:, half:ROT] = sines
    reps = LANES // HEAD
    return np.concatenate([np.tile(t, (1, reps)) for t in (keep, up, down)], axis=1)


def turn(values, table, sign):
    half = ROT // 2
    above = pltpu.roll(values, LANES - half, 1)
    below = pltpu.roll(values, half, 1)
    moved = above * table[:, LANES : 2 * LANES] + below * table[:, 2 * LANES :]
    return values * table[:, :LANES] + sign * moved


def params(mib):
    return pltpu.CompilerParams(vmem_limit_bytes=mib << 20)


def cost(flops, count):
    return pl.CostEstimate(flops=flops, bytes_accessed=count, transcendentals=0)


def whole_spec(shape):
    return pl.BlockSpec(shape, lambda *_: (0,) * len(shape))


def columns_body(inverse, width, order_ref, x_ref, o_ref):
    for i in range(x_ref.shape[1] // width):
        there = pl.ds(pl.multiple_of(order_ref[i] * width, LANES), width)
        here = slice(i * width, (i + 1) * width)
        if inverse:
            o_ref[:, there] = x_ref[:, here]
        else:
            o_ref[:, here] = x_ref[:, there]


def order_columns(values, order, inverse=False):
    width = values.shape[1] // order.shape[0]
    if width % LANES:
        return values
    spec = whole_spec(values.shape)
    return pl.pallas_call(
        functools.partial(columns_body, inverse, width),
        out_shape=jax.ShapeDtypeStruct(values.shape, values.dtype),
        grid_spec=pltpu.PrefetchScalarGridSpec(
            num_scalar_prefetch=1, grid=(1,), in_specs=[spec], out_specs=spec
        ),
        cost_estimate=cost(0, 2 * values.size * values.dtype.itemsize),
        name="order_columns",
    )(order, values)


def blocks_body(order_ref, x_ref, o_ref):
    for i in range(o_ref.shape[0]):
        o_ref[i] = x_ref[order_ref[i]]


def order_blocks(values, order):
    spec = whole_spec(values.shape)
    return pl.pallas_call(
        blocks_body,
        out_shape=jax.ShapeDtypeStruct(values.shape, values.dtype),
        grid_spec=pltpu.PrefetchScalarGridSpec(
            num_scalar_prefetch=1, grid=(1,), in_specs=[spec], out_specs=spec
        ),
        cost_estimate=cost(0, 2 * values.size * values.dtype.itemsize),
        name="order_blocks",
    )(order, values)


def front_body(
    width, order_ref, n_ref, vec_ref, low_ref, high_ref, bias_ref, rope_ref, h1_ref, h2_ref, qkv_ref, act_ref, slope_ref
):
    j = pl.program_id(0)

    @pl.when(j == 0)
    def _():
        normed = n_ref[...].astype(f32)
        h1_ref[...] = (normed * vec_ref[0:1, :] + vec_ref[1:2, :]).astype(bf16)
        h2_ref[...] = (normed * vec_ref[2:3, :] + vec_ref[3:4, :]).astype(bf16)

    half = low_ref.shape[0]

    def product(h_ref):
        total = plain_dot(h_ref[:, :half], low_ref[...]) + plain_dot(h_ref[:, half:], high_ref[...])
        return total + bias_ref[...]

    @pl.when(j < 2)
    def _():
        lin = product(h1_ref)
        for c in range(0, TILE, LANES):
            qkv_ref[:, c : c + LANES] = turn(lin[:, c : c + LANES], rope_ref[...], 1.0).astype(bf16)

    @pl.when(j == 2)
    def _():
        qkv_ref[...] = product(h1_ref).astype(bf16)

    @pl.when(j > 2)
    def _():
        lin = product(h2_ref)
        above = 0.5 * (1.0 + lax.erf(lin * INV_ROOT_TWO))
        act = (lin * above).astype(bf16)
        slope = above + lin * jnp.exp(-0.5 * lin * lin) * INV_ROOT_TAU
        for c in range(0, TILE, LANES):
            at = (j - 3) * TILE + c
            if width % LANES == 0:
                block = at // width
                place = order_ref[order_ref.shape[0] // 2 + block] * width
                at = place + (at - block * width)
            at = pl.ds(pl.multiple_of(at, LANES), LANES)
            act_ref[:, at] = act[:, c : c + LANES]
            slope_ref[:, at] = slope[:, c : c + LANES]


def front(orders, normed, vec, low, high, bias, rope, width):
    tokens = normed.shape[0]
    half, cols = low.shape
    tiles = cols // TILE
    gaps = D
    call = pl.pallas_call(
        functools.partial(front_body, width),
        out_shape=(
            jax.ShapeDtypeStruct((tokens, D), bf16),
            jax.ShapeDtypeStruct((tokens, D), bf16),
            jax.ShapeDtypeStruct((tokens, 3 * TILE), bf16),
            jax.ShapeDtypeStruct((tokens, cols - 3 * TILE), bf16),
            jax.ShapeDtypeStruct((tokens, cols - 3 * TILE), f32),
        ),
        grid_spec=pltpu.PrefetchScalarGridSpec(
            num_scalar_prefetch=1,
            grid=(tiles,),
            in_specs=[
                whole_spec((tokens, gaps)),
                whole_spec(vec.shape),
                pl.BlockSpec((half, TILE), lambda j, o: (0, j)),
                pl.BlockSpec((half, TILE), lambda j, o: (0, j)),
                pl.BlockSpec((1, TILE), lambda j, o: (0, j)),
                whole_spec(rope.shape),
            ],
            out_specs=(
                whole_spec((tokens, D)),
                whole_spec((tokens, D)),
                pl.BlockSpec((tokens, TILE), lambda j, o: (0, jnp.minimum(j, 2))),
                whole_spec((tokens, cols - 3 * TILE)),
                whole_spec((tokens, cols - 3 * TILE)),
            ),
        ),
        compiler_params=params(40),
        cost_estimate=cost(2 * tokens * D * cols, 12 << 20),
        name="front",
    )
    return call(orders, normed, vec, low, high, bias, rope)


def hidden_body(width, order_ref, dy_ref, out_ref, down_ref, slope_ref, dmix_ref, du_ref, sum_ref):
    dy = dy_ref[...]
    dmix_ref[...] = contract_cols(dy, out_ref[...]).astype(bf16)
    for c in range(0, down_ref.shape[0], LANES):
        du = contract_cols(dy, down_ref[c : c + LANES, :]) * slope_ref[:, c : c + LANES]
        at = c
        if width % LANES == 0:
            block = c // width
            at = pl.multiple_of(order_ref[block] * width + (c - block * width), LANES)
        at = pl.ds(at, LANES)
        du_ref[:, at] = du.astype(bf16)
        sum_ref[:, at] = jnp.sum(du, axis=0, keepdims=True)


def hidden(orders, dy, out_whole, down_whole, slope, width):
    tokens = dy.shape[0]
    feats, units = out_whole.shape[0], down_whole.shape[0]
    return pl.pallas_call(
        functools.partial(hidden_body, width),
        out_shape=(
            jax.ShapeDtypeStruct((tokens, feats), bf16),
            jax.ShapeDtypeStruct((tokens, units), bf16),
            jax.ShapeDtypeStruct((1, units), f32),
        ),
        grid_spec=pltpu.PrefetchScalarGridSpec(
            num_scalar_prefetch=1,
            grid=(1,),
            in_specs=[whole_spec(a.shape) for a in (dy, out_whole, down_whole, slope)],
            out_specs=(
                whole_spec((tokens, feats)),
                whole_spec((tokens, units)),
                whole_spec((1, units)),
            ),
        ),
        compiler_params=params(40),
        cost_estimate=cost(2 * tokens * D * (feats + units), 8 << 20),
        name="hidden",
    )(orders, dy, out_whole, down_whole, slope)


def attend_body(q_ref, k_ref, v_ref, dm_ref, mask_ref, rope_ref, mix_ref, dqkv_ref, sum_ref, dk_ref, dv_ref):
    pair = pl.program_id(0)
    tokens = q_ref.shape[0]
    chunk = LANES
    scale = HEAD ** (-0.5)
    first = lax.broadcasted_iota(jnp.int32, (chunk, LANES), 1) < HEAD
    every = lax.broadcasted_iota(jnp.int32, (tokens, LANES), 1) < HEAD
    k = k_ref[...]
    v = v_ref[...]
    pairs = pl.num_programs(0)

    def columns(part):
        return pl.ds(pl.multiple_of(part * pairs * LANES + pair * LANES, LANES), LANES)

    dq_total = jnp.zeros((1, LANES), f32)
    for c in range(0, tokens, chunk):
        rows = slice(c, c + chunk)
        q = q_ref[rows, :]
        dm = dm_ref[rows, :]
        mixes, dqs, dks, dvs = [], [], [], []
        for h in range(2):
            mine = first if h == 0 else jnp.logical_not(first)
            qh = jnp.where(mine, q, jnp.zeros_like(q))
            dmh = jnp.where(mine, dm, jnp.zeros_like(dm))
            score = contract_cols(qh, k) * scale + mask_ref[rows, :]
            expo = jnp.exp(score - jnp.max(score, axis=-1, keepdims=True))
            prob = expo * (1.0 / jnp.sum(expo, axis=-1, keepdims=True))
            prob16 = prob.astype(bf16)
            mix16 = plain_dot(prob16, v).astype(bf16)
            delta = jnp.sum(dmh.astype(f32) * mix16.astype(f32), axis=-1, keepdims=True)
            d_prob = contract_cols(dmh, v)
            ds16 = (prob * (d_prob - delta) * scale).astype(bf16)
            mixes.append(mix16)
            dqs.append(plain_dot(ds16, k))
            dks.append(contract_rows(ds16, q))
            dvs.append(contract_rows(prob16, dm))
        mix_ref[rows, :] = jnp.where(first, mixes[0], mixes[1])
        dq = turn(jnp.where(first, dqs[0], dqs[1]), rope_ref[rows, :], -1.0)
        dqkv_ref[rows, columns(0)] = dq.astype(bf16)
        dq_total = dq_total + jnp.sum(dq, axis=0, keepdims=True)
        dk = jnp.where(every, dks[0], dks[1])
        dv = jnp.where(every, dvs[0], dvs[1])
        if c == 0:
            dk_ref[...] = dk
            dv_ref[...] = dv
        else:
            dk_ref[...] += dk
            dv_ref[...] += dv
    dk = turn(dk_ref[...], rope_ref[...], -1.0)
    dv = dv_ref[...]
    dqkv_ref[:, columns(1)] = dk.astype(bf16)
    dqkv_ref[:, columns(2)] = dv.astype(bf16)
    sum_ref[:, columns(0)] = dq_total
    sum_ref[:, columns(1)] = jnp.sum(dk, axis=0, keepdims=True)
    sum_ref[:, columns(2)] = jnp.sum(dv, axis=0, keepdims=True)


def attend(qkv, d_mix, mask, rope):
    tokens, feats = d_mix.shape
    pairs = feats // LANES

    def part(first):
        return pl.BlockSpec((tokens, LANES), lambda j: (0, first * pairs + j))

    return pl.pallas_call(
        attend_body,
        out_shape=(
            jax.ShapeDtypeStruct((tokens, feats), bf16),
            jax.ShapeDtypeStruct((tokens, 3 * feats), bf16),
            jax.ShapeDtypeStruct((1, 3 * feats), f32),
        ),
        grid=(pairs,),
        in_specs=[
            part(0),
            part(1),
            part(2),
            part(0),
            whole_spec(mask.shape),
            whole_spec(rope.shape),
        ],
        out_specs=(
            pl.BlockSpec((tokens, LANES), lambda j: (0, j)),
            whole_spec((tokens, 3 * feats)),
            whole_spec((1, 3 * feats)),
        ),
        scratch_shapes=[pltpu.VMEM((tokens, LANES), f32), pltpu.VMEM((tokens, LANES), f32)],
        compiler_params=params(40),
        cost_estimate=cost(60 * tokens * tokens * feats, 6 << 20),
        name="attend",
    )(qkv, qkv, qkv, d_mix, mask, rope)


def back_body(dqkv_ref, du_ref, n_ref, vec_ref, low_ref, high_ref, sent_ref, own_ref, sum_ref):
    feats = dqkv_ref.shape[1]
    weights = jnp.where(pl.program_id(0) * 2 < pl.num_programs(0), low_ref[...], high_ref[...])
    d_one = contract_cols(dqkv_ref[...], weights[:, :feats])
    d_two = contract_cols(du_ref[...], weights[:, feats:])
    scaled = d_one * vec_ref[0:1, :] + d_two * vec_ref[2:3, :]
    sent_ref[...] = scaled.astype(bf16)
    own_ref[...] = scaled[: own_ref.shape[0], :]
    normed = n_ref[...].astype(f32)
    sum_ref[0:1, :] = jnp.sum(d_one * normed, axis=0, keepdims=True)
    sum_ref[1:2, :] = jnp.sum(d_one, axis=0, keepdims=True)
    sum_ref[2:3, :] = jnp.sum(d_two * normed, axis=0, keepdims=True)
    sum_ref[3:4, :] = jnp.sum(d_two, axis=0, keepdims=True)


def back(d_qkv, d_up, normed, vec, low, high, own_rows):
    tokens = normed.shape[0]
    half, cols = low.shape
    near = half // TILE
    return pl.pallas_call(
        back_body,
        out_shape=(
            jax.ShapeDtypeStruct((tokens, D), bf16),
            jax.ShapeDtypeStruct((own_rows, D), f32),
            jax.ShapeDtypeStruct((4, D), f32),
        ),
        grid=(2 * near,),
        in_specs=[
            whole_spec(d_qkv.shape),
            whole_spec(d_up.shape),
            pl.BlockSpec((tokens, TILE), lambda j: (0, j)),
            pl.BlockSpec((4, TILE), lambda j: (0, j)),
            pl.BlockSpec((TILE, cols), lambda j: (jnp.minimum(j, near - 1), 0)),
            pl.BlockSpec((TILE, cols), lambda j: (jnp.maximum(j - near, 0), 0)),
        ],
        out_specs=(
            pl.BlockSpec((tokens, TILE), lambda j: (0, j)),
            pl.BlockSpec((own_rows, TILE), lambda j: (0, j)),
            pl.BlockSpec((4, TILE), lambda j: (0, j)),
        ),
        compiler_params=params(40),
        cost_estimate=cost(2 * tokens * D * cols, 10 << 20),
        name="back",
    )(d_qkv, d_up, normed, vec, low, high)


def hop(value, axis, size, mask):
    return lax.ppermute(value, axis, [(i, i ^ mask) for i in range(size)])


def stages(size):
    bits = size.bit_length() - 1
    found = []
    while bits > 0:
        take = 2 if bits >= 2 else 1
        bits -= take
        found.append((bits, 1 << take))
    return found


def relative_masks(size):
    masks = np.zeros((1,), np.int32)
    for shift, count in stages(size):
        masks = np.concatenate([masks ^ (k << shift) for k in range(count)])
    return masks


def gather_halves(own, axis, size, relative):
    if not relative:
        whole = lax.all_gather(own, axis)
        return whole[: size // 2], whole[size // 2 :]
    current = own[None]
    pieces = []
    for shift, count in stages(size):
        pieces = [current] + [hop(current, axis, size, k << shift) for k in range(1, count)]
        if shift:
            current = jnp.concatenate(pieces, axis=0)
    if len(pieces) == 2:
        return pieces
    middle = len(pieces) // 2
    return jnp.concatenate(pieces[:middle]), jnp.concatenate(pieces[middle:])


def reduce_relative(keep, sent, axis, size):
    for shift, count in reversed(stages(size)):
        total = keep
        for k in range(1, count):
            total = total + hop(sent[k - 1], axis, size, k << shift).astype(f32)
        if shift == 0 and len(stages(size)) == 1:
            return total
        if total.shape[0] == 1:
            return total[0]
        upper = [c for t, c in stages(size) if t > shift][-1]
        view = total.reshape((upper, total.shape[0] // upper) + total.shape[1:])
        keep, sent = view[0], [view[k].astype(bf16) for k in range(1, upper)]
    return keep


def shards(
    block_in,
    cotangent,
    segments,
    qkv_weight,
    out_weight,
    up_weight,
    down_weight,
    vectors,
    first_qkv,
    first_out,
    first_up,
    first_down,
    first_vec,
    second_qkv,
    second_out,
    second_up,
    second_down,
    second_vec,
):
    tok_count = block_in.shape[0]
    n_rep = lax.axis_size("rep")
    n_shard = lax.axis_size("shard")
    rep = lax.axis_index("rep")
    shard = lax.axis_index("shard")
    seq_len = tok_count * n_shard
    own_heads = HEADS // n_shard
    own_feats = own_heads * HEAD
    rows = qkv_weight.shape[0]
    units = down_weight.shape[0]
    own_units = units * n_rep
    n_vec, cols = vectors.shape
    groups = own_feats // LANES
    width = D // n_rep
    relative = width % LANES == 0
    masks = relative_masks(n_rep)
    if relative:
        order = rep ^ jnp.asarray(masks)
        mask_of = rep ^ jnp.arange(n_rep, dtype=jnp.int32)
        place = jnp.sum(
            jnp.where(mask_of[:, None] == jnp.asarray(masks)[None], jnp.arange(n_rep)[None], 0), axis=1
        ).astype(jnp.int32)
    else:
        order = jnp.arange(n_rep, dtype=jnp.int32)
        place = order
    orders = jnp.concatenate([order, place]).astype(jnp.int32)
    near = shard ^ jnp.arange(n_shard, dtype=jnp.int32)

    qkv_cols = qkv_weight.astype(bf16).reshape(rows, 3 * groups, n_shard, LANES)
    up_cols = up_weight.astype(bf16).reshape(rows, n_rep, n_shard, units)
    in_cols = jnp.concatenate(
        [
            qkv_cols.transpose(2, 0, 1, 3).reshape(n_shard, rows, 3 * own_feats),
            up_cols.transpose(2, 0, 1, 3).reshape(n_shard, rows, own_units),
        ],
        axis=2,
    )
    in_cols = order_blocks(in_cols, near)
    in_rows = jnp.stack(
        [in_cols[0]] + [hop(in_cols[k], "shard", n_shard, k) for k in range(1, n_shard)]
    )
    in_rows = order_blocks(in_rows, near).reshape(n_shard * rows, 3 * own_feats + own_units)

    center = block_in - jnp.mean(block_in, axis=-1, keepdims=True)
    inv_std = lax.rsqrt(jnp.mean(center * center, axis=-1, keepdims=True) + LN_EPS)
    normed = center * inv_std
    normed_own = order_columns(normed.astype(bf16), order)
    normed_seq = jnp.concatenate(
        [normed_own] + [hop(normed_own, "shard", n_shard, k) for k in range(1, n_shard)], axis=0
    )

    vec_all = vectors
    vec_all = jnp.stack(
        [vec_all] + [hop(vec_all, "shard", n_shard, k) for k in range(1, n_shard)], axis=0
    )
    vec_low, vec_high = gather_halves(vec_all, "rep", n_rep, relative)
    vec_all = jnp.concatenate([vec_low, vec_high], axis=0).reshape(
        n_rep * n_shard, n_vec, cols
    )
    flat = jnp.arange(n_rep * n_shard, dtype=jnp.int32)
    vec_all = order_blocks(vec_all, flat ^ shard)
    norm_vec = vec_all[:, :4].transpose(1, 0, 2).reshape(4, D)
    if relative:
        vec_all = order_blocks(
            vec_all, (place[:, None] * n_shard + jnp.arange(n_shard)[None]).reshape(-1)
        )
    vec_abs = vec_all.transpose(1, 0, 2).reshape(n_vec, D)

    low, high = gather_halves(in_rows, "rep", n_rep, relative)
    low = low.reshape(D // 2, 3 * own_feats + own_units)
    high = high.reshape(D // 2, 3 * own_feats + own_units)

    dy_own = cotangent.astype(bf16)
    upstream16 = jnp.concatenate(
        [dy_own] + [hop(dy_own, "shard", n_shard, k) for k in range(1, n_shard)], axis=0
    )

    share = HEAD // rows
    pair = LANES // HEAD
    moves = []
    for device in range(n_rep * n_shard):
        head, part = device // share, device % share
        owner = (head // pair) % n_shard
        local = (head // (pair * n_shard)) * pair + head % pair
        moves.append((device, (local * share + part) * n_shard + owner))
    out_rows = lax.ppermute(out_weight.astype(bf16), ("rep", "shard"), moves)
    both_rows = jnp.concatenate([out_rows, down_weight.astype(bf16)], axis=0)
    both = jnp.concatenate(gather_halves(both_rows, "rep", n_rep, relative), axis=0)
    out_whole = both[:, :rows]
    if relative:
        out_whole = order_blocks(out_whole, place)
    out_whole = out_whole.reshape(own_feats, D)
    down_whole = both[:, rows:].reshape(own_units, D)

    per_row = FF // D
    qkv_bias = vec_abs[4:7].reshape(3 * groups, n_shard, LANES)
    up_bias = vec_abs[8 : 8 + per_row].reshape(n_rep, n_shard, units)
    bias = jnp.concatenate(
        [
            lax.dynamic_index_in_dim(qkv_bias, shard, 1, keepdims=False).reshape(1, 3 * own_feats),
            lax.dynamic_index_in_dim(up_bias, shard, 1, keepdims=False).reshape(1, own_units),
        ],
        axis=1,
    )
    rope = order_blocks(
        jnp.asarray(rope_lanes(seq_len)).reshape(n_shard, tok_count, 3 * LANES), near
    ).reshape(seq_len, 3 * LANES)
    seg_row = jnp.concatenate(
        [lax.dynamic_slice(segments[0], (near[k] * tok_count,), (tok_count,)) for k in range(n_shard)]
    )
    positions = (near[:, None] * tok_count + jnp.arange(tok_count)[None, :]).reshape(seq_len)
    allowed = (seg_row[:, None] == seg_row[None, :]) & (positions[None, :] <= positions[:, None])
    mask = jnp.where(allowed, 0.0, HIDDEN).astype(f32)

    h_one, h_two, qkv16, act16, slope = front(
        orders, normed_seq, norm_vec, low, high, bias, rope, units
    )
    d_mixed16, d_up16, up_sum = hidden(orders, upstream16, out_whole, down_whole, slope, units)
    term_half = D // 2

    def split_terms(left, right):
        keep = contract_rows(left[:, :term_half], right)
        sent = contract_rows(left[:, term_half:], right).astype(bf16)
        return keep, sent

    def reduce_rep(keep, sent, block):
        if relative:
            return reduce_relative(keep, [sent], "rep", n_rep)
        terms = jnp.concatenate([keep, sent.astype(f32)], axis=0)
        return lax.psum_scatter(terms, "rep", scatter_dimension=0, tiled=True)[0]

    up_keep, up_sent = split_terms(h_two, d_up16)
    half_rep = n_rep // 2
    sum_up = reduce_rep(
        up_keep.reshape(half_rep, n_shard * rows, own_units),
        up_sent.reshape(half_rep, n_shard * rows, own_units),
        n_shard * rows,
    )

    mixed16, d_qkv16, qkv_sum = attend(qkv16, d_mixed16, mask, rope)

    qkv_keep, qkv_sent = split_terms(h_one, d_qkv16)
    sum_qkv = reduce_rep(
        qkv_keep.reshape(half_rep, n_shard * rows, 3 * own_feats),
        qkv_sent.reshape(half_rep, n_shard * rows, 3 * own_feats),
        n_shard * rows,
    )

    scaled16, scaled_own, norm_sum = back(
        d_qkv16, d_up16, normed_seq, norm_vec, low, high, tok_count
    )
    scaled = scaled_own
    for k in range(1, n_shard):
        piece = scaled16[k * tok_count : (k + 1) * tok_count]
        scaled = scaled + hop(piece, "shard", n_shard, k).astype(f32)
    scaled = order_columns(scaled, order, inverse=True)
    grad_input = cotangent + inv_std * (
        scaled
        - jnp.mean(scaled, axis=-1, keepdims=True)
        - normed * jnp.mean(scaled * normed, axis=-1, keepdims=True)
    )

    def branch(some):
        return plain_dot(mixed16[some], out_whole) + plain_dot(act16[some], down_whole)

    block_out = block_in + branch(slice(0, tok_count)) + vec_abs[7] + vec_abs[8 + per_row]
    sent_out = branch(slice(tok_count, seq_len)).astype(bf16)
    for k in range(1, n_shard):
        piece = sent_out[(k - 1) * tok_count : k * tok_count]
        block_out = block_out + hop(piece, "shard", n_shard, k).astype(f32)

    down_keep, down_sent = split_terms(act16, upstream16)
    term_out = contract_rows(mixed16, upstream16).reshape(n_rep, rows, D)
    if relative:
        term_out = order_blocks(term_out, order)
    sum_both = reduce_rep(
        jnp.concatenate([down_keep.reshape(half_rep, units, D), term_out[:half_rep]], axis=1),
        jnp.concatenate(
            [down_sent.reshape(half_rep, units, D), term_out[half_rep:].astype(bf16)], axis=1
        ),
        units + rows,
    )
    grad_down = sum_both[:units]
    grad_out = lax.ppermute(sum_both[units:], ("rep", "shard"), [(b, a) for a, b in moves])

    def back_rows(sums):
        blocks = order_blocks(sums.reshape(n_shard, rows, sums.shape[1]), near)
        got = [blocks[0]]
        for k in range(1, n_shard):
            got.append(hop(blocks[k].astype(bf16), "shard", n_shard, k).astype(f32))
        return order_blocks(jnp.stack(got), near)

    grad_up = back_rows(sum_up).reshape(n_shard, rows, n_rep, units)
    grad_up = grad_up.transpose(1, 2, 0, 3).reshape(rows, FF)
    grad_qkv = back_rows(sum_qkv).reshape(n_shard, rows, 3 * groups, LANES)
    grad_qkv = grad_qkv.transpose(1, 2, 0, 3).reshape(rows, 3 * D)

    mine = jnp.arange(n_shard) == shard
    cot_sum = jnp.sum(cotangent, axis=0)[None]
    bias_qkv = jnp.where(
        mine[None, :, None], qkv_sum.reshape(3 * groups, 1, LANES), 0.0
    ).reshape(3, D)
    bias_up = jnp.where(
        mine[None, :, None], up_sum.reshape(n_rep, 1, units), 0.0
    ).reshape(per_row, D)
    late = jnp.concatenate([bias_qkv, cot_sum, bias_up, cot_sum], axis=0)
    late = late.reshape(n_vec - 4, n_rep * n_shard, cols).transpose(1, 0, 2)
    early = norm_sum.reshape(4, n_rep * n_shard, cols).transpose(1, 0, 2)
    late = order_blocks(late, (order[:, None] * n_shard + near[None]).reshape(-1))
    early = order_blocks(early, flat ^ shard)
    vec_terms = jnp.concatenate([early, late], axis=1)
    vec_terms = vec_terms.reshape(n_rep, n_shard, n_vec, cols).transpose(1, 0, 2, 3)
    grad_vec = vec_terms[0]
    for k in range(1, n_shard):
        grad_vec = grad_vec + hop(vec_terms[k], "shard", n_shard, k)
    if relative:
        for shift, count in reversed(stages(n_rep)):
            view = grad_vec.reshape((count, grad_vec.shape[0] // count) + grad_vec.shape[1:])
            grad_vec = view[0]
            for k in range(1, count):
                grad_vec = grad_vec + hop(view[k], "rep", n_rep, k << shift)
        grad_vec = grad_vec[0]
    else:
        grad_vec = lax.psum_scatter(grad_vec, "rep", scatter_dimension=0, tiled=True)[0]

    new_qkv, new_first_qkv, new_second_qkv = adam_update(
        qkv_weight, grad_qkv, first_qkv, second_qkv, LR_MATRIX, WEIGHT_DECAY
    )
    new_out, new_first_out, new_second_out = adam_update(
        out_weight, grad_out, first_out, second_out, LR_MATRIX, WEIGHT_DECAY
    )
    new_up, new_first_up, new_second_up = adam_update(
        up_weight, grad_up, first_up, second_up, LR_MATRIX, WEIGHT_DECAY
    )
    new_down, new_first_down, new_second_down = adam_update(
        down_weight, grad_down, first_down, second_down, LR_MATRIX, WEIGHT_DECAY
    )
    new_vec, new_first_vec, new_second_vec = adam_update(
        vectors, grad_vec, first_vec, second_vec, LR_VECTOR, 0.0
    )
    return (
        block_out,
        grad_input,
        grad_qkv,
        grad_out,
        grad_up,
        grad_down,
        grad_vec,
        new_qkv,
        new_out,
        new_up,
        new_down,
        new_vec,
        new_first_qkv,
        new_first_out,
        new_first_up,
        new_first_down,
        new_first_vec,
        new_second_qkv,
        new_second_out,
        new_second_up,
        new_second_down,
        new_second_vec,
    )


def solution(mesh):
    return jax.shard_map(
        shards,
        mesh=mesh,
        in_specs=(
            P(("rep", "shard"), None),
            P(("rep", "shard"), None),
            P("rep", None),
            P(("rep", "shard"), None),
            P(("rep", "shard"), None),
            P(("rep", "shard"), None),
            P(("rep", "shard"), None),
            P(None, ("rep", "shard")),
            P(("rep", "shard"), None),
            P(("rep", "shard"), None),
            P(("rep", "shard"), None),
            P(("rep", "shard"), None),
            P(None, ("rep", "shard")),
            P(("rep", "shard"), None),
            P(("rep", "shard"), None),
            P(("rep", "shard"), None),
            P(("rep", "shard"), None),
            P(None, ("rep", "shard")),
        ),
        out_specs=(
            P(("rep", "shard"), None),
            P(("rep", "shard"), None),
            P(("rep", "shard"), None),
            P(("rep", "shard"), None),
            P(("rep", "shard"), None),
            P(("rep", "shard"), None),
            P(None, ("rep", "shard")),
            P(("rep", "shard"), None),
            P(("rep", "shard"), None),
            P(("rep", "shard"), None),
            P(("rep", "shard"), None),
            P(None, ("rep", "shard")),
            P(("rep", "shard"), None),
            P(("rep", "shard"), None),
            P(("rep", "shard"), None),
            P(("rep", "shard"), None),
            P(None, ("rep", "shard")),
            P(("rep", "shard"), None),
            P(("rep", "shard"), None),
            P(("rep", "shard"), None),
            P(("rep", "shard"), None),
            P(None, ("rep", "shard")),
        ),
        check_vma=False,
    )
```

```python
import jax
import jax.numpy as jnp
import numpy as np
from jax import lax
from jax.experimental import pallas as pl
from jax.experimental.pallas import tpu as pltpu
from jax.sharding import PartitionSpec as P

D = 1024
HEADS = 16
HEAD = D // HEADS
FF = 4096
ROT = 16
STEP = 10
LANES = 128


LN_EPS = 1e-05
BETA_ONE = 0.9
BETA_TWO = 0.95
ADAM_EPS = 1e-08
LR_MATRIX = 0.03
LR_VECTOR = 0.2
WEIGHT_DECAY = 0.01
ROPE_BASE = 10000.0
INV_ROOT_TWO = 0.7071067811865476
INV_ROOT_TAU = 0.3989422804014327
HIDDEN = -1e30
bf16 = jnp.bfloat16
f32 = jnp.float32
TILE = 256


def adam_update(param, grad, first, second, rate, decay):
    first_new = BETA_ONE * first + (1.0 - BETA_ONE) * grad
    second_new = BETA_TWO * second + (1.0 - BETA_TWO) * grad * grad
    first_hat = first_new / (1.0 - BETA_ONE**STEP)
    second_hat = second_new / (1.0 - BETA_TWO**STEP)
    return (
        param - rate * (first_hat / (jnp.sqrt(second_hat) + ADAM_EPS) + decay * param),
        first_new,
        second_new,
    )


def contract_rows(left, right):
    return lax.dot_general(left, right, (((0,), (0,)), ((), ())), preferred_element_type=f32)


def contract_cols(left, right):
    return lax.dot_general(left, right, (((1,), (1,)), ((), ())), preferred_element_type=f32)


def plain_dot(left, right):
    return jnp.dot(left, right, preferred_element_type=f32)


def rope_lanes(seq_len):
    half = ROT // 2
    freqs = (ROPE_BASE ** (-(2.0 * np.arange(half, dtype=np.float32) / ROT))).astype(np.float32)
    angles = np.arange(seq_len, dtype=np.float32)[:, None] * freqs[None, :]
    cosines, sines = np.cos(angles), np.sin(angles)
    keep = np.ones((seq_len, HEAD), np.float32)
    up = np.zeros((seq_len, HEAD), np.float32)
    down = np.zeros((seq_len, HEAD), np.float32)
    keep[:, :half], keep[:, half:ROT] = cosines, cosines
    up[:, :half] = -sines
    down[:, half:ROT] = sines
    reps = LANES // HEAD
    return np.concatenate([np.tile(t, (1, reps)) for t in (keep, up, down)], axis=1)


def turn(values, table, sign):
    half = ROT // 2
    above = pltpu.roll(values, LANES - half, 1)
    below = pltpu.roll(values, half, 1)
    moved = above * table[:, LANES : 2 * LANES] + below * table[:, 2 * LANES :]
    return values * table[:, :LANES] + sign * moved


def params(mib):
    return pltpu.CompilerParams(vmem_limit_bytes=mib << 20)


def cost(flops, count):
    return pl.CostEstimate(flops=flops, bytes_accessed=count, transcendentals=0)


def whole_spec(shape):
    return pl.BlockSpec(shape, lambda *_: (0,) * len(shape))


def rope_tables(positions):
    half_rot = ROT // 2
    freqs = ROPE_BASE ** (-(2.0 * jnp.arange(half_rot).astype(jnp.float32) / ROT))
    angles = positions.astype(jnp.float32)[:, None] * freqs[None, :]
    return (jnp.cos(angles)[:, None, :], jnp.sin(angles)[:, None, :])


def rotate(heads, cosines, sines):
    half_rot = ROT // 2
    lower = heads[..., :half_rot]
    upper = heads[..., half_rot:ROT]
    return jnp.concatenate(
        [lower * cosines - upper * sines, upper * cosines + lower * sines, heads[..., ROT:]],
        axis=-1,
    )


def unrotate(heads, cosines, sines):
    half_rot = ROT // 2
    lower = heads[..., :half_rot]
    upper = heads[..., half_rot:ROT]
    return jnp.concatenate(
        [lower * cosines + upper * sines, upper * cosines - lower * sines, heads[..., ROT:]],
        axis=-1,
    )


def gelu_value(inner):
    return 0.5 * inner * (1.0 + jax.scipy.special.erf(inner * INV_ROOT_TWO))


def gelu_slope(inner):
    return (
        0.5 * (1.0 + jax.scipy.special.erf(inner * INV_ROOT_TWO))
        + inner * jnp.exp(-0.5 * inner * inner) * INV_ROOT_TAU
    )


def hop(value, axis, size, mask):
    return lax.ppermute(value, axis, [(i, i ^ mask) for i in range(size)])


def pick(blocks, index, axis=0):
    return lax.dynamic_index_in_dim(blocks, index, axis, keepdims=False)


def stages(size):
    bits = size.bit_length() - 1
    found = []
    while bits > 0:
        take = 2 if bits >= 2 else 1
        bits -= take
        found.append((bits, 1 << take))
    return found


def gather_axis(own, axis, me, size):
    if size > 16:
        return lax.all_gather(own, axis)
    pieces = {0: own}
    for shift, count in stages(size):
        more = dict(pieces)
        for k in range(1, count):
            for mask, piece in pieces.items():
                more[mask ^ (k << shift)] = hop(piece, axis, size, k << shift)
        pieces = more
    whole = jnp.zeros((size,) + own.shape, own.dtype)
    for mask in range(size):
        whole = lax.dynamic_update_index_in_dim(whole, pieces[mask], me ^ mask, 0)
    return whole


def exchange_axis(blocks, axis, me, size, wire):
    got = [(0, pick(blocks, me))]
    for mask in range(1, size):
        got.append((mask, hop(pick(blocks, me ^ mask).astype(wire), axis, size, mask)))
    return got


def reduce_axis(blocks, axis, me, size, wire):
    current = blocks
    for shift, count in reversed(stages(size)):
        left = current.shape[0] // count
        view = current.reshape((left, count) + current.shape[1:])
        digit = (me >> shift) & (count - 1)
        total = pick(view, digit, 1)
        for k in range(1, count):
            sent = pick(view, digit ^ k, 1).astype(wire)
            total = total + hop(sent, axis, size, k << shift).astype(jnp.float32)
        current = total
    return current[0]


def general(
    block_in,
    cotangent,
    segments,
    qkv_weight,
    out_weight,
    up_weight,
    down_weight,
    vectors,
    first_qkv,
    first_out,
    first_up,
    first_down,
    first_vec,
    second_qkv,
    second_out,
    second_up,
    second_down,
    second_vec,
):
    tok_count = block_in.shape[0]
    n_rep = lax.axis_size("rep")
    n_shard = lax.axis_size("shard")
    rep = lax.axis_index("rep")
    shard = lax.axis_index("shard")
    seq_len = tok_count * n_shard
    head_dim = D // HEADS
    own_heads = HEADS // n_shard
    own_feats = own_heads * head_dim
    rows = qkv_weight.shape[0]
    units = down_weight.shape[0]
    own_units = units * n_rep
    cols = vectors.shape[1]
    score_scale = head_dim ** (-0.5)

    qkv_cols = qkv_weight.astype(bf16).reshape(rows, 3, own_heads, n_shard, head_dim)
    qkv_cols = qkv_cols.transpose(3, 0, 1, 2, 4).reshape(n_shard, rows, 3 * own_feats)
    up_cols = up_weight.astype(bf16).reshape(rows, n_rep, n_shard, units)
    up_cols = up_cols.transpose(2, 0, 1, 3).reshape(n_shard, rows, own_units)
    in_cols = jnp.concatenate([qkv_cols, up_cols], axis=2)
    in_rows = jnp.zeros_like(in_cols)
    for mask, piece in exchange_axis(in_cols, "shard", shard, n_shard, bf16):
        in_rows = lax.dynamic_update_index_in_dim(in_rows, piece, shard ^ mask, 0)
    in_rows = in_rows.reshape(n_shard * rows, 3 * own_feats + own_units)

    center = block_in - jnp.mean(block_in, axis=-1, keepdims=True)
    inv_std = lax.rsqrt(jnp.mean(center * center, axis=-1, keepdims=True) + LN_EPS)
    normed = center * inv_std
    normed_seq = gather_axis(normed.astype(bf16), "shard", shard, n_shard).reshape(seq_len, D)
    normed_seq = normed_seq.astype(f32)

    vec_some = gather_axis(vectors, "shard", shard, n_shard)
    vec_all = gather_axis(vec_some, "rep", rep, n_rep)
    vec_all = vec_all.transpose(2, 0, 1, 3).reshape(vectors.shape[0], D)

    in_whole = gather_axis(in_rows, "rep", rep, n_rep).reshape(D, 3 * own_feats + own_units)
    upstream16 = gather_axis(cotangent.astype(bf16), "shard", shard, n_shard).reshape(seq_len, D)
    down_whole = gather_axis(down_weight.astype(bf16), "rep", rep, n_rep).reshape(own_units, D)
    share = head_dim // rows
    moves = []
    for device in range(n_rep * n_shard):
        head, part = device // share, device % share
        moves.append((device, ((head // n_shard) * share + part) * n_shard + head % n_shard))
    out_rows = lax.ppermute(out_weight.astype(bf16), ("rep", "shard"), moves)
    out_whole = gather_axis(out_rows, "rep", rep, n_rep).reshape(own_feats, D)

    per_row = FF // D
    gain_one, shift_one, gain_two, shift_two = (vec_all[0], vec_all[1], vec_all[2], vec_all[3])
    qkv_bias = pick(vec_all[4:7].reshape(3, own_heads, n_shard, head_dim), shard, 2).reshape(
        3 * own_feats
    )
    up_bias = pick(vec_all[8 : 8 + per_row].reshape(n_rep, n_shard, units), shard, 1).reshape(
        own_units
    )
    out_bias = vec_all[7]
    down_bias = vec_all[8 + per_row]

    h_one = (normed_seq * gain_one + shift_one).astype(bf16)
    h_two = (normed_seq * gain_two + shift_two).astype(bf16)
    qkv_whole = in_whole[:, : 3 * own_feats]
    up_whole = in_whole[:, 3 * own_feats :]
    qkv_lin = jnp.dot(h_one, qkv_whole, preferred_element_type=f32) + qkv_bias
    up_lin = jnp.dot(h_two, up_whole, preferred_element_type=f32) + up_bias

    positions = jnp.arange(seq_len)
    cosines, sines = rope_tables(positions)

    def heads_of(values):
        return values.reshape(seq_len, own_heads, head_dim)

    query16 = rotate(heads_of(qkv_lin[:, :own_feats]), cosines, sines).astype(bf16)
    key16 = rotate(heads_of(qkv_lin[:, own_feats : 2 * own_feats]), cosines, sines).astype(bf16)
    value16 = heads_of(qkv_lin[:, 2 * own_feats :]).astype(bf16)
    seg_row = segments[0]
    allowed = (seg_row[:, None] == seg_row[None, :]) & (positions[None, :] <= positions[:, None])
    scores = jnp.where(
        allowed[None],
        jnp.einsum("qhd,khd->hqk", query16, key16, preferred_element_type=f32) * score_scale,
        -jnp.inf,
    )
    row_max = jnp.max(scores, axis=-1, keepdims=True)
    expo = jnp.exp(scores - row_max)
    row_sum = jnp.sum(expo, axis=-1, keepdims=True)
    log_total = row_max + jnp.log(row_sum)
    probs16 = (expo / row_sum).astype(bf16)
    mixed16 = (
        jnp.einsum("hqk,khd->qhd", probs16, value16, preferred_element_type=f32)
        .reshape(seq_len, own_feats)
        .astype(bf16)
    )
    act16 = gelu_value(up_lin).astype(bf16)
    branches = jnp.dot(mixed16, out_whole, preferred_element_type=f32)
    branches = branches + jnp.dot(act16, down_whole, preferred_element_type=f32)
    branches = reduce_axis(
        branches.reshape(n_shard, tok_count, D), "shard", shard, n_shard, bf16
    )
    block_out = block_in + branches + out_bias + down_bias

    term_down = contract_rows(act16, upstream16)
    sum_down = reduce_axis(term_down.reshape(n_rep, units, D), "rep", rep, n_rep, bf16)
    term_out = contract_rows(mixed16, upstream16)
    sum_out = reduce_axis(term_out.reshape(n_rep, rows, D), "rep", rep, n_rep, bf16)
    grad_out = lax.ppermute(sum_out, ("rep", "shard"), [(b, a) for a, b in moves])
    grad_down = sum_down
    d_act = contract_cols(upstream16, down_whole)
    d_mixed16 = heads_of(contract_cols(upstream16, out_whole)).astype(bf16)
    d_up = d_act * gelu_slope(up_lin)
    d_up16 = d_up.astype(bf16)
    term_up = contract_rows(h_two, d_up16)
    sum_up = reduce_axis(
        term_up.reshape(n_rep, n_shard * rows, own_units), "rep", rep, n_rep, bf16
    )

    def back_rows(sums, width):
        whole = jnp.zeros((n_shard, rows, width), f32)
        blocks = sums.reshape(n_shard, rows, width)
        for mask, piece in exchange_axis(blocks, "shard", shard, n_shard, bf16):
            whole = lax.dynamic_update_index_in_dim(whole, piece.astype(f32), shard ^ mask, 0)
        return whole

    grad_up = back_rows(sum_up, own_units).reshape(n_shard, rows, n_rep, units)
    grad_up = grad_up.transpose(1, 2, 0, 3).reshape(rows, FF)

    row_delta = jnp.sum(
        d_mixed16.astype(f32) * heads_of(mixed16).astype(f32),
        axis=-1,
    ).T[:, :, None]
    probs_again = jnp.exp(scores - log_total)
    d_probs = jnp.einsum("qhd,khd->hqk", d_mixed16, value16, preferred_element_type=f32)
    d_scores16 = (probs_again * (d_probs - row_delta) * score_scale).astype(bf16)
    probs_back16 = probs_again.astype(bf16)
    d_query = jnp.einsum("hqk,khd->qhd", d_scores16, key16, preferred_element_type=f32)
    d_keys = jnp.einsum("hqk,qhd->khd", d_scores16, query16, preferred_element_type=f32)
    d_values = jnp.einsum("hqk,qhd->khd", probs_back16, d_mixed16, preferred_element_type=f32)
    d_qkv = jnp.concatenate(
        [
            unrotate(d_query, cosines, sines).reshape(seq_len, own_feats),
            unrotate(d_keys, cosines, sines).reshape(seq_len, own_feats),
            d_values.reshape(seq_len, own_feats),
        ],
        axis=1,
    )
    d_qkv16 = d_qkv.astype(bf16)
    term_qkv = contract_rows(h_one, d_qkv16)
    sum_qkv = reduce_axis(
        term_qkv.reshape(n_rep, n_shard * rows, 3 * own_feats), "rep", rep, n_rep, bf16
    )
    grad_qkv = back_rows(sum_qkv, 3 * own_feats)
    grad_qkv = grad_qkv.reshape(n_shard, rows, 3, own_heads, head_dim)
    grad_qkv = grad_qkv.transpose(1, 2, 3, 0, 4).reshape(rows, 3 * D)

    d_one = contract_cols(d_qkv16, qkv_whole)
    d_two = contract_cols(d_up16, up_whole)
    scaled = d_one * gain_one + d_two * gain_two
    scaled = reduce_axis(scaled.reshape(n_shard, tok_count, D), "shard", shard, n_shard, bf16)
    grad_input = cotangent + inv_std * (
        scaled
        - jnp.mean(scaled, axis=-1, keepdims=True)
        - normed * jnp.mean(scaled * normed, axis=-1, keepdims=True)
    )

    mine = jnp.arange(n_shard) == shard
    cot_sum = jnp.sum(cotangent, axis=0)
    bias_qkv = jnp.where(
        mine[None, None, :, None],
        jnp.sum(d_qkv, axis=0).reshape(3, own_heads, 1, head_dim),
        0.0,
    ).reshape(3, D)
    bias_up = jnp.where(
        mine[None, :, None], jnp.sum(d_up, axis=0).reshape(n_rep, 1, units), 0.0
    ).reshape(per_row, D)
    vec_terms = jnp.concatenate(
        [
            jnp.sum(d_one * normed_seq, axis=0)[None],
            jnp.sum(d_one, axis=0)[None],
            jnp.sum(d_two * normed_seq, axis=0)[None],
            jnp.sum(d_two, axis=0)[None],
            bias_qkv,
            cot_sum[None],
            bias_up,
            cot_sum[None],
        ],
        axis=0,
    )
    vec_blocks = vec_terms.reshape(vectors.shape[0], n_rep, n_shard, cols).transpose(1, 2, 0, 3)
    grad_vec = reduce_axis(
        reduce_axis(vec_blocks, "rep", rep, n_rep, f32), "shard", shard, n_shard, f32
    )

    new_qkv, new_first_qkv, new_second_qkv = adam_update(
        qkv_weight, grad_qkv, first_qkv, second_qkv, LR_MATRIX, WEIGHT_DECAY
    )
    new_out, new_first_out, new_second_out = adam_update(
        out_weight, grad_out, first_out, second_out, LR_MATRIX, WEIGHT_DECAY
    )
    new_up, new_first_up, new_second_up = adam_update(
        up_weight, grad_up, first_up, second_up, LR_MATRIX, WEIGHT_DECAY
    )
    new_down, new_first_down, new_second_down = adam_update(
        down_weight, grad_down, first_down, second_down, LR_MATRIX, WEIGHT_DECAY
    )
    new_vec, new_first_vec, new_second_vec = adam_update(
        vectors, grad_vec, first_vec, second_vec, LR_VECTOR, 0.0
    )
    return (
        block_out,
        grad_input,
        grad_qkv,
        grad_out,
        grad_up,
        grad_down,
        grad_vec,
        new_qkv,
        new_out,
        new_up,
        new_down,
        new_vec,
        new_first_qkv,
        new_first_out,
        new_first_up,
        new_first_down,
        new_first_vec,
        new_second_qkv,
        new_second_out,
        new_second_up,
        new_second_down,
        new_second_vec,
    )


def single(body, outs, prefetch, ins, flops, name, scratch=(), mib=48):
    shapes = tuple(jax.ShapeDtypeStruct(s, d) for s, d in outs)
    moved = sum(a.size * a.dtype.itemsize for a in ins)
    moved += sum(s.size * s.dtype.itemsize for s in shapes)
    return pl.pallas_call(
        body,
        out_shape=shapes,
        grid_spec=pltpu.PrefetchScalarGridSpec(
            num_scalar_prefetch=1,
            grid=(1,),
            in_specs=[whole_spec(a.shape) for a in ins],
            out_specs=tuple(whole_spec(s.shape) for s in shapes),
            scratch_shapes=list(scratch),
        ),
        compiler_params=params(mib),
        cost_estimate=cost(flops, moved),
        name=name,
    )(prefetch, *ins)


def lane_block(index):
    return pl.ds(pl.multiple_of(index * LANES, LANES), LANES)


def row_block(index, size):
    return pl.ds(pl.multiple_of(index * size, size), size)


N_REP = 8
N_SHARD = 4
ORDER = 0
PLACE = N_REP
NEAR = 2 * N_REP
SHARD = NEAR + N_SHARD
QKV = 3 * TILE
UP = D
OUT = TILE


def pack_body(s_ref, qkv_ref, up_ref, vec_ref, *outs):
    for k in range(N_SHARD):
        t = s_ref[NEAR + k]
        o_ref = outs[k]
        for c in range(QKV // LANES):
            o_ref[:, c * LANES : (c + 1) * LANES] = qkv_ref[:, lane_block(c * N_SHARD + t)].astype(bf16)
        for c in range(UP // LANES):
            at = QKV + c * LANES
            o_ref[:, at : at + LANES] = up_ref[:, lane_block(c * N_SHARD + t)].astype(bf16)
        o_ref[:, QKV + UP :] = vec_ref[...]


def norm_body(s_ref, x_ref, o_ref, n_ref):
    x = x_ref[...]
    center = x - jnp.mean(x, axis=-1, keepdims=True)
    inv_std = lax.rsqrt(jnp.mean(center * center, axis=-1, keepdims=True) + LN_EPS)
    n_ref[...] = center * inv_std
    for i in range(N_REP):
        o_ref[:, i * LANES : (i + 1) * LANES] = n_ref[:, lane_block(s_ref[ORDER + i])].astype(bf16)


def join_body(s_ref, *refs):
    out_ref, o_ref = refs[N_SHARD], refs[N_SHARD + 1]
    rows = out_ref.shape[0]
    for k in range(N_SHARD):
        at = row_block(s_ref[NEAR + k], rows)
        o_ref[at, : QKV + UP] = refs[k][:, : QKV + UP]
        o_ref[at, QKV + UP + OUT :] = refs[k][:, QKV + UP :]
    for c in range(D // OUT):
        o_ref[c * rows : (c + 1) * rows, QKV + UP : QKV + UP + OUT] = out_ref[:, c * OUT : (c + 1) * OUT]


def bias_places(s_ref):
    shard = s_ref[SHARD]
    found = []
    for c in range(QKV // LANES):
        found.append((4 + c // 2, s_ref[PLACE + (c % 2) * N_SHARD + shard], c * LANES))
    for c in range(UP // LANES):
        found.append((8 + c // 2, s_ref[PLACE + (c % 2) * N_SHARD + shard], QKV + c * LANES))
    return found


def front_body(s_ref, *refs):
    n_refs, refs = refs[:N_SHARD], refs[N_SHARD:]
    w_refs, refs = refs[:N_REP], refs[N_REP:]
    v_refs, refs = refs[:N_REP], refs[N_REP:]
    rope_ref, h1_ref, h2_ref, qkv_ref, act_ref, slope_ref, vec_ref, last_ref, bias_ref = refs
    j = pl.program_id(0)
    rows = n_refs[0].shape[0]

    @pl.when(j == 0)
    def _():
        for i in range(N_REP):
            parts = v_refs[i][...].astype(f32).T
            vec_ref[:, i * LANES : (i + 1) * LANES] = (parts[0:16] + parts[16:32]) + parts[32:48]
        for k in range(N_SHARD):
            normed = n_refs[k][...].astype(f32)
            at = slice(k * rows, (k + 1) * rows)
            h1_ref[at, :] = (normed * vec_ref[0:1, :] + vec_ref[1:2, :]).astype(bf16)
            h2_ref[at, :] = (normed * vec_ref[2:3, :] + vec_ref[3:4, :]).astype(bf16)
        for row, block, at in bias_places(s_ref):
            bias_ref[at // TILE, 0:1, at % TILE : at % TILE + LANES] = vec_ref[row : row + 1, lane_block(block)]
        both = vec_ref[7:8, :] + vec_ref[12:13, :]
        for i in range(N_REP):
            last_ref[0:1, lane_block(s_ref[ORDER + i])] = both[:, i * LANES : (i + 1) * LANES]

    def product(h_ref):
        total = bias_ref[j, 0:1, :]
        for i in range(0, N_REP, 2):
            weights = jnp.concatenate([w_refs[i][...], w_refs[i + 1][...]], axis=0)
            total = total + plain_dot(h_ref[:, i * LANES : (i + 2) * LANES], weights)
        return total

    @pl.when(j < 2)
    def _():
        lin = product(h1_ref)
        for c in range(0, TILE, LANES):
            qkv_ref[:, c : c + LANES] = turn(lin[:, c : c + LANES], rope_ref[...], 1.0).astype(bf16)

    @pl.when(j == 2)
    def _():
        qkv_ref[...] = product(h1_ref).astype(bf16)

    @pl.when(j > 2)
    def _():
        lin = product(h2_ref)
        above = 0.5 * (1.0 + lax.erf(lin * INV_ROOT_TWO))
        act = (lin * above).astype(bf16)
        slope = above + lin * jnp.exp(-0.5 * lin * lin) * INV_ROOT_TAU
        for c in range(2):
            at = lane_block(s_ref[PLACE + (j - 3) * 2 + c])
            act_ref[:, at] = act[:, c * LANES : (c + 1) * LANES]
            slope_ref[:, at] = slope[:, c * LANES : (c + 1) * LANES]


def front(scalars, normed, pieces, rope):
    tokens = rope.shape[0]
    block = pieces[0].shape[0]
    shapes = (
        ((tokens, D), bf16),
        ((tokens, D), bf16),
        ((tokens, QKV), bf16),
        ((tokens, UP), bf16),
        ((tokens, UP), f32),
        ((16, D), f32),
        ((8, D), f32),
    )
    specs = [whole_spec(s) for s, _ in shapes]
    specs[2] = pl.BlockSpec((tokens, TILE), lambda j, s: (0, jnp.minimum(j, 2)))
    return pl.pallas_call(
        front_body,
        out_shape=tuple(jax.ShapeDtypeStruct(s, d) for s, d in shapes),
        grid_spec=pltpu.PrefetchScalarGridSpec(
            num_scalar_prefetch=1,
            grid=((QKV + UP) // TILE,),
            in_specs=[whole_spec(n.shape) for n in normed]
            + [pl.BlockSpec((block, TILE), lambda j, s: (0, j))] * N_REP
            + [pl.BlockSpec((block, LANES), lambda j, s: (0, (QKV + UP + OUT) // LANES))] * N_REP
            + [whole_spec(rope.shape)],
            out_specs=tuple(specs),
            scratch_shapes=[pltpu.VMEM(((QKV + UP) // TILE, 8, TILE), f32)],
        ),
        compiler_params=params(40),
        cost_estimate=cost(2 * tokens * D * (QKV + UP), 14 << 20),
        name="front",
    )(scalars, *normed, *pieces, *pieces, rope)


def hidden_body(s_ref, *refs):
    dy_refs, refs = refs[:N_SHARD], refs[N_SHARD:]
    out_refs, refs = refs[:N_REP], refs[N_REP:]
    down_refs, refs = refs[:N_REP], refs[N_REP:]
    slope_ref, seq_ref, whole_ref, dmix_ref, du_ref, sum_ref = refs
    tokens = dy_refs[0].shape[0]
    for k in range(N_SHARD):
        seq_ref[k * tokens : (k + 1) * tokens, :] = dy_refs[k][...]
    chunks = D // OUT
    rows = out_refs[0].shape[0] // chunks
    for i in range(N_REP):
        at = row_block(s_ref[ORDER + i], rows)
        for c in range(chunks):
            whole_ref[at, c * OUT : (c + 1) * OUT] = out_refs[i][c * rows : (c + 1) * rows, :]
    dy = seq_ref[...]
    dmix_ref[...] = contract_cols(dy, whole_ref[...]).astype(bf16)
    for i in range(N_REP):
        du = contract_cols(dy, down_refs[i][...]) * slope_ref[:, i * LANES : (i + 1) * LANES]
        at = lane_block(s_ref[ORDER + i])
        du_ref[:, at] = du.astype(bf16)
        sum_ref[0:1, at] = jnp.sum(du, axis=0, keepdims=True)


def hidden(scalars, dys, pieces, downs, slope):
    tokens = slope.shape[0]
    block = pieces[0].shape[0]
    shapes = (
        ((tokens, D), bf16),
        ((OUT, D), bf16),
        ((tokens, OUT), bf16),
        ((tokens, UP), bf16),
        ((8, UP), f32),
    )
    return pl.pallas_call(
        hidden_body,
        out_shape=tuple(jax.ShapeDtypeStruct(s, d) for s, d in shapes),
        grid_spec=pltpu.PrefetchScalarGridSpec(
            num_scalar_prefetch=1,
            grid=(1,),
            in_specs=[whole_spec(a.shape) for a in dys]
            + [pl.BlockSpec((block, OUT), lambda j, s: (0, (QKV + UP) // OUT))] * N_REP
            + [whole_spec(a.shape) for a in downs]
            + [whole_spec(slope.shape)],
            out_specs=tuple(whole_spec(s) for s, _ in shapes),
        ),
        compiler_params=params(40),
        cost_estimate=cost(2 * tokens * D * (OUT + UP), 9 << 20),
        name="hidden",
    )(scalars, *dys, *pieces, *downs, slope)


def attend_body(q_ref, k_ref, v_ref, dm_ref, mask_ref, rope_ref, mix_ref, dqkv_ref, sum_ref, dk_ref, dv_ref):
    pair = pl.program_id(0)
    tokens = q_ref.shape[0]
    chunk = LANES
    scale = HEAD ** (-0.5)
    first = lax.broadcasted_iota(jnp.int32, (chunk, LANES), 1) < HEAD
    every = lax.broadcasted_iota(jnp.int32, (tokens, LANES), 1) < HEAD
    k = k_ref[...]
    v = v_ref[...]
    pairs = pl.num_programs(0)

    def columns(part):
        return pl.ds(pl.multiple_of(part * pairs * LANES + pair * LANES, LANES), LANES)

    dq_total = jnp.zeros((1, LANES), f32)
    for c in range(0, tokens, chunk):
        rows = slice(c, c + chunk)
        q = q_ref[rows, :]
        dm = dm_ref[rows, :]
        mixes, dqs, dks, dvs = [], [], [], []
        for h in range(2):
            mine = first if h == 0 else jnp.logical_not(first)
            qh = jnp.where(mine, q, jnp.zeros_like(q))
            dmh = jnp.where(mine, dm, jnp.zeros_like(dm))
            score = contract_cols(qh, k) * scale + mask_ref[rows, :]
            expo = jnp.exp(score - jnp.max(score, axis=-1, keepdims=True))
            prob = expo * (1.0 / jnp.sum(expo, axis=-1, keepdims=True))
            prob16 = prob.astype(bf16)
            mix16 = plain_dot(prob16, v).astype(bf16)
            delta = jnp.sum(dmh.astype(f32) * mix16.astype(f32), axis=-1, keepdims=True)
            d_prob = contract_cols(dmh, v)
            ds16 = (prob * (d_prob - delta) * scale).astype(bf16)
            mixes.append(mix16)
            dqs.append(plain_dot(ds16, k))
            dks.append(contract_rows(ds16, q))
            dvs.append(contract_rows(prob16, dm))
        mix_ref[rows, :] = jnp.where(first, mixes[0], mixes[1])
        dq = turn(jnp.where(first, dqs[0], dqs[1]), rope_ref[rows, :], -1.0)
        dqkv_ref[rows, columns(0)] = dq.astype(bf16)
        dq_total = dq_total + jnp.sum(dq, axis=0, keepdims=True)
        dk = jnp.where(every, dks[0], dks[1])
        dv = jnp.where(every, dvs[0], dvs[1])
        if c == 0:
            dk_ref[...] = dk
            dv_ref[...] = dv
        else:
            dk_ref[...] += dk
            dv_ref[...] += dv
    dk = turn(dk_ref[...], rope_ref[...], -1.0)
    dv = dv_ref[...]
    dqkv_ref[:, columns(1)] = dk.astype(bf16)
    dqkv_ref[:, columns(2)] = dv.astype(bf16)
    sum_ref[:, columns(0)] = dq_total
    sum_ref[:, columns(1)] = jnp.sum(dk, axis=0, keepdims=True)
    sum_ref[:, columns(2)] = jnp.sum(dv, axis=0, keepdims=True)


def attend(qkv, d_mix, mask, rope):
    tokens, feats = d_mix.shape
    pairs = feats // LANES

    def part(first):
        return pl.BlockSpec((tokens, LANES), lambda j: (0, first * pairs + j))

    return pl.pallas_call(
        attend_body,
        out_shape=(
            jax.ShapeDtypeStruct((tokens, feats), bf16),
            jax.ShapeDtypeStruct((tokens, 3 * feats), bf16),
            jax.ShapeDtypeStruct((1, 3 * feats), f32),
        ),
        grid=(pairs,),
        in_specs=[
            part(0),
            part(1),
            part(2),
            part(0),
            whole_spec(mask.shape),
            whole_spec(rope.shape),
        ],
        out_specs=(
            pl.BlockSpec((tokens, LANES), lambda j: (0, j)),
            whole_spec((tokens, 3 * feats)),
            whole_spec((1, 3 * feats)),
        ),
        scratch_shapes=[pltpu.VMEM((tokens, LANES), f32), pltpu.VMEM((tokens, LANES), f32)],
        compiler_params=params(40),
        cost_estimate=cost(60 * tokens * tokens * feats, 6 << 20),
        name="attend",
    )(qkv, qkv, qkv, d_mix, mask, rope)


def back_body(s_ref, dqkv_ref, du_ref, vec_ref, *refs):
    n_refs, refs = refs[:N_SHARD], refs[N_SHARD:]
    w_refs, refs = refs[:N_REP], refs[N_REP:]
    own_ref, sent_refs, sum_ref = refs[0], refs[1:N_SHARD], refs[N_SHARD]
    rows = n_refs[0].shape[0]
    for i in range(0, N_REP, 2):
        cols = slice(i * LANES, (i + 2) * LANES)
        weights = jnp.concatenate([w_refs[i][:, : QKV + UP], w_refs[i + 1][:, : QKV + UP]], axis=0)
        d_one = contract_cols(dqkv_ref[...], weights[:, :QKV])
        d_two = contract_cols(du_ref[...], weights[:, QKV:])
        scaled = d_one * vec_ref[0:1, cols] + d_two * vec_ref[2:3, cols]
        own_ref[:, cols] = scaled[:rows]
        sums = [jnp.sum(d, axis=0, keepdims=True) for d in (d_one, d_two)]
        turned = [jnp.zeros_like(sums[0])] * 2
        for k in range(N_SHARD):
            at = slice(k * rows, (k + 1) * rows)
            if k:
                sent_refs[k - 1][:, cols] = scaled[at].astype(bf16)
            normed = n_refs[k][:, cols].astype(f32)
            turned = [
                t + jnp.sum(d[at] * normed, axis=0, keepdims=True)
                for t, d in zip(turned, (d_one, d_two))
            ]
        sum_ref[0:1, cols] = turned[0]
        sum_ref[1:2, cols] = sums[0]
        sum_ref[2:3, cols] = turned[1]
        sum_ref[3:4, cols] = sums[1]


def branch_body(s_ref, mix_ref, act_ref, out_ref, last_ref, x_ref, *refs):
    down_refs, refs = refs[:N_REP], refs[N_REP:]
    own_ref, sent_refs = refs[0], refs[1:]
    rows = x_ref.shape[0]
    total = plain_dot(mix_ref[...], out_ref[...])
    for i in range(0, N_REP, 2):
        weights = jnp.concatenate([down_refs[i][...], down_refs[i + 1][...]], axis=0)
        total = total + plain_dot(act_ref[:, i * LANES : (i + 2) * LANES], weights)
    own_ref[...] = x_ref[...] + total[:rows] + last_ref[0:1, :]
    for k in range(1, N_SHARD):
        sent_refs[k - 1][...] = total[k * rows : (k + 1) * rows].astype(bf16)


def terms_body(
    s_ref, h_ref, dqkv_ref, mix_ref, dy_ref, norm_ref, qkv_sum_ref, up_sum_ref, cot_ref, keep_ref, sent_ref, vec_ref, g_ref
):
    half = keep_ref.shape[0]
    keep_ref[:, :QKV] = contract_rows(h_ref[:, :half], dqkv_ref[...])
    sent_ref[:, :QKV] = contract_rows(h_ref[:, half:], dqkv_ref[...]).astype(bf16)
    g_ref[...] = contract_rows(mix_ref[...], dy_ref[...])
    vec_ref[...] = jnp.zeros_like(vec_ref)
    vec_ref[0:4, :] = norm_ref[0:4, :]
    for row, block, at in bias_places(s_ref):
        ref, at = (qkv_sum_ref, at) if at < QKV else (up_sum_ref, at - QKV)
        vec_ref[row : row + 1, lane_block(block)] = ref[0:1, at : at + LANES]
    rows = OUT // N_REP
    for i in range(N_REP):
        here = slice(i * LANES, (i + 1) * LANES)
        cot = cot_ref[0:1, lane_block(s_ref[ORDER + i])]
        vec_ref[7:8, here] = cot
        vec_ref[12:13, here] = cot
        ref = keep_ref if i < N_REP // 2 else sent_ref
        base = i * LANES % half
        found = g_ref[row_block(s_ref[ORDER + i], rows), :]
        for c in range(D // OUT):
            ref[base + c * rows : base + (c + 1) * rows, QKV : QKV + OUT] = found[
                :, c * OUT : (c + 1) * OUT
            ].astype(ref.dtype)
        ref[base : base + LANES, QKV + OUT :] = vec_ref[:, here].T.astype(ref.dtype)


def fold_body(s_ref, *refs):
    up_refs, refs = refs[:4], refs[4:]
    qkv_refs, refs = refs[:4], refs[4:]
    own_ref, sent_refs, out_ref, up_sum, qkv_sum = refs[0], refs[1:4], refs[4], refs[5], refs[6]
    for some, total in ((up_refs, up_sum), (qkv_refs, qkv_sum)):
        total[...] = some[0][...] + some[1][...].astype(f32) + some[2][...].astype(f32) + some[3][...].astype(f32)
    rows = own_ref.shape[0]
    for k in range(N_SHARD):
        at = row_block(s_ref[NEAR + k], rows)
        ref = own_ref if k == 0 else sent_refs[k - 1]
        ref[:, :QKV] = qkv_sum[at, :QKV].astype(ref.dtype)
        ref[:, QKV : QKV + UP] = up_sum[at, :].astype(ref.dtype)
        ref[:, QKV + UP :] = qkv_sum[at, QKV + OUT :].astype(ref.dtype)
    for c in range(D // OUT):
        out_ref[:, c * OUT : (c + 1) * OUT] = qkv_sum[c * rows : (c + 1) * rows, QKV : QKV + OUT]


def adam_body(s_ref, *refs):
    got, refs = refs[:N_SHARD], refs[N_SHARD:]
    states, refs = (refs[0:3], refs[3:6]), refs[6:]
    results, refs = (refs[0:4], refs[4:8]), refs[8:]
    vec_ref, all_ref = refs
    for k in range(N_SHARD):
        all_ref[k] = got[k][...].astype(f32)
    vec_ref[...] = sum(all_ref[k, :, QKV + UP :] for k in range(N_SHARD))
    first = 0
    for state, result in zip(states, results):
        for c in range(state[0].shape[1] // (N_SHARD * LANES)):
            for t in range(N_SHARD):
                grad = all_ref[s_ref[NEAR + t], :, first : first + LANES]
                at = slice((c * N_SHARD + t) * LANES, (c * N_SHARD + t + 1) * LANES)
                result[0][:, at] = grad
                new = adam_update(
                    state[0][:, at], grad, state[1][:, at], state[2][:, at], LR_MATRIX, WEIGHT_DECAY
                )
                for ref, value in zip(result[1:], new):
                    ref[:, at] = value
            first += LANES


def finish_body(s_ref, own_ref, r1_ref, r2_ref, r3_ref, x_ref, cot_ref, o_ref, e_ref):
    total = own_ref[...] + r1_ref[...].astype(f32) + r2_ref[...].astype(f32) + r3_ref[...].astype(f32)
    for i in range(N_REP):
        e_ref[:, lane_block(s_ref[ORDER + i])] = total[:, i * LANES : (i + 1) * LANES]
    x = x_ref[...]
    center = x - jnp.mean(x, axis=-1, keepdims=True)
    inv_std = lax.rsqrt(jnp.mean(center * center, axis=-1, keepdims=True) + LN_EPS)
    normed = center * inv_std
    scaled = e_ref[...]
    o_ref[...] = cot_ref[...] + inv_std * (
        scaled
        - jnp.mean(scaled, axis=-1, keepdims=True)
        - normed * jnp.mean(scaled * normed, axis=-1, keepdims=True)
    )


def to_shards(values):
    return [hop(values[k - 1], "shard", N_SHARD, k) for k in range(1, N_SHARD)]


def to_chips(values):
    return [hop(values[k - 1], "rep", N_REP, 2 * k) for k in range(1, 4)]


def gather_chips(own):
    near = [own] + to_chips([own] * 3)
    return near + [hop(piece, "rep", N_REP, 1) for piece in near]


def sum_rep(keep, sent):
    got = hop(sent, "rep", N_REP, 1)
    parts = [keep[k] + got[k].astype(f32) for k in range(4)]
    return [parts[0]] + to_chips([part.astype(bf16) for part in parts[1:]])


def after(value, *others):
    return lax.optimization_barrier((value,) + others)[0]


def shards(
    block_in,
    cotangent,
    segments,
    qkv_weight,
    out_weight,
    up_weight,
    down_weight,
    vectors,
    first_qkv,
    first_out,
    first_up,
    first_down,
    first_vec,
    second_qkv,
    second_out,
    second_up,
    second_down,
    second_vec,
):
    tok_count = block_in.shape[0]
    rep = lax.axis_index("rep")
    shard = lax.axis_index("shard")
    seq_len = tok_count * N_SHARD
    rows = qkv_weight.shape[0]
    units = down_weight.shape[0]
    n_vec, cols = vectors.shape
    masks = np.array([0, 2, 4, 6, 1, 3, 5, 7], np.int32)
    spots = np.argsort(masks)
    device = np.arange(N_REP)
    places = spots[device[:, None] ^ device[None, :]].astype(np.int32)
    orders = (device[:, None] ^ masks[None, :]).astype(np.int32)
    near = shard ^ jnp.arange(N_SHARD, dtype=jnp.int32)
    table = jnp.asarray(np.concatenate([orders, places], axis=1))
    scalars = jnp.concatenate(
        [lax.dynamic_index_in_dim(table, rep, 0, keepdims=False), near, shard[None]]
    ).astype(jnp.int32)

    vec_t = vectors.T
    high = lax.reduce_precision(vec_t, 8, 7)
    middle = lax.reduce_precision(vec_t - high, 8, 7)
    low = (vec_t - high) - middle
    gap = jnp.zeros((cols, 16 - n_vec), f32)
    vec16 = jnp.concatenate(
        [high, gap, middle, gap, low, gap, jnp.zeros((cols, LANES - 48), f32)], axis=1
    ).astype(bf16)

    share = HEAD // rows
    pair = LANES // HEAD
    moves = []
    for at in range(N_REP * N_SHARD):
        head, part = at // share, at % share
        owner = (head // pair) % N_SHARD
        local = (head // (pair * N_SHARD)) * pair + head % pair
        moves.append((at, (local * share + part) * N_SHARD + owner))

    own_cols = [((rows, QKV + UP + LANES), bf16)] * N_SHARD
    packed = single(pack_body, own_cols, scalars, [qkv_weight, up_weight, vec16], 0, "pack")
    got_cols = to_shards(packed[1:])
    out_rows = lax.ppermute(out_weight.astype(bf16), ("rep", "shard"), moves)
    (normed_own,) = single(
        norm_body,
        [((tok_count, D), bf16)],
        scalars,
        [block_in],
        0,
        "norm",
        [pltpu.VMEM((tok_count, D), f32)],
    )
    downs = gather_chips(down_weight.astype(bf16))
    (in_rows,) = single(
        join_body,
        [((N_SHARD * rows, QKV + UP + OUT + LANES), bf16)],
        scalars,
        [packed[0], *got_cols, out_rows],
        0,
        "join",
    )
    normed = [normed_own] + to_shards([normed_own] * 3)
    pieces = gather_chips(in_rows)
    dy_own = cotangent.astype(bf16)
    dys = [dy_own] + to_shards([dy_own] * 3)

    rope_parts = jnp.asarray(rope_lanes(seq_len)).reshape(N_SHARD, tok_count, 3 * LANES)
    rope = jnp.concatenate(
        [lax.dynamic_index_in_dim(rope_parts, near[k], 0, keepdims=False) for k in range(N_SHARD)]
    )
    seg_row = jnp.concatenate(
        [lax.dynamic_slice(segments[0], (near[k] * tok_count,), (tok_count,)) for k in range(N_SHARD)]
    )
    positions = (near[:, None] * tok_count + jnp.arange(tok_count)[None, :]).reshape(seq_len)
    allowed = (seg_row[:, None] == seg_row[None, :]) & (positions[None, :] <= positions[:, None])
    mask = jnp.where(allowed, 0.0, HIDDEN).astype(f32)

    h_one, h_two, qkv16, act16, slope, vec_rel, last = front(scalars, normed, pieces, rope)
    dy_seq, out_whole, d_mixed16, d_up16, up_sum = hidden(scalars, dys, pieces, downs, slope)
    half = D // 2

    def split_terms(left, right):
        keep = contract_rows(left[:, :half], right).reshape(4, LANES, D)
        sent = contract_rows(left[:, half:], right).astype(bf16).reshape(4, LANES, D)
        return keep, sent

    down_parts = sum_rep(*split_terms(act16, dy_seq))
    up_parts = sum_rep(*split_terms(h_two, d_up16))

    mixed16, d_qkv16, qkv_sum = attend(qkv16, d_mixed16, mask, rope)

    block16 = ((tok_count, D), bf16)
    block32 = ((tok_count, D), f32)
    size = 2 * seq_len * D
    out_own, *out_sent = single(
        branch_body,
        [block32, block16, block16, block16],
        scalars,
        [mixed16, act16, out_whole, last, block_in, *downs],
        size * (OUT + UP),
        "branch",
    )
    e_own, *e_sent, norm_sum = single(
        back_body,
        [block32, block16, block16, block16, ((8, D), f32)],
        scalars,
        [d_qkv16, d_up16, vec_rel, *normed, *pieces],
        size * (QKV + UP),
        "back",
    )
    out_got = to_shards(out_sent)
    e_got = to_shards(e_sent)
    cot_sum = jnp.sum(cotangent, axis=0, keepdims=True)
    wide = QKV + OUT + LANES
    qkv_keep, qkv_sent = single(
        terms_body,
        [((half, wide), f32), ((half, wide), bf16)],
        scalars,
        [h_one, d_qkv16, mixed16, dy_seq, norm_sum, qkv_sum, up_sum, cot_sum],
        size * (QKV + OUT),
        "terms",
        [pltpu.VMEM((LANES, D), f32), pltpu.VMEM((OUT, D), f32)],
    )
    qkv_parts = sum_rep(qkv_keep.reshape(4, LANES, wide), qkv_sent.reshape(4, LANES, wide))
    narrow = (rows, QKV + UP + LANES)
    g_own, g1, g2, g3, out_sum = single(
        fold_body,
        [(narrow, f32), (narrow, bf16), (narrow, bf16), (narrow, bf16), ((rows, D), f32)],
        scalars,
        [*up_parts, *qkv_parts],
        0,
        "fold",
        [pltpu.VMEM((LANES, UP), f32), pltpu.VMEM((LANES, wide), f32)],
    )
    g_got = to_shards([g1, g2, g3])
    grad_out = lax.ppermute(out_sum, ("rep", "shard"), [(b, a) for a, b in moves])
    block_out = out_own + out_got[0].astype(f32) + out_got[1].astype(f32) + out_got[2].astype(f32)
    grad_down = (
        down_parts[0]
        + down_parts[1].astype(f32)
        + down_parts[2].astype(f32)
        + down_parts[3].astype(f32)
    )
    (grad_input,) = single(
        finish_body,
        [block32],
        scalars,
        [e_own, *e_got, block_in, cotangent],
        0,
        "finish",
        [pltpu.VMEM((tok_count, D), f32)],
    )
    qkv_shape = (qkv_weight.shape, f32)
    up_shape = (up_weight.shape, f32)
    (
        grad_qkv,
        new_qkv,
        new_first_qkv,
        new_second_qkv,
        grad_up,
        new_up,
        new_first_up,
        new_second_up,
        vec_sum,
    ) = single(
        adam_body,
        [qkv_shape] * 4 + [up_shape] * 4 + [((rows, LANES), f32)],
        scalars,
        [g_own, *g_got, qkv_weight, first_qkv, second_qkv, up_weight, first_up, second_up],
        0,
        "adam",
        [pltpu.VMEM((N_SHARD,) + narrow, f32)],
    )
    grad_vec = vec_sum[:, :n_vec].T

    new_out, new_first_out, new_second_out = adam_update(
        out_weight, grad_out, first_out, second_out, LR_MATRIX, WEIGHT_DECAY
    )
    new_down, new_first_down, new_second_down = adam_update(
        down_weight, grad_down, first_down, second_down, LR_MATRIX, WEIGHT_DECAY
    )
    new_vec, new_first_vec, new_second_vec = adam_update(
        vectors, grad_vec, first_vec, second_vec, LR_VECTOR, 0.0
    )
    return (
        block_out,
        grad_input,
        grad_qkv,
        grad_out,
        grad_up,
        grad_down,
        grad_vec,
        new_qkv,
        new_out,
        new_up,
        new_down,
        new_vec,
        new_first_qkv,
        new_first_out,
        new_first_up,
        new_first_down,
        new_first_vec,
        new_second_qkv,
        new_second_out,
        new_second_up,
        new_second_down,
        new_second_vec,
    )


def solution(mesh):
    aligned = mesh.shape["rep"] == N_REP and mesh.shape["shard"] == N_SHARD
    return jax.shard_map(
        shards if aligned else general,
        mesh=mesh,
        in_specs=(
            P(("rep", "shard"), None),
            P(("rep", "shard"), None),
            P("rep", None),
            P(("rep", "shard"), None),
            P(("rep", "shard"), None),
            P(("rep", "shard"), None),
            P(("rep", "shard"), None),
            P(None, ("rep", "shard")),
            P(("rep", "shard"), None),
            P(("rep", "shard"), None),
            P(("rep", "shard"), None),
            P(("rep", "shard"), None),
            P(None, ("rep", "shard")),
            P(("rep", "shard"), None),
            P(("rep", "shard"), None),
            P(("rep", "shard"), None),
            P(("rep", "shard"), None),
            P(None, ("rep", "shard")),
        ),
        out_specs=(
            P(("rep", "shard"), None),
            P(("rep", "shard"), None),
            P(("rep", "shard"), None),
            P(("rep", "shard"), None),
            P(("rep", "shard"), None),
            P(("rep", "shard"), None),
            P(None, ("rep", "shard")),
            P(("rep", "shard"), None),
            P(("rep", "shard"), None),
            P(("rep", "shard"), None),
            P(("rep", "shard"), None),
            P(None, ("rep", "shard")),
            P(("rep", "shard"), None),
            P(("rep", "shard"), None),
            P(("rep", "shard"), None),
            P(("rep", "shard"), None),
            P(None, ("rep", "shard")),
            P(("rep", "shard"), None),
            P(("rep", "shard"), None),
            P(("rep", "shard"), None),
            P(("rep", "shard"), None),
            P(None, ("rep", "shard")),
        ),
        check_vma=False,
    )
```

```python
import jax
import jax.numpy as jnp
import numpy as np
from jax import lax
from jax.experimental import pallas as pl
from jax.experimental.pallas import tpu as pltpu
from jax.sharding import PartitionSpec as P

D = 1024
HEADS = 16
HEAD = D // HEADS
FF = 4096
ROT = 16
STEP = 10
LANES = 128


LN_EPS = 1e-05
BETA_ONE = 0.9
BETA_TWO = 0.95
ADAM_EPS = 1e-08
LR_MATRIX = 0.03
LR_VECTOR = 0.2
WEIGHT_DECAY = 0.01
ROPE_BASE = 10000.0
INV_ROOT_TWO = 0.7071067811865476
INV_ROOT_TAU = 0.3989422804014327
HIDDEN = -1e30
bf16 = jnp.bfloat16
f32 = jnp.float32
TILE = 256


def adam_update(param, grad, first, second, rate, decay):
    first_new = BETA_ONE * first + (1.0 - BETA_ONE) * grad
    second_new = BETA_TWO * second + (1.0 - BETA_TWO) * grad * grad
    first_hat = first_new / (1.0 - BETA_ONE**STEP)
    second_hat = second_new / (1.0 - BETA_TWO**STEP)
    return (
        param - rate * (first_hat / (jnp.sqrt(second_hat) + ADAM_EPS) + decay * param),
        first_new,
        second_new,
    )


def contract_rows(left, right):
    return lax.dot_general(left, right, (((0,), (0,)), ((), ())), preferred_element_type=f32)


def contract_cols(left, right):
    return lax.dot_general(left, right, (((1,), (1,)), ((), ())), preferred_element_type=f32)


def plain_dot(left, right):
    return jnp.dot(left, right, preferred_element_type=f32)


def rope_lanes(seq_len):
    half = ROT // 2
    freqs = (ROPE_BASE ** (-(2.0 * np.arange(half, dtype=np.float32) / ROT))).astype(np.float32)
    angles = np.arange(seq_len, dtype=np.float32)[:, None] * freqs[None, :]
    cosines, sines = np.cos(angles), np.sin(angles)
    keep = np.ones((seq_len, HEAD), np.float32)
    up = np.zeros((seq_len, HEAD), np.float32)
    down = np.zeros((seq_len, HEAD), np.float32)
    keep[:, :half], keep[:, half:ROT] = cosines, cosines
    up[:, :half] = -sines
    down[:, half:ROT] = sines
    reps = LANES // HEAD
    return np.concatenate([np.tile(t, (1, reps)) for t in (keep, up, down)], axis=1)


def turn(values, table, sign):
    half = ROT // 2
    above = pltpu.roll(values, LANES - half, 1)
    below = pltpu.roll(values, half, 1)
    moved = above * table[:, LANES : 2 * LANES] + below * table[:, 2 * LANES :]
    return values * table[:, :LANES] + sign * moved


def params(mib):
    return pltpu.CompilerParams(vmem_limit_bytes=mib << 20)


def cost(micros):
    return pl.CostEstimate(flops=int(micros * 1.15e9), bytes_accessed=1 << 20, transcendentals=0)


def whole_spec(shape):
    return pl.BlockSpec(shape, lambda *_: (0,) * len(shape))


def rope_tables(positions):
    half_rot = ROT // 2
    freqs = ROPE_BASE ** (-(2.0 * jnp.arange(half_rot).astype(jnp.float32) / ROT))
    angles = positions.astype(jnp.float32)[:, None] * freqs[None, :]
    return (jnp.cos(angles)[:, None, :], jnp.sin(angles)[:, None, :])


def rotate(heads, cosines, sines):
    half_rot = ROT // 2
    lower = heads[..., :half_rot]
    upper = heads[..., half_rot:ROT]
    return jnp.concatenate(
        [lower * cosines - upper * sines, upper * cosines + lower * sines, heads[..., ROT:]],
        axis=-1,
    )


def unrotate(heads, cosines, sines):
    half_rot = ROT // 2
    lower = heads[..., :half_rot]
    upper = heads[..., half_rot:ROT]
    return jnp.concatenate(
        [lower * cosines + upper * sines, upper * cosines - lower * sines, heads[..., ROT:]],
        axis=-1,
    )


def gelu_value(inner):
    return 0.5 * inner * (1.0 + jax.scipy.special.erf(inner * INV_ROOT_TWO))


def gelu_slope(inner):
    return (
        0.5 * (1.0 + jax.scipy.special.erf(inner * INV_ROOT_TWO))
        + inner * jnp.exp(-0.5 * inner * inner) * INV_ROOT_TAU
    )


def hop(value, axis, size, mask):
    return lax.ppermute(value, axis, [(i, i ^ mask) for i in range(size)])


def pick(blocks, index, axis=0):
    return lax.dynamic_index_in_dim(blocks, index, axis, keepdims=False)


def stages(size):
    bits = size.bit_length() - 1
    found = []
    while bits > 0:
        take = 2 if bits >= 2 else 1
        bits -= take
        found.append((bits, 1 << take))
    return found


def gather_axis(own, axis, me, size):
    if size > 16:
        return lax.all_gather(own, axis)
    pieces = {0: own}
    for shift, count in stages(size):
        more = dict(pieces)
        for k in range(1, count):
            for mask, piece in pieces.items():
                more[mask ^ (k << shift)] = hop(piece, axis, size, k << shift)
        pieces = more
    whole = jnp.zeros((size,) + own.shape, own.dtype)
    for mask in range(size):
        whole = lax.dynamic_update_index_in_dim(whole, pieces[mask], me ^ mask, 0)
    return whole


def exchange_axis(blocks, axis, me, size, wire):
    got = [(0, pick(blocks, me))]
    for mask in range(1, size):
        got.append((mask, hop(pick(blocks, me ^ mask).astype(wire), axis, size, mask)))
    return got


def reduce_axis(blocks, axis, me, size, wire):
    current = blocks
    for shift, count in reversed(stages(size)):
        left = current.shape[0] // count
        view = current.reshape((left, count) + current.shape[1:])
        digit = (me >> shift) & (count - 1)
        total = pick(view, digit, 1)
        for k in range(1, count):
            sent = pick(view, digit ^ k, 1).astype(wire)
            total = total + hop(sent, axis, size, k << shift).astype(jnp.float32)
        current = total
    return current[0]


def general(
    block_in,
    cotangent,
    segments,
    qkv_weight,
    out_weight,
    up_weight,
    down_weight,
    vectors,
    first_qkv,
    first_out,
    first_up,
    first_down,
    first_vec,
    second_qkv,
    second_out,
    second_up,
    second_down,
    second_vec,
):
    tok_count = block_in.shape[0]
    n_rep = lax.axis_size("rep")
    n_shard = lax.axis_size("shard")
    rep = lax.axis_index("rep")
    shard = lax.axis_index("shard")
    seq_len = tok_count * n_shard
    head_dim = D // HEADS
    own_heads = HEADS // n_shard
    own_feats = own_heads * head_dim
    rows = qkv_weight.shape[0]
    units = down_weight.shape[0]
    own_units = units * n_rep
    cols = vectors.shape[1]
    score_scale = head_dim ** (-0.5)

    qkv_cols = qkv_weight.astype(bf16).reshape(rows, 3, own_heads, n_shard, head_dim)
    qkv_cols = qkv_cols.transpose(3, 0, 1, 2, 4).reshape(n_shard, rows, 3 * own_feats)
    up_cols = up_weight.astype(bf16).reshape(rows, n_rep, n_shard, units)
    up_cols = up_cols.transpose(2, 0, 1, 3).reshape(n_shard, rows, own_units)
    in_cols = jnp.concatenate([qkv_cols, up_cols], axis=2)
    in_rows = jnp.zeros_like(in_cols)
    for mask, piece in exchange_axis(in_cols, "shard", shard, n_shard, bf16):
        in_rows = lax.dynamic_update_index_in_dim(in_rows, piece, shard ^ mask, 0)
    in_rows = in_rows.reshape(n_shard * rows, 3 * own_feats + own_units)

    center = block_in - jnp.mean(block_in, axis=-1, keepdims=True)
    inv_std = lax.rsqrt(jnp.mean(center * center, axis=-1, keepdims=True) + LN_EPS)
    normed = center * inv_std
    normed_seq = gather_axis(normed.astype(bf16), "shard", shard, n_shard).reshape(seq_len, D)
    normed_seq = normed_seq.astype(f32)

    vec_some = gather_axis(vectors, "shard", shard, n_shard)
    vec_all = gather_axis(vec_some, "rep", rep, n_rep)
    vec_all = vec_all.transpose(2, 0, 1, 3).reshape(vectors.shape[0], D)

    in_whole = gather_axis(in_rows, "rep", rep, n_rep).reshape(D, 3 * own_feats + own_units)
    upstream16 = gather_axis(cotangent.astype(bf16), "shard", shard, n_shard).reshape(seq_len, D)
    down_whole = gather_axis(down_weight.astype(bf16), "rep", rep, n_rep).reshape(own_units, D)
    share = head_dim // rows
    moves = []
    for device in range(n_rep * n_shard):
        head, part = device // share, device % share
        moves.append((device, ((head // n_shard) * share + part) * n_shard + head % n_shard))
    out_rows = lax.ppermute(out_weight.astype(bf16), ("rep", "shard"), moves)
    out_whole = gather_axis(out_rows, "rep", rep, n_rep).reshape(own_feats, D)

    per_row = FF // D
    gain_one, shift_one, gain_two, shift_two = (vec_all[0], vec_all[1], vec_all[2], vec_all[3])
    qkv_bias = pick(vec_all[4:7].reshape(3, own_heads, n_shard, head_dim), shard, 2).reshape(
        3 * own_feats
    )
    up_bias = pick(vec_all[8 : 8 + per_row].reshape(n_rep, n_shard, units), shard, 1).reshape(
        own_units
    )
    out_bias = vec_all[7]
    down_bias = vec_all[8 + per_row]

    h_one = (normed_seq * gain_one + shift_one).astype(bf16)
    h_two = (normed_seq * gain_two + shift_two).astype(bf16)
    qkv_whole = in_whole[:, : 3 * own_feats]
    up_whole = in_whole[:, 3 * own_feats :]
    qkv_lin = jnp.dot(h_one, qkv_whole, preferred_element_type=f32) + qkv_bias
    up_lin = jnp.dot(h_two, up_whole, preferred_element_type=f32) + up_bias

    positions = jnp.arange(seq_len)
    cosines, sines = rope_tables(positions)

    def heads_of(values):
        return values.reshape(seq_len, own_heads, head_dim)

    query16 = rotate(heads_of(qkv_lin[:, :own_feats]), cosines, sines).astype(bf16)
    key16 = rotate(heads_of(qkv_lin[:, own_feats : 2 * own_feats]), cosines, sines).astype(bf16)
    value16 = heads_of(qkv_lin[:, 2 * own_feats :]).astype(bf16)
    seg_row = segments[0]
    allowed = (seg_row[:, None] == seg_row[None, :]) & (positions[None, :] <= positions[:, None])
    scores = jnp.where(
        allowed[None],
        jnp.einsum("qhd,khd->hqk", query16, key16, preferred_element_type=f32) * score_scale,
        -jnp.inf,
    )
    row_max = jnp.max(scores, axis=-1, keepdims=True)
    expo = jnp.exp(scores - row_max)
    row_sum = jnp.sum(expo, axis=-1, keepdims=True)
    log_total = row_max + jnp.log(row_sum)
    probs16 = (expo / row_sum).astype(bf16)
    mixed16 = (
        jnp.einsum("hqk,khd->qhd", probs16, value16, preferred_element_type=f32)
        .reshape(seq_len, own_feats)
        .astype(bf16)
    )
    act16 = gelu_value(up_lin).astype(bf16)
    branches = jnp.dot(mixed16, out_whole, preferred_element_type=f32)
    branches = branches + jnp.dot(act16, down_whole, preferred_element_type=f32)
    branches = reduce_axis(
        branches.reshape(n_shard, tok_count, D), "shard", shard, n_shard, bf16
    )
    block_out = block_in + branches + out_bias + down_bias

    term_down = contract_rows(act16, upstream16)
    sum_down = reduce_axis(term_down.reshape(n_rep, units, D), "rep", rep, n_rep, bf16)
    term_out = contract_rows(mixed16, upstream16)
    sum_out = reduce_axis(term_out.reshape(n_rep, rows, D), "rep", rep, n_rep, bf16)
    grad_out = lax.ppermute(sum_out, ("rep", "shard"), [(b, a) for a, b in moves])
    grad_down = sum_down
    d_act = contract_cols(upstream16, down_whole)
    d_mixed16 = heads_of(contract_cols(upstream16, out_whole)).astype(bf16)
    d_up = d_act * gelu_slope(up_lin)
    d_up16 = d_up.astype(bf16)
    term_up = contract_rows(h_two, d_up16)
    sum_up = reduce_axis(
        term_up.reshape(n_rep, n_shard * rows, own_units), "rep", rep, n_rep, bf16
    )

    def back_rows(sums, width):
        whole = jnp.zeros((n_shard, rows, width), f32)
        blocks = sums.reshape(n_shard, rows, width)
        for mask, piece in exchange_axis(blocks, "shard", shard, n_shard, bf16):
            whole = lax.dynamic_update_index_in_dim(whole, piece.astype(f32), shard ^ mask, 0)
        return whole

    grad_up = back_rows(sum_up, own_units).reshape(n_shard, rows, n_rep, units)
    grad_up = grad_up.transpose(1, 2, 0, 3).reshape(rows, FF)

    row_delta = jnp.sum(
        d_mixed16.astype(f32) * heads_of(mixed16).astype(f32),
        axis=-1,
    ).T[:, :, None]
    probs_again = jnp.exp(scores - log_total)
    d_probs = jnp.einsum("qhd,khd->hqk", d_mixed16, value16, preferred_element_type=f32)
    d_scores16 = (probs_again * (d_probs - row_delta) * score_scale).astype(bf16)
    probs_back16 = probs_again.astype(bf16)
    d_query = jnp.einsum("hqk,khd->qhd", d_scores16, key16, preferred_element_type=f32)
    d_keys = jnp.einsum("hqk,qhd->khd", d_scores16, query16, preferred_element_type=f32)
    d_values = jnp.einsum("hqk,qhd->khd", probs_back16, d_mixed16, preferred_element_type=f32)
    d_qkv = jnp.concatenate(
        [
            unrotate(d_query, cosines, sines).reshape(seq_len, own_feats),
            unrotate(d_keys, cosines, sines).reshape(seq_len, own_feats),
            d_values.reshape(seq_len, own_feats),
        ],
        axis=1,
    )
    d_qkv16 = d_qkv.astype(bf16)
    term_qkv = contract_rows(h_one, d_qkv16)
    sum_qkv = reduce_axis(
        term_qkv.reshape(n_rep, n_shard * rows, 3 * own_feats), "rep", rep, n_rep, bf16
    )
    grad_qkv = back_rows(sum_qkv, 3 * own_feats)
    grad_qkv = grad_qkv.reshape(n_shard, rows, 3, own_heads, head_dim)
    grad_qkv = grad_qkv.transpose(1, 2, 3, 0, 4).reshape(rows, 3 * D)

    d_one = contract_cols(d_qkv16, qkv_whole)
    d_two = contract_cols(d_up16, up_whole)
    scaled = d_one * gain_one + d_two * gain_two
    scaled = reduce_axis(scaled.reshape(n_shard, tok_count, D), "shard", shard, n_shard, bf16)
    grad_input = cotangent + inv_std * (
        scaled
        - jnp.mean(scaled, axis=-1, keepdims=True)
        - normed * jnp.mean(scaled * normed, axis=-1, keepdims=True)
    )

    mine = jnp.arange(n_shard) == shard
    cot_sum = jnp.sum(cotangent, axis=0)
    bias_qkv = jnp.where(
        mine[None, None, :, None],
        jnp.sum(d_qkv, axis=0).reshape(3, own_heads, 1, head_dim),
        0.0,
    ).reshape(3, D)
    bias_up = jnp.where(
        mine[None, :, None], jnp.sum(d_up, axis=0).reshape(n_rep, 1, units), 0.0
    ).reshape(per_row, D)
    vec_terms = jnp.concatenate(
        [
            jnp.sum(d_one * normed_seq, axis=0)[None],
            jnp.sum(d_one, axis=0)[None],
            jnp.sum(d_two * normed_seq, axis=0)[None],
            jnp.sum(d_two, axis=0)[None],
            bias_qkv,
            cot_sum[None],
            bias_up,
            cot_sum[None],
        ],
        axis=0,
    )
    vec_blocks = vec_terms.reshape(vectors.shape[0], n_rep, n_shard, cols).transpose(1, 2, 0, 3)
    grad_vec = reduce_axis(
        reduce_axis(vec_blocks, "rep", rep, n_rep, f32), "shard", shard, n_shard, f32
    )

    new_qkv, new_first_qkv, new_second_qkv = adam_update(
        qkv_weight, grad_qkv, first_qkv, second_qkv, LR_MATRIX, WEIGHT_DECAY
    )
    new_out, new_first_out, new_second_out = adam_update(
        out_weight, grad_out, first_out, second_out, LR_MATRIX, WEIGHT_DECAY
    )
    new_up, new_first_up, new_second_up = adam_update(
        up_weight, grad_up, first_up, second_up, LR_MATRIX, WEIGHT_DECAY
    )
    new_down, new_first_down, new_second_down = adam_update(
        down_weight, grad_down, first_down, second_down, LR_MATRIX, WEIGHT_DECAY
    )
    new_vec, new_first_vec, new_second_vec = adam_update(
        vectors, grad_vec, first_vec, second_vec, LR_VECTOR, 0.0
    )
    return (
        block_out,
        grad_input,
        grad_qkv,
        grad_out,
        grad_up,
        grad_down,
        grad_vec,
        new_qkv,
        new_out,
        new_up,
        new_down,
        new_vec,
        new_first_qkv,
        new_first_out,
        new_first_up,
        new_first_down,
        new_first_vec,
        new_second_qkv,
        new_second_out,
        new_second_up,
        new_second_down,
        new_second_vec,
    )


def single(body, outs, prefetch, ins, micros, name, scratch=(), mib=48):
    shapes = tuple(jax.ShapeDtypeStruct(s, d) for s, d in outs)
    return pl.pallas_call(
        body,
        out_shape=shapes,
        grid_spec=pltpu.PrefetchScalarGridSpec(
            num_scalar_prefetch=1,
            grid=(1,),
            in_specs=[whole_spec(a.shape) for a in ins],
            out_specs=tuple(whole_spec(s.shape) for s in shapes),
            scratch_shapes=list(scratch),
        ),
        compiler_params=params(mib),
        cost_estimate=cost(micros),
        name=name,
    )(prefetch, *ins)


def lane_block(index):
    return pl.ds(pl.multiple_of(index * LANES, LANES), LANES)


def row_block(index, size):
    return pl.ds(pl.multiple_of(index * size, size), size)


N_REP = 8
N_SHARD = 4
ORDER = 0
PLACE = N_REP
NEAR = 2 * N_REP
SHARD = NEAR + N_SHARD
QKV = 3 * TILE
UP = D
OUT = TILE


def pack_body(s_ref, qkv_ref, up_ref, vec_ref, *refs):
    outs, turn_ref = refs[:-1], refs[-1]
    count, cols = vec_ref.shape
    turn_ref[...] = jnp.zeros_like(turn_ref)
    vec = vec_ref[...]
    for i in range(3):
        part = vec.astype(bf16).astype(f32)
        turn_ref[16 * i : 16 * i + count, :cols] = part
        vec = vec - part
    vec16 = turn_ref[...].T[:cols, :].astype(bf16)
    for k in range(N_SHARD):
        t = s_ref[NEAR + k]
        o_ref = outs[k]
        for c in range(QKV // LANES):
            o_ref[:, c * LANES : (c + 1) * LANES] = qkv_ref[:, lane_block(c * N_SHARD + t)].astype(bf16)
        for c in range(UP // LANES):
            at = QKV + c * LANES
            o_ref[:, at : at + LANES] = up_ref[:, lane_block(c * N_SHARD + t)].astype(bf16)
        o_ref[:, QKV + UP :] = vec16


def norm_body(s_ref, x_ref, o_ref, n_ref):
    x = x_ref[...]
    center = x - jnp.mean(x, axis=-1, keepdims=True)
    inv_std = lax.rsqrt(jnp.mean(center * center, axis=-1, keepdims=True) + LN_EPS)
    n_ref[...] = center * inv_std
    for i in range(N_REP):
        o_ref[:, i * LANES : (i + 1) * LANES] = n_ref[:, lane_block(s_ref[ORDER + i])].astype(bf16)


def join_body(s_ref, *refs):
    out_ref, o_ref = refs[N_SHARD], refs[N_SHARD + 1]
    rows = out_ref.shape[0]
    for k in range(N_SHARD):
        at = row_block(s_ref[NEAR + k], rows)
        o_ref[at, : QKV + UP] = refs[k][:, : QKV + UP]
        o_ref[at, QKV + UP + OUT :] = refs[k][:, QKV + UP :]
    for c in range(D // OUT):
        o_ref[c * rows : (c + 1) * rows, QKV + UP : QKV + UP + OUT] = out_ref[:, c * OUT : (c + 1) * OUT]


def bias_places(s_ref):
    shard = s_ref[SHARD]
    found = []
    for c in range(QKV // LANES):
        found.append((4 + c // 2, s_ref[PLACE + (c % 2) * N_SHARD + shard], c * LANES))
    for c in range(UP // LANES):
        found.append((8 + c // 2, s_ref[PLACE + (c % 2) * N_SHARD + shard], QKV + c * LANES))
    return found


def front_body(s_ref, *refs):
    n_refs, refs = refs[:N_SHARD], refs[N_SHARD:]
    w_refs, refs = refs[:N_REP], refs[N_REP:]
    v_refs, refs = refs[:N_REP], refs[N_REP:]
    out_refs, refs = refs[:N_REP], refs[N_REP:]
    rope_ref, whole_ref, h1_ref, h2_ref, qkv_ref, act_ref, slope_ref, vec_ref, last_ref, bias_ref = refs
    j = pl.program_id(0)
    rows = n_refs[0].shape[0]

    @pl.when(j == 0)
    def _():
        for i in range(N_REP):
            parts = v_refs[i][...].astype(f32).T
            vec_ref[:, i * LANES : (i + 1) * LANES] = (parts[0:16] + parts[16:32]) + parts[32:48]
        for k in range(N_SHARD):
            normed = n_refs[k][...].astype(f32)
            at = slice(k * rows, (k + 1) * rows)
            h1_ref[at, :] = (normed * vec_ref[0:1, :] + vec_ref[1:2, :]).astype(bf16)
            h2_ref[at, :] = (normed * vec_ref[2:3, :] + vec_ref[3:4, :]).astype(bf16)
        for row, block, at in bias_places(s_ref):
            bias_ref[at // TILE, 0:1, at % TILE : at % TILE + LANES] = vec_ref[row : row + 1, lane_block(block)]
        both = vec_ref[7:8, :] + vec_ref[12:13, :]
        for i in range(N_REP):
            last_ref[0:1, lane_block(s_ref[ORDER + i])] = both[:, i * LANES : (i + 1) * LANES]
        chunks = D // OUT
        size = out_refs[0].shape[0] // chunks
        for i in range(N_REP):
            at = row_block(s_ref[ORDER + i], size)
            for c in range(chunks):
                whole_ref[at, c * OUT : (c + 1) * OUT] = out_refs[i][c * size : (c + 1) * size, :]

    def product(h_ref):
        total = bias_ref[j, 0:1, :]
        for i in range(0, N_REP, 2):
            weights = jnp.concatenate([w_refs[i][...], w_refs[i + 1][...]], axis=0)
            total = total + plain_dot(h_ref[:, i * LANES : (i + 2) * LANES], weights)
        return total

    @pl.when(j < 2)
    def _():
        lin = product(h1_ref)
        for c in range(0, TILE, LANES):
            qkv_ref[:, c : c + LANES] = turn(lin[:, c : c + LANES], rope_ref[...], 1.0).astype(bf16)

    @pl.when(j == 2)
    def _():
        qkv_ref[...] = product(h1_ref).astype(bf16)

    @pl.when(j > 2)
    def _():
        lin = product(h2_ref)
        above = 0.5 * (1.0 + lax.erf(lin * INV_ROOT_TWO))
        act = (lin * above).astype(bf16)
        slope = above + lin * jnp.exp(-0.5 * lin * lin) * INV_ROOT_TAU
        for c in range(2):
            at = lane_block(s_ref[PLACE + (j - 3) * 2 + c])
            act_ref[:, at] = act[:, c * LANES : (c + 1) * LANES]
            slope_ref[:, at] = slope[:, c * LANES : (c + 1) * LANES]


def front(scalars, normed, pieces, rope):
    tokens = rope.shape[0]
    block = pieces[0].shape[0]
    shapes = (
        ((OUT, D), bf16),
        ((tokens, D), bf16),
        ((tokens, D), bf16),
        ((tokens, QKV), bf16),
        ((tokens, UP), bf16),
        ((tokens, UP), f32),
        ((16, D), f32),
        ((8, D), f32),
    )
    specs = [whole_spec(s) for s, _ in shapes]
    specs[3] = pl.BlockSpec((tokens, TILE), lambda j, s: (0, jnp.minimum(j, 2)))
    return pl.pallas_call(
        front_body,
        out_shape=tuple(jax.ShapeDtypeStruct(s, d) for s, d in shapes),
        grid_spec=pltpu.PrefetchScalarGridSpec(
            num_scalar_prefetch=1,
            grid=((QKV + UP) // TILE,),
            in_specs=[whole_spec(n.shape) for n in normed]
            + [pl.BlockSpec((block, TILE), lambda j, s: (0, j))] * N_REP
            + [pl.BlockSpec((block, LANES), lambda j, s: (0, (QKV + UP + OUT) // LANES))] * N_REP
            + [pl.BlockSpec((block, OUT), lambda j, s: (0, (QKV + UP) // OUT))] * N_REP
            + [whole_spec(rope.shape)],
            out_specs=tuple(specs),
            scratch_shapes=[pltpu.VMEM(((QKV + UP) // TILE, 8, TILE), f32)],
        ),
        compiler_params=params(40),
        cost_estimate=cost(9),
        name="front",
    )(scalars, *normed, *pieces, *pieces, *pieces, rope)


def hidden_body(s_ref, *refs):
    dy_ref, refs = refs[0], refs[1:]
    down_refs, refs = refs[:N_REP], refs[N_REP:]
    slope_ref, whole_ref, seq_ref, dmix_ref, du_ref, sum_ref = refs
    tokens = dy_ref.shape[0] // N_SHARD
    for k in range(N_SHARD):
        seq_ref[k * tokens : (k + 1) * tokens, :] = dy_ref[row_block(s_ref[NEAR + k], tokens), :]
    dy = seq_ref[...]
    dmix_ref[...] = contract_cols(dy, whole_ref[...]).astype(bf16)
    for i in range(N_REP):
        du = contract_cols(dy, down_refs[i][...]) * slope_ref[:, i * LANES : (i + 1) * LANES]
        at = lane_block(s_ref[ORDER + i])
        du_ref[:, at] = du.astype(bf16)
        sum_ref[0:1, at] = jnp.sum(du, axis=0, keepdims=True)


def weigh(q, k, mask):
    score = contract_cols(q, k) * (HEAD ** (-0.5)) + mask
    expo = jnp.exp(score - jnp.max(score, axis=-1, keepdims=True))
    return expo * (1.0 / jnp.sum(expo, axis=-1, keepdims=True))


def only(values, mine):
    return jnp.where(mine, values, jnp.zeros_like(values))


def mix_body(q_ref, k_ref, v_ref, mask_ref, mix_ref):
    first = lax.broadcasted_iota(jnp.int32, (LANES, LANES), 1) < HEAD
    k = k_ref[...]
    v = v_ref[...]
    for c in range(0, q_ref.shape[0], LANES):
        rows = slice(c, c + LANES)
        q = q_ref[rows, :]
        mixes = []
        for mine in (first, jnp.logical_not(first)):
            prob = weigh(only(q, mine), k, mask_ref[rows, :])
            mixes.append(plain_dot(prob.astype(bf16), v))
        mix_ref[rows, :] = jnp.where(first, mixes[0], mixes[1]).astype(bf16)


def attend_body(
    q_ref, k_ref, v_ref, dm_ref, mix_ref, mask_ref, rope_ref, dqkv_ref, sum_ref, dk_ref, dv_ref
):
    pair = pl.program_id(0)
    tokens = q_ref.shape[0]
    scale = HEAD ** (-0.5)
    first = lax.broadcasted_iota(jnp.int32, (LANES, LANES), 1) < HEAD
    every = lax.broadcasted_iota(jnp.int32, (tokens, LANES), 1) < HEAD
    k = k_ref[...]
    v = v_ref[...]
    pairs = pl.num_programs(0)

    def columns(part):
        return lane_block(part * pairs + pair)

    dq_total = jnp.zeros((1, LANES), f32)
    for c in range(0, tokens, LANES):
        rows = slice(c, c + LANES)
        q = q_ref[rows, :]
        dm = dm_ref[rows, :]
        mix = mix_ref[rows, :].astype(f32)
        dqs, dks, dvs = [], [], []
        for mine in (first, jnp.logical_not(first)):
            dmh = only(dm, mine)
            prob = weigh(only(q, mine), k, mask_ref[rows, :])
            delta = jnp.sum(dmh.astype(f32) * mix, axis=-1, keepdims=True)
            d_prob = contract_cols(dmh, v)
            ds16 = (prob * (d_prob - delta) * scale).astype(bf16)
            dqs.append(plain_dot(ds16, k))
            dks.append(contract_rows(ds16, q))
            dvs.append(contract_rows(prob.astype(bf16), dm))
        dq = turn(jnp.where(first, dqs[0], dqs[1]), rope_ref[rows, :], -1.0)
        dqkv_ref[rows, columns(0)] = dq.astype(bf16)
        dq_total = dq_total + jnp.sum(dq, axis=0, keepdims=True)
        dk = jnp.where(every, dks[0], dks[1])
        dv = jnp.where(every, dvs[0], dvs[1])
        if c == 0:
            dk_ref[...] = dk
            dv_ref[...] = dv
        else:
            dk_ref[...] += dk
            dv_ref[...] += dv
    dk = turn(dk_ref[...], rope_ref[...], -1.0)
    dv = dv_ref[...]
    dqkv_ref[:, columns(1)] = dk.astype(bf16)
    dqkv_ref[:, columns(2)] = dv.astype(bf16)
    sum_ref[:, columns(0)] = dq_total
    sum_ref[:, columns(1)] = jnp.sum(dk, axis=0, keepdims=True)
    sum_ref[:, columns(2)] = jnp.sum(dv, axis=0, keepdims=True)


def pair_spec(tokens, first):
    return pl.BlockSpec((tokens, LANES), lambda j: (0, first + j))


def mix_heads(qkv, mask):
    tokens = qkv.shape[0]
    pairs = OUT // LANES
    return pl.pallas_call(
        mix_body,
        out_shape=jax.ShapeDtypeStruct((tokens, OUT), bf16),
        grid=(pairs,),
        in_specs=[pair_spec(tokens, i * pairs) for i in range(3)] + [whole_spec(mask.shape)],
        out_specs=pair_spec(tokens, 0),
        compiler_params=params(24),
        cost_estimate=cost(6),
        name="mix_heads",
    )(qkv, qkv, qkv, mask)


def attend_back(qkv, d_mix, mixed, mask, rope):
    tokens = qkv.shape[0]
    pairs = OUT // LANES
    return pl.pallas_call(
        attend_body,
        out_shape=(
            jax.ShapeDtypeStruct((tokens, QKV), bf16),
            jax.ShapeDtypeStruct((1, QKV), f32),
        ),
        grid=(pairs,),
        in_specs=[pair_spec(tokens, i * pairs) for i in range(3)]
        + [pair_spec(tokens, 0), pair_spec(tokens, 0), whole_spec(mask.shape), whole_spec(rope.shape)],
        out_specs=(whole_spec((tokens, QKV)), whole_spec((1, QKV))),
        scratch_shapes=[pltpu.VMEM((tokens, LANES), f32), pltpu.VMEM((tokens, LANES), f32)],
        compiler_params=params(32),
        cost_estimate=cost(11),
        name="attend_back",
    )(qkv, qkv, qkv, d_mix, mixed, mask, rope)


def back_body(s_ref, dqkv_ref, du_ref, vec_ref, *refs):
    n_refs, refs = refs[:N_SHARD], refs[N_SHARD:]
    w_refs, refs = refs[:N_REP], refs[N_REP:]
    own_ref, sent_refs, sum_ref = refs[0], refs[1:N_SHARD], refs[N_SHARD]
    rows = n_refs[0].shape[0]
    for i in range(0, N_REP, 2):
        cols = slice(i * LANES, (i + 2) * LANES)
        weights = jnp.concatenate([w_refs[i][:, : QKV + UP], w_refs[i + 1][:, : QKV + UP]], axis=0)
        d_one = contract_cols(dqkv_ref[...], weights[:, :QKV])
        d_two = contract_cols(du_ref[...], weights[:, QKV:])
        scaled = d_one * vec_ref[0:1, cols] + d_two * vec_ref[2:3, cols]
        own_ref[:, cols] = scaled[:rows]
        sums = [jnp.sum(d, axis=0, keepdims=True) for d in (d_one, d_two)]
        turned = [jnp.zeros_like(sums[0])] * 2
        for k in range(N_SHARD):
            at = slice(k * rows, (k + 1) * rows)
            if k:
                sent_refs[k - 1][:, cols] = scaled[at].astype(bf16)
            normed = n_refs[k][:, cols].astype(f32)
            turned = [
                t + jnp.sum(d[at] * normed, axis=0, keepdims=True)
                for t, d in zip(turned, (d_one, d_two))
            ]
        sum_ref[0:1, cols] = turned[0]
        sum_ref[1:2, cols] = sums[0]
        sum_ref[2:3, cols] = turned[1]
        sum_ref[3:4, cols] = sums[1]


def branch_body(s_ref, mix_ref, act_ref, out_ref, *refs):
    down_refs, total_ref = refs[:N_REP], refs[N_REP]
    total = plain_dot(mix_ref[...], out_ref[...])
    for i in range(0, N_REP, 2):
        weights = jnp.concatenate([down_refs[i][...], down_refs[i + 1][...]], axis=0)
        total = total + plain_dot(act_ref[:, i * LANES : (i + 2) * LANES], weights)
    rows = total.shape[0] // N_SHARD
    for k in range(N_SHARD):
        at = row_block(s_ref[NEAR + k], rows)
        total_ref[at, :] = total[k * rows : (k + 1) * rows].astype(bf16)


def terms_body(
    s_ref, h_ref, dqkv_ref, mix_ref, dy_ref, norm_ref, qkv_sum_ref, up_sum_ref, cot_ref, keep_ref, sent_ref, vec_ref, g_ref
):
    half = keep_ref.shape[0]
    keep_ref[:, :QKV] = contract_rows(h_ref[:, :half], dqkv_ref[...])
    sent_ref[:, :QKV] = contract_rows(h_ref[:, half:], dqkv_ref[...]).astype(bf16)
    g_ref[...] = contract_rows(mix_ref[...], dy_ref[...])
    vec_ref[...] = jnp.zeros_like(vec_ref)
    vec_ref[0:4, :] = norm_ref[0:4, :]
    for row, block, at in bias_places(s_ref):
        ref, at = (qkv_sum_ref, at) if at < QKV else (up_sum_ref, at - QKV)
        vec_ref[row : row + 1, lane_block(block)] = ref[0:1, at : at + LANES]
    rows = OUT // N_REP
    for i in range(N_REP):
        here = slice(i * LANES, (i + 1) * LANES)
        cot = cot_ref[0:1, lane_block(s_ref[ORDER + i])]
        vec_ref[7:8, here] = cot
        vec_ref[12:13, here] = cot
        ref = keep_ref if i < N_REP // 2 else sent_ref
        base = i * LANES % half
        found = g_ref[row_block(s_ref[ORDER + i], rows), :]
        for c in range(D // OUT):
            ref[base + c * rows : base + (c + 1) * rows, QKV : QKV + OUT] = found[
                :, c * OUT : (c + 1) * OUT
            ].astype(ref.dtype)
        ref[base : base + LANES, QKV + OUT :] = vec_ref[:, here].T.astype(ref.dtype)


def fold_body(s_ref, *refs):
    up_refs, refs = refs[:4], refs[4:]
    qkv_refs, refs = refs[:4], refs[4:]
    own_ref, sent_refs, out_ref, up_sum, qkv_sum = refs[0], refs[1:4], refs[4], refs[5], refs[6]
    for some, total in ((up_refs, up_sum), (qkv_refs, qkv_sum)):
        total[...] = some[0][...] + some[1][...].astype(f32) + some[2][...].astype(f32) + some[3][...].astype(f32)
    rows = own_ref.shape[0]
    for k in range(N_SHARD):
        at = row_block(s_ref[NEAR + k], rows)
        ref = own_ref if k == 0 else sent_refs[k - 1]
        ref[:, :QKV] = qkv_sum[at, :QKV].astype(ref.dtype)
        ref[:, QKV : QKV + UP] = up_sum[at, :].astype(ref.dtype)
        ref[:, QKV + UP :] = qkv_sum[at, QKV + OUT :].astype(ref.dtype)
    for c in range(D // OUT):
        out_ref[:, c * OUT : (c + 1) * OUT] = qkv_sum[c * rows : (c + 1) * rows, QKV : QKV + OUT]


def adam_body(s_ref, *refs):
    got, refs = refs[:N_SHARD], refs[N_SHARD:]
    states, vec_state, refs = (refs[0:3], refs[3:6]), refs[6:9], refs[9:]
    results, vec_result, refs = (refs[0:4], refs[4:8]), refs[8:12], refs[12:]
    all_ref, turn_ref = refs
    for k in range(N_SHARD):
        all_ref[k] = got[k][...].astype(f32)
    count, cols = vec_state[0].shape
    turn_ref[...] = jnp.zeros_like(turn_ref)
    turn_ref[:cols, :] = sum(all_ref[k, :, QKV + UP :] for k in range(N_SHARD))
    turn_ref[...] = turn_ref[...].T
    grad = turn_ref[:count, :cols]
    vec_result[0][...] = grad
    new = adam_update(vec_state[0][...], grad, vec_state[1][...], vec_state[2][...], LR_VECTOR, 0.0)
    for ref, value in zip(vec_result[1:], new):
        ref[...] = value
    first = 0
    for state, result in zip(states, results):
        for c in range(state[0].shape[1] // (N_SHARD * LANES)):
            for t in range(N_SHARD):
                grad = all_ref[s_ref[NEAR + t], :, first : first + LANES]
                at = slice((c * N_SHARD + t) * LANES, (c * N_SHARD + t + 1) * LANES)
                result[0][:, at] = grad
                new = adam_update(
                    state[0][:, at], grad, state[1][:, at], state[2][:, at], LR_MATRIX, WEIGHT_DECAY
                )
                for ref, value in zip(result[1:], new):
                    ref[:, at] = value
            first += LANES


def finish_body(s_ref, own_ref, r1_ref, r2_ref, r3_ref, x_ref, cot_ref, o_ref, e_ref):
    total = own_ref[...] + r1_ref[...].astype(f32) + r2_ref[...].astype(f32) + r3_ref[...].astype(f32)
    for i in range(N_REP):
        e_ref[:, lane_block(s_ref[ORDER + i])] = total[:, i * LANES : (i + 1) * LANES]
    x = x_ref[...]
    center = x - jnp.mean(x, axis=-1, keepdims=True)
    inv_std = lax.rsqrt(jnp.mean(center * center, axis=-1, keepdims=True) + LN_EPS)
    normed = center * inv_std
    scaled = e_ref[...]
    o_ref[...] = cot_ref[...] + inv_std * (
        scaled
        - jnp.mean(scaled, axis=-1, keepdims=True)
        - normed * jnp.mean(scaled * normed, axis=-1, keepdims=True)
    )


def to_shards(values):
    return [hop(values[k - 1], "shard", N_SHARD, k) for k in range(1, N_SHARD)]


def to_chips(values):
    return [hop(values[k - 1], "rep", N_REP, 2 * k) for k in range(1, 4)]


def gather_chips(own):
    near = [own] + to_chips([own] * 3)
    return near + [hop(piece, "rep", N_REP, 1) for piece in near]


def sum_rep(keep, got, *earlier):
    parts = [keep[k] + got[k].astype(f32) for k in range(4)]
    sent = [part.astype(bf16) for part in parts[1:]]
    if earlier:
        sent = [after(part, *earlier) for part in sent]
    return [parts[0]] + to_chips(sent)


def after(value, *others):
    return lax.optimization_barrier((value,) + others)[0]


def shards(
    block_in,
    cotangent,
    segments,
    qkv_weight,
    out_weight,
    up_weight,
    down_weight,
    vectors,
    first_qkv,
    first_out,
    first_up,
    first_down,
    first_vec,
    second_qkv,
    second_out,
    second_up,
    second_down,
    second_vec,
):
    tok_count = block_in.shape[0]
    rep = lax.axis_index("rep")
    shard = lax.axis_index("shard")
    seq_len = tok_count * N_SHARD
    rows = qkv_weight.shape[0]
    units = down_weight.shape[0]
    n_vec, cols = vectors.shape
    masks = np.array([0, 2, 4, 6, 1, 3, 5, 7], np.int32)
    spots = np.argsort(masks)
    device = np.arange(N_REP)
    places = spots[device[:, None] ^ device[None, :]].astype(np.int32)
    orders = (device[:, None] ^ masks[None, :]).astype(np.int32)
    near = shard ^ jnp.arange(N_SHARD, dtype=jnp.int32)
    table = jnp.asarray(np.concatenate([orders, places], axis=1))
    scalars = jnp.concatenate(
        [lax.dynamic_index_in_dim(table, rep, 0, keepdims=False), near, shard[None]]
    ).astype(jnp.int32)

    share = HEAD // rows
    pair = LANES // HEAD
    moves = []
    for at in range(N_REP * N_SHARD):
        head, part = at // share, at % share
        owner = (head // pair) % N_SHARD
        local = (head // (pair * N_SHARD)) * pair + head % pair
        moves.append((at, (local * share + part) * N_SHARD + owner))

    own_cols = [((rows, QKV + UP + LANES), bf16)] * N_SHARD
    square = pltpu.VMEM((LANES, LANES), f32)
    packed = single(
        pack_body, own_cols, scalars, [qkv_weight, up_weight, vectors], 1, "pack", [square]
    )
    got_cols = to_shards(packed[1:])
    out_rows = lax.ppermute(out_weight.astype(bf16), ("rep", "shard"), moves)
    down_own = down_weight.astype(bf16)
    late_down = after(down_own, out_rows, got_cols[0])
    downs = [
        down_own,
        hop(down_own, "rep", N_REP, 2),
        hop(late_down, "rep", N_REP, 4),
    ]
    (normed_own,) = single(
        norm_body,
        [((tok_count, D), bf16)],
        scalars,
        [block_in],
        1,
        "norm",
        [pltpu.VMEM((tok_count, D), f32)],
    )
    (in_rows,) = single(
        join_body,
        [((N_SHARD * rows, QKV + UP + OUT + LANES), bf16)],
        scalars,
        [packed[0], *got_cols[:2], after(got_cols[2], normed_own), out_rows],
        1,
        "join",
    )
    in_rows = after(in_rows, *downs[1:])
    normed = [normed_own] + to_shards([after(normed_own, *got_cols)] * 3)
    pieces = gather_chips(in_rows)
    downs.append(hop(after(down_own, *pieces[1:4]), "rep", N_REP, 6))
    downs = downs + [hop(piece, "rep", N_REP, 1) for piece in downs]
    dy_all = lax.all_gather(cotangent.astype(bf16), "shard", axis=0, tiled=True)

    rope_parts = jnp.asarray(rope_lanes(seq_len)).reshape(N_SHARD, tok_count, 3 * LANES)
    rope = jnp.concatenate(
        [lax.dynamic_index_in_dim(rope_parts, near[k], 0, keepdims=False) for k in range(N_SHARD)]
    )
    seg_row = jnp.concatenate(
        [lax.dynamic_slice(segments[0], (near[k] * tok_count,), (tok_count,)) for k in range(N_SHARD)]
    )
    positions = (near[:, None] * tok_count + jnp.arange(tok_count)[None, :]).reshape(seq_len)
    allowed = (seg_row[:, None] == seg_row[None, :]) & (positions[None, :] <= positions[:, None])
    mask = jnp.where(allowed, 0.0, HIDDEN).astype(f32)

    out_whole, h_one, h_two, qkv16, act16, slope, vec_rel, last = front(
        scalars, normed, pieces, rope
    )
    block16 = ((tok_count, D), bf16)
    block32 = ((tok_count, D), f32)
    half = D // 2
    dy_seq, d_mixed16, d_up16, up_sum = single(
        hidden_body,
        [((seq_len, D), bf16), ((seq_len, OUT), bf16), ((seq_len, UP), bf16), ((8, UP), f32)],
        scalars,
        [dy_all, *downs, slope, out_whole],
        4,
        "hidden",
    )

    def split_terms(left, right):
        sent = contract_rows(left[:, half:], right).astype(bf16).reshape(4, LANES, D)
        got = hop(sent, "rep", N_REP, 1)
        keep = contract_rows(left[:, :half], right).reshape(4, LANES, D)
        return keep, got

    down_keep, down_got = split_terms(act16, dy_seq)
    up_keep, up_got = split_terms(h_two, d_up16)
    down_parts = sum_rep(down_keep, down_got)
    up_parts = sum_rep(up_keep, up_got, *down_parts[1:])
    mixed16 = mix_heads(after(qkv16, down_got, up_got), mask)
    (branches,) = single(
        branch_body,
        [((seq_len, D), bf16)],
        scalars,
        [mixed16, act16, out_whole, *downs],
        3,
        "branch",
    )
    d_mixed16 = after(d_mixed16, branches, *down_parts[1:])
    branches = lax.psum_scatter(branches, "shard", scatter_dimension=0, tiled=True)
    d_qkv16, qkv_sum = attend_back(qkv16, d_mixed16, mixed16, mask, rope)
    d_qkv16 = after(d_qkv16, *up_parts[1:])

    e_own, *e_sent, norm_sum = single(
        back_body,
        [block32, block16, block16, block16, ((8, D), f32)],
        scalars,
        [d_qkv16, d_up16, vec_rel, *normed, *pieces],
        5,
        "back",
    )
    e_got = to_shards(e_sent)
    cot_sum = jnp.sum(cotangent, axis=0, keepdims=True)
    wide = QKV + OUT + LANES
    qkv_keep, qkv_sent = single(
        terms_body,
        [((half, wide), f32), ((half, wide), bf16)],
        scalars,
        [h_one, d_qkv16, mixed16, dy_seq, norm_sum, qkv_sum, up_sum, cot_sum],
        4,
        "terms",
        [pltpu.VMEM((LANES, D), f32), pltpu.VMEM((OUT, D), f32)],
    )
    qkv_got = hop(qkv_sent.reshape(4, LANES, wide), "rep", N_REP, 1)
    qkv_parts = sum_rep(qkv_keep.reshape(4, LANES, wide), qkv_got, *up_parts[1:])
    narrow = (rows, QKV + UP + LANES)
    g_own, g1, g2, g3, out_sum = single(
        fold_body,
        [(narrow, f32), (narrow, bf16), (narrow, bf16), (narrow, bf16), ((rows, D), f32)],
        scalars,
        [*up_parts, *qkv_parts],
        1,
        "fold",
        [pltpu.VMEM((LANES, UP), f32), pltpu.VMEM((LANES, wide), f32)],
    )
    g_got = to_shards([g1, g2, g3])
    grad_out = lax.ppermute(out_sum, ("rep", "shard"), [(b, a) for a, b in moves])
    block_out = block_in + branches.astype(f32) + last[0]
    grad_down = (
        down_parts[0]
        + down_parts[1].astype(f32)
        + down_parts[2].astype(f32)
        + down_parts[3].astype(f32)
    )
    (grad_input,) = single(
        finish_body,
        [block32],
        scalars,
        [e_own, *e_got, block_in, cotangent],
        2,
        "finish",
        [pltpu.VMEM((tok_count, D), f32)],
    )
    qkv_shape = (qkv_weight.shape, f32)
    up_shape = (up_weight.shape, f32)
    vec_shape = (vectors.shape, f32)
    (
        grad_qkv,
        new_qkv,
        new_first_qkv,
        new_second_qkv,
        grad_up,
        new_up,
        new_first_up,
        new_second_up,
        grad_vec,
        new_vec,
        new_first_vec,
        new_second_vec,
    ) = single(
        adam_body,
        [qkv_shape] * 4 + [up_shape] * 4 + [vec_shape] * 4,
        scalars,
        [
            g_own,
            *g_got,
            qkv_weight,
            first_qkv,
            second_qkv,
            up_weight,
            first_up,
            second_up,
            vectors,
            first_vec,
            second_vec,
        ],
        3,
        "adam",
        [pltpu.VMEM((N_SHARD,) + narrow, f32), square],
    )

    new_out, new_first_out, new_second_out = adam_update(
        out_weight, grad_out, first_out, second_out, LR_MATRIX, WEIGHT_DECAY
    )
    new_down, new_first_down, new_second_down = adam_update(
        down_weight, grad_down, first_down, second_down, LR_MATRIX, WEIGHT_DECAY
    )
    return (
        block_out,
        grad_input,
        grad_qkv,
        grad_out,
        grad_up,
        grad_down,
        grad_vec,
        new_qkv,
        new_out,
        new_up,
        new_down,
        new_vec,
        new_first_qkv,
        new_first_out,
        new_first_up,
        new_first_down,
        new_first_vec,
        new_second_qkv,
        new_second_out,
        new_second_up,
        new_second_down,
        new_second_vec,
    )


def solution(mesh):
    aligned = mesh.shape["rep"] == N_REP and mesh.shape["shard"] == N_SHARD
    return jax.shard_map(
        shards if aligned else general,
        mesh=mesh,
        in_specs=(
            P(("rep", "shard"), None),
            P(("rep", "shard"), None),
            P("rep", None),
            P(("rep", "shard"), None),
            P(("rep", "shard"), None),
            P(("rep", "shard"), None),
            P(("rep", "shard"), None),
            P(None, ("rep", "shard")),
            P(("rep", "shard"), None),
            P(("rep", "shard"), None),
            P(("rep", "shard"), None),
            P(("rep", "shard"), None),
            P(None, ("rep", "shard")),
            P(("rep", "shard"), None),
            P(("rep", "shard"), None),
            P(("rep", "shard"), None),
            P(("rep", "shard"), None),
            P(None, ("rep", "shard")),
        ),
        out_specs=(
            P(("rep", "shard"), None),
            P(("rep", "shard"), None),
            P(("rep", "shard"), None),
            P(("rep", "shard"), None),
            P(("rep", "shard"), None),
            P(("rep", "shard"), None),
            P(None, ("rep", "shard")),
            P(("rep", "shard"), None),
            P(("rep", "shard"), None),
            P(("rep", "shard"), None),
            P(("rep", "shard"), None),
            P(None, ("rep", "shard")),
            P(("rep", "shard"), None),
            P(("rep", "shard"), None),
            P(("rep", "shard"), None),
            P(("rep", "shard"), None),
            P(None, ("rep", "shard")),
            P(("rep", "shard"), None),
            P(("rep", "shard"), None),
            P(("rep", "shard"), None),
            P(("rep", "shard"), None),
            P(None, ("rep", "shard")),
        ),
        check_vma=False,
    )
```

```python
import jax
import jax.numpy as jnp
import numpy as np
from jax import lax
from jax.experimental import pallas as pl
from jax.experimental.pallas import tpu as pltpu
from jax.sharding import PartitionSpec as P

D = 1024
HEADS = 16
HEAD = D // HEADS
FF = 4096
ROT = 16
STEP = 10
LANES = 128


LN_EPS = 1e-05
BETA_ONE = 0.9
BETA_TWO = 0.95
ADAM_EPS = 1e-08
LR_MATRIX = 0.03
LR_VECTOR = 0.2
WEIGHT_DECAY = 0.01
ROPE_BASE = 10000.0
INV_ROOT_TWO = 0.7071067811865476
INV_ROOT_TAU = 0.3989422804014327
HIDDEN = -1e30
bf16 = jnp.bfloat16
f32 = jnp.float32
TILE = 256


def adam_update(param, grad, first, second, rate, decay):
    first_new = BETA_ONE * first + (1.0 - BETA_ONE) * grad
    second_new = BETA_TWO * second + (1.0 - BETA_TWO) * grad * grad
    first_hat = first_new / (1.0 - BETA_ONE**STEP)
    second_hat = second_new / (1.0 - BETA_TWO**STEP)
    return (
        param - rate * (first_hat / (jnp.sqrt(second_hat) + ADAM_EPS) + decay * param),
        first_new,
        second_new,
    )


def contract_rows(left, right):
    return lax.dot_general(left, right, (((0,), (0,)), ((), ())), preferred_element_type=f32)


def contract_cols(left, right):
    return lax.dot_general(left, right, (((1,), (1,)), ((), ())), preferred_element_type=f32)


def plain_dot(left, right):
    return jnp.dot(left, right, preferred_element_type=f32)


def rope_lanes(seq_len):
    half = ROT // 2
    freqs = (ROPE_BASE ** (-(2.0 * np.arange(half, dtype=np.float32) / ROT))).astype(np.float32)
    angles = np.arange(seq_len, dtype=np.float32)[:, None] * freqs[None, :]
    cosines, sines = np.cos(angles), np.sin(angles)
    keep = np.ones((seq_len, HEAD), np.float32)
    up = np.zeros((seq_len, HEAD), np.float32)
    down = np.zeros((seq_len, HEAD), np.float32)
    keep[:, :half], keep[:, half:ROT] = cosines, cosines
    up[:, :half] = -sines
    down[:, half:ROT] = sines
    reps = LANES // HEAD
    return np.concatenate([np.tile(t, (1, reps)) for t in (keep, up, down)], axis=1)


def turn(values, table, sign):
    half = ROT // 2
    above = pltpu.roll(values, LANES - half, 1)
    below = pltpu.roll(values, half, 1)
    moved = above * table[:, LANES : 2 * LANES] + below * table[:, 2 * LANES :]
    return values * table[:, :LANES] + sign * moved


def params(mib):
    return pltpu.CompilerParams(vmem_limit_bytes=mib << 20)


def cost(micros):
    return pl.CostEstimate(flops=int(micros * 1.15e9), bytes_accessed=1 << 20, transcendentals=0)


def whole_spec(shape):
    return pl.BlockSpec(shape, lambda *_: (0,) * len(shape))


def rope_tables(positions):
    half_rot = ROT // 2
    freqs = ROPE_BASE ** (-(2.0 * jnp.arange(half_rot).astype(jnp.float32) / ROT))
    angles = positions.astype(jnp.float32)[:, None] * freqs[None, :]
    return (jnp.cos(angles)[:, None, :], jnp.sin(angles)[:, None, :])


def rotate(heads, cosines, sines):
    half_rot = ROT // 2
    lower = heads[..., :half_rot]
    upper = heads[..., half_rot:ROT]
    return jnp.concatenate(
        [lower * cosines - upper * sines, upper * cosines + lower * sines, heads[..., ROT:]],
        axis=-1,
    )


def unrotate(heads, cosines, sines):
    half_rot = ROT // 2
    lower = heads[..., :half_rot]
    upper = heads[..., half_rot:ROT]
    return jnp.concatenate(
        [lower * cosines + upper * sines, upper * cosines - lower * sines, heads[..., ROT:]],
        axis=-1,
    )


def gelu_value(inner):
    return 0.5 * inner * (1.0 + jax.scipy.special.erf(inner * INV_ROOT_TWO))


def gelu_slope(inner):
    return (
        0.5 * (1.0 + jax.scipy.special.erf(inner * INV_ROOT_TWO))
        + inner * jnp.exp(-0.5 * inner * inner) * INV_ROOT_TAU
    )


def hop(value, axis, size, mask):
    return lax.ppermute(value, axis, [(i, i ^ mask) for i in range(size)])


def pick(blocks, index, axis=0):
    return lax.dynamic_index_in_dim(blocks, index, axis, keepdims=False)


def stages(size):
    bits = size.bit_length() - 1
    found = []
    while bits > 0:
        take = 2 if bits >= 2 else 1
        bits -= take
        found.append((bits, 1 << take))
    return found


def gather_axis(own, axis, me, size):
    if size > 16:
        return lax.all_gather(own, axis)
    pieces = {0: own}
    for shift, count in stages(size):
        more = dict(pieces)
        for k in range(1, count):
            for mask, piece in pieces.items():
                more[mask ^ (k << shift)] = hop(piece, axis, size, k << shift)
        pieces = more
    whole = jnp.zeros((size,) + own.shape, own.dtype)
    for mask in range(size):
        whole = lax.dynamic_update_index_in_dim(whole, pieces[mask], me ^ mask, 0)
    return whole


def exchange_axis(blocks, axis, me, size, wire):
    got = [(0, pick(blocks, me))]
    for mask in range(1, size):
        got.append((mask, hop(pick(blocks, me ^ mask).astype(wire), axis, size, mask)))
    return got


def reduce_axis(blocks, axis, me, size, wire):
    current = blocks
    for shift, count in reversed(stages(size)):
        left = current.shape[0] // count
        view = current.reshape((left, count) + current.shape[1:])
        digit = (me >> shift) & (count - 1)
        total = pick(view, digit, 1)
        for k in range(1, count):
            sent = pick(view, digit ^ k, 1).astype(wire)
            total = total + hop(sent, axis, size, k << shift).astype(jnp.float32)
        current = total
    return current[0]


def general(
    block_in,
    cotangent,
    segments,
    qkv_weight,
    out_weight,
    up_weight,
    down_weight,
    vectors,
    first_qkv,
    first_out,
    first_up,
    first_down,
    first_vec,
    second_qkv,
    second_out,
    second_up,
    second_down,
    second_vec,
):
    tok_count = block_in.shape[0]
    n_rep = lax.axis_size("rep")
    n_shard = lax.axis_size("shard")
    rep = lax.axis_index("rep")
    shard = lax.axis_index("shard")
    seq_len = tok_count * n_shard
    head_dim = D // HEADS
    own_heads = HEADS // n_shard
    own_feats = own_heads * head_dim
    rows = qkv_weight.shape[0]
    units = down_weight.shape[0]
    own_units = units * n_rep
    cols = vectors.shape[1]
    score_scale = head_dim ** (-0.5)

    qkv_cols = qkv_weight.astype(bf16).reshape(rows, 3, own_heads, n_shard, head_dim)
    qkv_cols = qkv_cols.transpose(3, 0, 1, 2, 4).reshape(n_shard, rows, 3 * own_feats)
    up_cols = up_weight.astype(bf16).reshape(rows, n_rep, n_shard, units)
    up_cols = up_cols.transpose(2, 0, 1, 3).reshape(n_shard, rows, own_units)
    in_cols = jnp.concatenate([qkv_cols, up_cols], axis=2)
    in_rows = jnp.zeros_like(in_cols)
    for mask, piece in exchange_axis(in_cols, "shard", shard, n_shard, bf16):
        in_rows = lax.dynamic_update_index_in_dim(in_rows, piece, shard ^ mask, 0)
    in_rows = in_rows.reshape(n_shard * rows, 3 * own_feats + own_units)

    center = block_in - jnp.mean(block_in, axis=-1, keepdims=True)
    inv_std = lax.rsqrt(jnp.mean(center * center, axis=-1, keepdims=True) + LN_EPS)
    normed = center * inv_std
    normed_seq = gather_axis(normed.astype(bf16), "shard", shard, n_shard).reshape(seq_len, D)
    normed_seq = normed_seq.astype(f32)

    vec_some = gather_axis(vectors, "shard", shard, n_shard)
    vec_all = gather_axis(vec_some, "rep", rep, n_rep)
    vec_all = vec_all.transpose(2, 0, 1, 3).reshape(vectors.shape[0], D)

    in_whole = gather_axis(in_rows, "rep", rep, n_rep).reshape(D, 3 * own_feats + own_units)
    upstream16 = gather_axis(cotangent.astype(bf16), "shard", shard, n_shard).reshape(seq_len, D)
    down_whole = gather_axis(down_weight.astype(bf16), "rep", rep, n_rep).reshape(own_units, D)
    share = head_dim // rows
    moves = []
    for device in range(n_rep * n_shard):
        head, part = device // share, device % share
        moves.append((device, ((head // n_shard) * share + part) * n_shard + head % n_shard))
    out_rows = lax.ppermute(out_weight.astype(bf16), ("rep", "shard"), moves)
    out_whole = gather_axis(out_rows, "rep", rep, n_rep).reshape(own_feats, D)

    per_row = FF // D
    gain_one, shift_one, gain_two, shift_two = (vec_all[0], vec_all[1], vec_all[2], vec_all[3])
    qkv_bias = pick(vec_all[4:7].reshape(3, own_heads, n_shard, head_dim), shard, 2).reshape(
        3 * own_feats
    )
    up_bias = pick(vec_all[8 : 8 + per_row].reshape(n_rep, n_shard, units), shard, 1).reshape(
        own_units
    )
    out_bias = vec_all[7]
    down_bias = vec_all[8 + per_row]

    h_one = (normed_seq * gain_one + shift_one).astype(bf16)
    h_two = (normed_seq * gain_two + shift_two).astype(bf16)
    qkv_whole = in_whole[:, : 3 * own_feats]
    up_whole = in_whole[:, 3 * own_feats :]
    qkv_lin = jnp.dot(h_one, qkv_whole, preferred_element_type=f32) + qkv_bias
    up_lin = jnp.dot(h_two, up_whole, preferred_element_type=f32) + up_bias

    positions = jnp.arange(seq_len)
    cosines, sines = rope_tables(positions)

    def heads_of(values):
        return values.reshape(seq_len, own_heads, head_dim)

    query16 = rotate(heads_of(qkv_lin[:, :own_feats]), cosines, sines).astype(bf16)
    key16 = rotate(heads_of(qkv_lin[:, own_feats : 2 * own_feats]), cosines, sines).astype(bf16)
    value16 = heads_of(qkv_lin[:, 2 * own_feats :]).astype(bf16)
    seg_row = segments[0]
    allowed = (seg_row[:, None] == seg_row[None, :]) & (positions[None, :] <= positions[:, None])
    scores = jnp.where(
        allowed[None],
        jnp.einsum("qhd,khd->hqk", query16, key16, preferred_element_type=f32) * score_scale,
        -jnp.inf,
    )
    row_max = jnp.max(scores, axis=-1, keepdims=True)
    expo = jnp.exp(scores - row_max)
    row_sum = jnp.sum(expo, axis=-1, keepdims=True)
    log_total = row_max + jnp.log(row_sum)
    probs16 = (expo / row_sum).astype(bf16)
    mixed16 = (
        jnp.einsum("hqk,khd->qhd", probs16, value16, preferred_element_type=f32)
        .reshape(seq_len, own_feats)
        .astype(bf16)
    )
    act16 = gelu_value(up_lin).astype(bf16)
    branches = jnp.dot(mixed16, out_whole, preferred_element_type=f32)
    branches = branches + jnp.dot(act16, down_whole, preferred_element_type=f32)
    branches = reduce_axis(
        branches.reshape(n_shard, tok_count, D), "shard", shard, n_shard, bf16
    )
    block_out = block_in + branches + out_bias + down_bias

    term_down = contract_rows(act16, upstream16)
    sum_down = reduce_axis(term_down.reshape(n_rep, units, D), "rep", rep, n_rep, bf16)
    term_out = contract_rows(mixed16, upstream16)
    sum_out = reduce_axis(term_out.reshape(n_rep, rows, D), "rep", rep, n_rep, bf16)
    grad_out = lax.ppermute(sum_out, ("rep", "shard"), [(b, a) for a, b in moves])
    grad_down = sum_down
    d_act = contract_cols(upstream16, down_whole)
    d_mixed16 = heads_of(contract_cols(upstream16, out_whole)).astype(bf16)
    d_up = d_act * gelu_slope(up_lin)
    d_up16 = d_up.astype(bf16)
    term_up = contract_rows(h_two, d_up16)
    sum_up = reduce_axis(
        term_up.reshape(n_rep, n_shard * rows, own_units), "rep", rep, n_rep, bf16
    )

    def back_rows(sums, width):
        whole = jnp.zeros((n_shard, rows, width), f32)
        blocks = sums.reshape(n_shard, rows, width)
        for mask, piece in exchange_axis(blocks, "shard", shard, n_shard, bf16):
            whole = lax.dynamic_update_index_in_dim(whole, piece.astype(f32), shard ^ mask, 0)
        return whole

    grad_up = back_rows(sum_up, own_units).reshape(n_shard, rows, n_rep, units)
    grad_up = grad_up.transpose(1, 2, 0, 3).reshape(rows, FF)

    row_delta = jnp.sum(
        d_mixed16.astype(f32) * heads_of(mixed16).astype(f32),
        axis=-1,
    ).T[:, :, None]
    probs_again = jnp.exp(scores - log_total)
    d_probs = jnp.einsum("qhd,khd->hqk", d_mixed16, value16, preferred_element_type=f32)
    d_scores16 = (probs_again * (d_probs - row_delta) * score_scale).astype(bf16)
    probs_back16 = probs_again.astype(bf16)
    d_query = jnp.einsum("hqk,khd->qhd", d_scores16, key16, preferred_element_type=f32)
    d_keys = jnp.einsum("hqk,qhd->khd", d_scores16, query16, preferred_element_type=f32)
    d_values = jnp.einsum("hqk,qhd->khd", probs_back16, d_mixed16, preferred_element_type=f32)
    d_qkv = jnp.concatenate(
        [
            unrotate(d_query, cosines, sines).reshape(seq_len, own_feats),
            unrotate(d_keys, cosines, sines).reshape(seq_len, own_feats),
            d_values.reshape(seq_len, own_feats),
        ],
        axis=1,
    )
    d_qkv16 = d_qkv.astype(bf16)
    term_qkv = contract_rows(h_one, d_qkv16)
    sum_qkv = reduce_axis(
        term_qkv.reshape(n_rep, n_shard * rows, 3 * own_feats), "rep", rep, n_rep, bf16
    )
    grad_qkv = back_rows(sum_qkv, 3 * own_feats)
    grad_qkv = grad_qkv.reshape(n_shard, rows, 3, own_heads, head_dim)
    grad_qkv = grad_qkv.transpose(1, 2, 3, 0, 4).reshape(rows, 3 * D)

    d_one = contract_cols(d_qkv16, qkv_whole)
    d_two = contract_cols(d_up16, up_whole)
    scaled = d_one * gain_one + d_two * gain_two
    scaled = reduce_axis(scaled.reshape(n_shard, tok_count, D), "shard", shard, n_shard, bf16)
    grad_input = cotangent + inv_std * (
        scaled
        - jnp.mean(scaled, axis=-1, keepdims=True)
        - normed * jnp.mean(scaled * normed, axis=-1, keepdims=True)
    )

    mine = jnp.arange(n_shard) == shard
    cot_sum = jnp.sum(cotangent, axis=0)
    bias_qkv = jnp.where(
        mine[None, None, :, None],
        jnp.sum(d_qkv, axis=0).reshape(3, own_heads, 1, head_dim),
        0.0,
    ).reshape(3, D)
    bias_up = jnp.where(
        mine[None, :, None], jnp.sum(d_up, axis=0).reshape(n_rep, 1, units), 0.0
    ).reshape(per_row, D)
    vec_terms = jnp.concatenate(
        [
            jnp.sum(d_one * normed_seq, axis=0)[None],
            jnp.sum(d_one, axis=0)[None],
            jnp.sum(d_two * normed_seq, axis=0)[None],
            jnp.sum(d_two, axis=0)[None],
            bias_qkv,
            cot_sum[None],
            bias_up,
            cot_sum[None],
        ],
        axis=0,
    )
    vec_blocks = vec_terms.reshape(vectors.shape[0], n_rep, n_shard, cols).transpose(1, 2, 0, 3)
    grad_vec = reduce_axis(
        reduce_axis(vec_blocks, "rep", rep, n_rep, f32), "shard", shard, n_shard, f32
    )

    new_qkv, new_first_qkv, new_second_qkv = adam_update(
        qkv_weight, grad_qkv, first_qkv, second_qkv, LR_MATRIX, WEIGHT_DECAY
    )
    new_out, new_first_out, new_second_out = adam_update(
        out_weight, grad_out, first_out, second_out, LR_MATRIX, WEIGHT_DECAY
    )
    new_up, new_first_up, new_second_up = adam_update(
        up_weight, grad_up, first_up, second_up, LR_MATRIX, WEIGHT_DECAY
    )
    new_down, new_first_down, new_second_down = adam_update(
        down_weight, grad_down, first_down, second_down, LR_MATRIX, WEIGHT_DECAY
    )
    new_vec, new_first_vec, new_second_vec = adam_update(
        vectors, grad_vec, first_vec, second_vec, LR_VECTOR, 0.0
    )
    return (
        block_out,
        grad_input,
        grad_qkv,
        grad_out,
        grad_up,
        grad_down,
        grad_vec,
        new_qkv,
        new_out,
        new_up,
        new_down,
        new_vec,
        new_first_qkv,
        new_first_out,
        new_first_up,
        new_first_down,
        new_first_vec,
        new_second_qkv,
        new_second_out,
        new_second_up,
        new_second_down,
        new_second_vec,
    )


ROOM = {
    "pack": 6,
    "norm": 4,
    "join": 4,
    "branch": 16,
    "hidden": 22,
    "back": 28,
    "terms": 20,
    "mlp": 28,
    "fold": 16,
    "finish": 10,
    "adam": 22,
}


def single(body, outs, prefetch, ins, micros, name, scratch=()):
    shapes = tuple(jax.ShapeDtypeStruct(s, d) for s, d in outs)
    return pl.pallas_call(
        body,
        out_shape=shapes,
        grid_spec=pltpu.PrefetchScalarGridSpec(
            num_scalar_prefetch=1,
            grid=(1,),
            in_specs=[whole_spec(a.shape) for a in ins],
            out_specs=tuple(whole_spec(s.shape) for s in shapes),
            scratch_shapes=list(scratch),
        ),
        compiler_params=params(ROOM[name]),
        cost_estimate=cost(micros),
        name=name,
    )(prefetch, *ins)


def lane_block(index):
    return pl.ds(pl.multiple_of(index * LANES, LANES), LANES)


def row_block(index, size):
    return pl.ds(pl.multiple_of(index * size, size), size)


N_REP = 8
N_SHARD = 4
ORDER = 0
PLACE = N_REP
NEAR = 2 * N_REP
SHARD = NEAR + N_SHARD
QKV = 3 * TILE
UP = D
OUT = TILE


def pack_body(s_ref, qkv_ref, up_ref, vec_ref, *refs):
    outs, turn_ref = refs[:-1], refs[-1]
    count, cols = vec_ref.shape
    turn_ref[...] = jnp.zeros_like(turn_ref)
    vec = vec_ref[...]
    for i in range(3):
        part = vec.astype(bf16).astype(f32)
        turn_ref[16 * i : 16 * i + count, :cols] = part
        vec = vec - part
    vec16 = turn_ref[...].T[:cols, :].astype(bf16)
    for k in range(N_SHARD):
        t = s_ref[NEAR + k]
        o_ref = outs[k]
        for c in range(QKV // LANES):
            o_ref[:, c * LANES : (c + 1) * LANES] = qkv_ref[:, lane_block(c * N_SHARD + t)].astype(bf16)
        for c in range(UP // LANES):
            at = QKV + c * LANES
            o_ref[:, at : at + LANES] = up_ref[:, lane_block(c * N_SHARD + t)].astype(bf16)
        o_ref[:, QKV + UP :] = vec16


def norm_body(s_ref, x_ref, o_ref, n_ref):
    x = x_ref[...]
    center = x - jnp.mean(x, axis=-1, keepdims=True)
    inv_std = lax.rsqrt(jnp.mean(center * center, axis=-1, keepdims=True) + LN_EPS)
    n_ref[...] = center * inv_std
    for i in range(N_REP):
        o_ref[:, i * LANES : (i + 1) * LANES] = n_ref[:, lane_block(s_ref[ORDER + i])].astype(bf16)


def join_body(s_ref, *refs):
    out_ref, o_ref = refs[N_SHARD], refs[N_SHARD + 1]
    rows = out_ref.shape[0]
    for k in range(N_SHARD):
        at = row_block(s_ref[NEAR + k], rows)
        o_ref[at, : QKV + UP] = refs[k][:, : QKV + UP]
        o_ref[at, QKV + UP + OUT :] = refs[k][:, QKV + UP :]
    for c in range(D // OUT):
        o_ref[c * rows : (c + 1) * rows, QKV + UP : QKV + UP + OUT] = out_ref[:, c * OUT : (c + 1) * OUT]


def bias_places(s_ref):
    shard = s_ref[SHARD]
    found = []
    for c in range(QKV // LANES):
        found.append((4 + c // 2, s_ref[PLACE + (c % 2) * N_SHARD + shard], c * LANES))
    for c in range(UP // LANES):
        found.append((8 + c // 2, s_ref[PLACE + (c % 2) * N_SHARD + shard], QKV + c * LANES))
    return found


def front_body(s_ref, *refs):
    n_refs, refs = refs[:N_SHARD], refs[N_SHARD:]
    w_refs, refs = refs[:N_REP], refs[N_REP:]
    v_refs, refs = refs[:N_REP], refs[N_REP:]
    out_refs, refs = refs[:N_REP], refs[N_REP:]
    rope_ref, whole_ref, h1_ref, h2_ref, qkv_ref, act_ref, slope_ref, vec_ref, last_ref, bias_ref = refs
    j = pl.program_id(0)
    rows = n_refs[0].shape[0]

    @pl.when(j == 0)
    def _():
        for i in range(N_REP):
            parts = v_refs[i][...].astype(f32).T
            vec_ref[:, i * LANES : (i + 1) * LANES] = (parts[0:16] + parts[16:32]) + parts[32:48]
        for k in range(N_SHARD):
            normed = n_refs[k][...].astype(f32)
            at = slice(k * rows, (k + 1) * rows)
            h1_ref[at, :] = (normed * vec_ref[0:1, :] + vec_ref[1:2, :]).astype(bf16)
            h2_ref[at, :] = (normed * vec_ref[2:3, :] + vec_ref[3:4, :]).astype(bf16)
        for row, block, at in bias_places(s_ref):
            bias_ref[at // TILE, 0:1, at % TILE : at % TILE + LANES] = vec_ref[row : row + 1, lane_block(block)]
        both = vec_ref[7:8, :] + vec_ref[12:13, :]
        for i in range(N_REP):
            last_ref[0:1, lane_block(s_ref[ORDER + i])] = both[:, i * LANES : (i + 1) * LANES]
        chunks = D // OUT
        size = out_refs[0].shape[0] // chunks
        for i in range(N_REP):
            at = row_block(s_ref[ORDER + i], size)
            for c in range(chunks):
                whole_ref[at, c * OUT : (c + 1) * OUT] = out_refs[i][c * size : (c + 1) * size, :]

    def product(h_ref):
        total = bias_ref[j, 0:1, :]
        for i in range(0, N_REP, 2):
            weights = jnp.concatenate([w_refs[i][...], w_refs[i + 1][...]], axis=0)
            total = total + plain_dot(h_ref[:, i * LANES : (i + 2) * LANES], weights)
        return total

    @pl.when(j < 2)
    def _():
        lin = product(h1_ref)
        for c in range(0, TILE, LANES):
            qkv_ref[:, c : c + LANES] = turn(lin[:, c : c + LANES], rope_ref[...], 1.0).astype(bf16)

    @pl.when(j == 2)
    def _():
        qkv_ref[...] = product(h1_ref).astype(bf16)

    @pl.when(j > 2)
    def _():
        lin = product(h2_ref)
        above = 0.5 * (1.0 + lax.erf(lin * INV_ROOT_TWO))
        act = (lin * above).astype(bf16)
        slope = above + lin * jnp.exp(-0.5 * lin * lin) * INV_ROOT_TAU
        for c in range(2):
            at = lane_block(s_ref[PLACE + (j - 3) * 2 + c])
            act_ref[:, at] = act[:, c * LANES : (c + 1) * LANES]
            slope_ref[:, at] = slope[:, c * LANES : (c + 1) * LANES]


def front(scalars, normed, pieces, rope):
    tokens = rope.shape[0]
    block = pieces[0].shape[0]
    shapes = (
        ((OUT, D), bf16),
        ((tokens, D), bf16),
        ((tokens, D), bf16),
        ((tokens, QKV), bf16),
        ((tokens, UP), bf16),
        ((tokens, UP), f32),
        ((16, D), f32),
        ((8, D), f32),
    )
    specs = [whole_spec(s) for s, _ in shapes]
    specs[3] = pl.BlockSpec((tokens, TILE), lambda j, s: (0, jnp.minimum(j, 2)))
    return pl.pallas_call(
        front_body,
        out_shape=tuple(jax.ShapeDtypeStruct(s, d) for s, d in shapes),
        grid_spec=pltpu.PrefetchScalarGridSpec(
            num_scalar_prefetch=1,
            grid=((QKV + UP) // TILE,),
            in_specs=[whole_spec(n.shape) for n in normed]
            + [pl.BlockSpec((block, TILE), lambda j, s: (0, j))] * N_REP
            + [pl.BlockSpec((block, LANES), lambda j, s: (0, (QKV + UP + OUT) // LANES))] * N_REP
            + [pl.BlockSpec((block, OUT), lambda j, s: (0, (QKV + UP) // OUT))] * N_REP
            + [whole_spec(rope.shape)],
            out_specs=tuple(specs),
            scratch_shapes=[pltpu.VMEM(((QKV + UP) // TILE, 8, TILE), f32)],
        ),
        compiler_params=params(24),
        cost_estimate=cost(9),
        name="front",
    )(scalars, *normed, *pieces, *pieces, *pieces, rope)


def hidden_body(s_ref, *refs):
    dy_ref, refs = refs[0], refs[1:]
    down_refs, refs = refs[:N_REP], refs[N_REP:]
    slope_ref, whole_ref, seq_ref, dmix_ref, du_ref, sum_ref = refs
    tokens = dy_ref.shape[0] // N_SHARD
    for k in range(N_SHARD):
        seq_ref[k * tokens : (k + 1) * tokens, :] = dy_ref[row_block(s_ref[NEAR + k], tokens), :]
    dy = seq_ref[...]
    dmix_ref[...] = contract_cols(dy, whole_ref[...]).astype(bf16)
    for i in range(N_REP):
        du = contract_cols(dy, down_refs[i][...]) * slope_ref[:, i * LANES : (i + 1) * LANES]
        at = lane_block(s_ref[ORDER + i])
        du_ref[:, at] = du.astype(bf16)
        sum_ref[0:1, at] = jnp.sum(du, axis=0, keepdims=True)


def weigh(q, k, mask):
    score = contract_cols(q, k) * (HEAD ** (-0.5)) + mask
    expo = jnp.exp(score - jnp.max(score, axis=-1, keepdims=True))
    return expo * (1.0 / jnp.sum(expo, axis=-1, keepdims=True))


def only(values, mine):
    return jnp.where(mine, values, jnp.zeros_like(values))


def mix_body(q_ref, k_ref, v_ref, mask_ref, mix_ref):
    first = lax.broadcasted_iota(jnp.int32, (LANES, LANES), 1) < HEAD
    k = k_ref[...]
    v = v_ref[...]
    for c in range(0, q_ref.shape[0], LANES):
        rows = slice(c, c + LANES)
        q = q_ref[rows, :]
        mixes = []
        for mine in (first, jnp.logical_not(first)):
            prob = weigh(only(q, mine), k, mask_ref[rows, :])
            mixes.append(plain_dot(prob.astype(bf16), v))
        mix_ref[rows, :] = jnp.where(first, mixes[0], mixes[1]).astype(bf16)


def attend_body(
    q_ref, k_ref, v_ref, dm_ref, mix_ref, mask_ref, rope_ref, dqkv_ref, sum_ref, dk_ref, dv_ref
):
    pair = pl.program_id(0)
    tokens = q_ref.shape[0]
    scale = HEAD ** (-0.5)
    first = lax.broadcasted_iota(jnp.int32, (LANES, LANES), 1) < HEAD
    every = lax.broadcasted_iota(jnp.int32, (tokens, LANES), 1) < HEAD
    k = k_ref[...]
    v = v_ref[...]
    pairs = pl.num_programs(0)

    def columns(part):
        return lane_block(part * pairs + pair)

    dq_total = jnp.zeros((1, LANES), f32)
    for c in range(0, tokens, LANES):
        rows = slice(c, c + LANES)
        q = q_ref[rows, :]
        dm = dm_ref[rows, :]
        mix = mix_ref[rows, :].astype(f32)
        dqs, dks, dvs = [], [], []
        for mine in (first, jnp.logical_not(first)):
            dmh = only(dm, mine)
            prob = weigh(only(q, mine), k, mask_ref[rows, :])
            delta = jnp.sum(dmh.astype(f32) * mix, axis=-1, keepdims=True)
            d_prob = contract_cols(dmh, v)
            ds16 = (prob * (d_prob - delta) * scale).astype(bf16)
            dqs.append(plain_dot(ds16, k))
            dks.append(contract_rows(ds16, q))
            dvs.append(contract_rows(prob.astype(bf16), dm))
        dq = turn(jnp.where(first, dqs[0], dqs[1]), rope_ref[rows, :], -1.0)
        dqkv_ref[rows, columns(0)] = dq.astype(bf16)
        dq_total = dq_total + jnp.sum(dq, axis=0, keepdims=True)
        dk = jnp.where(every, dks[0], dks[1])
        dv = jnp.where(every, dvs[0], dvs[1])
        if c == 0:
            dk_ref[...] = dk
            dv_ref[...] = dv
        else:
            dk_ref[...] += dk
            dv_ref[...] += dv
    dk = turn(dk_ref[...], rope_ref[...], -1.0)
    dv = dv_ref[...]
    dqkv_ref[:, columns(1)] = dk.astype(bf16)
    dqkv_ref[:, columns(2)] = dv.astype(bf16)
    sum_ref[:, columns(0)] = dq_total
    sum_ref[:, columns(1)] = jnp.sum(dk, axis=0, keepdims=True)
    sum_ref[:, columns(2)] = jnp.sum(dv, axis=0, keepdims=True)


def pair_spec(tokens, first):
    return pl.BlockSpec((tokens, LANES), lambda j: (0, first + j))


def mix_heads(qkv, mask):
    tokens = qkv.shape[0]
    pairs = OUT // LANES
    return pl.pallas_call(
        mix_body,
        out_shape=jax.ShapeDtypeStruct((tokens, OUT), bf16),
        grid=(pairs,),
        in_specs=[pair_spec(tokens, i * pairs) for i in range(3)] + [whole_spec(mask.shape)],
        out_specs=pair_spec(tokens, 0),
        compiler_params=params(10),
        cost_estimate=cost(6),
        name="mix_heads",
    )(qkv, qkv, qkv, mask)


def attend_back(qkv, d_mix, mixed, mask, rope):
    tokens = qkv.shape[0]
    pairs = OUT // LANES
    return pl.pallas_call(
        attend_body,
        out_shape=(
            jax.ShapeDtypeStruct((tokens, QKV), bf16),
            jax.ShapeDtypeStruct((1, QKV), f32),
        ),
        grid=(pairs,),
        in_specs=[pair_spec(tokens, i * pairs) for i in range(3)]
        + [pair_spec(tokens, 0), pair_spec(tokens, 0), whole_spec(mask.shape), whole_spec(rope.shape)],
        out_specs=(whole_spec((tokens, QKV)), whole_spec((1, QKV))),
        scratch_shapes=[pltpu.VMEM((tokens, LANES), f32), pltpu.VMEM((tokens, LANES), f32)],
        compiler_params=params(12),
        cost_estimate=cost(4),
        name="attend_back",
    )(qkv, qkv, qkv, d_mix, mixed, mask, rope)


def back_body(s_ref, dqkv_ref, du_ref, vec_ref, *refs):
    n_refs, refs = refs[:N_SHARD], refs[N_SHARD:]
    w_refs, refs = refs[:N_REP], refs[N_REP:]
    own_ref, sent_refs, sum_ref = refs[0], refs[1:N_SHARD], refs[N_SHARD]
    rows = n_refs[0].shape[0]
    for i in range(0, N_REP, 2):
        cols = slice(i * LANES, (i + 2) * LANES)
        weights = jnp.concatenate([w_refs[i][:, : QKV + UP], w_refs[i + 1][:, : QKV + UP]], axis=0)
        d_one = contract_cols(dqkv_ref[...], weights[:, :QKV])
        d_two = contract_cols(du_ref[...], weights[:, QKV:])
        scaled = d_one * vec_ref[0:1, cols] + d_two * vec_ref[2:3, cols]
        own_ref[:, cols] = scaled[:rows]
        sums = [jnp.sum(d, axis=0, keepdims=True) for d in (d_one, d_two)]
        turned = [jnp.zeros_like(sums[0])] * 2
        for k in range(N_SHARD):
            at = slice(k * rows, (k + 1) * rows)
            if k:
                sent_refs[k - 1][:, cols] = scaled[at].astype(bf16)
            normed = n_refs[k][:, cols].astype(f32)
            turned = [
                t + jnp.sum(d[at] * normed, axis=0, keepdims=True)
                for t, d in zip(turned, (d_one, d_two))
            ]
        sum_ref[0:1, cols] = turned[0]
        sum_ref[1:2, cols] = sums[0]
        sum_ref[2:3, cols] = turned[1]
        sum_ref[3:4, cols] = sums[1]


def branch_body(s_ref, mix_ref, act_ref, out_ref, last_ref, x_ref, *refs):
    down_refs, refs = refs[:N_REP], refs[N_REP:]
    own_ref, sent_refs = refs[0], refs[1:]
    rows = x_ref.shape[0]
    total = plain_dot(mix_ref[...], out_ref[...])
    for i in range(0, N_REP, 2):
        weights = jnp.concatenate([down_refs[i][...], down_refs[i + 1][...]], axis=0)
        total = total + plain_dot(act_ref[:, i * LANES : (i + 2) * LANES], weights)
    own_ref[...] = x_ref[...] + total[:rows] + last_ref[0:1, :]
    for k in range(1, N_SHARD):
        sent_refs[k - 1][...] = total[k * rows : (k + 1) * rows].astype(bf16)


def terms_body(
    s_ref, h_ref, dqkv_ref, mix_ref, dy_ref, norm_ref, qkv_sum_ref, up_sum_ref, cot_ref, keep_ref, sent_ref, vec_ref, g_ref
):
    half = keep_ref.shape[0]
    keep_ref[:, :QKV] = contract_rows(h_ref[:, :half], dqkv_ref[...])
    sent_ref[:, :QKV] = contract_rows(h_ref[:, half:], dqkv_ref[...]).astype(bf16)
    g_ref[...] = contract_rows(mix_ref[...], dy_ref[...])
    vec_ref[...] = jnp.zeros_like(vec_ref)
    vec_ref[0:4, :] = norm_ref[0:4, :]
    for row, block, at in bias_places(s_ref):
        ref, at = (qkv_sum_ref, at) if at < QKV else (up_sum_ref, at - QKV)
        vec_ref[row : row + 1, lane_block(block)] = ref[0:1, at : at + LANES]
    rows = OUT // N_REP
    for i in range(N_REP):
        here = slice(i * LANES, (i + 1) * LANES)
        cot = cot_ref[0:1, lane_block(s_ref[ORDER + i])]
        vec_ref[7:8, here] = cot
        vec_ref[12:13, here] = cot
        ref = keep_ref if i < N_REP // 2 else sent_ref
        base = i * LANES % half
        found = g_ref[row_block(s_ref[ORDER + i], rows), :]
        for c in range(D // OUT):
            ref[base + c * rows : base + (c + 1) * rows, QKV : QKV + OUT] = found[
                :, c * OUT : (c + 1) * OUT
            ].astype(ref.dtype)
        ref[base : base + LANES, QKV + OUT :] = vec_ref[:, here].T.astype(ref.dtype)


def mlp_body(s_ref, act_ref, dy_ref, h_ref, du_ref, keep_ref, sent_ref):
    half = keep_ref.shape[0]
    for left, right, at in ((act_ref, dy_ref, 0), (h_ref, du_ref, D)):
        cols = slice(at, at + right.shape[1])
        sent_ref[:, cols] = contract_rows(left[:, half:], right[...]).astype(bf16)
        keep_ref[:, cols] = contract_rows(left[:, :half], right[...])


def fold_body(s_ref, *refs):
    up_refs, refs = refs[:4], refs[4:]
    qkv_refs, refs = refs[:4], refs[4:]
    own_ref, sent_refs, out_ref, up_sum, qkv_sum = refs[0], refs[1:4], refs[4], refs[5], refs[6]
    for some, total, first in ((up_refs, up_sum, D), (qkv_refs, qkv_sum, 0)):
        total[...] = sum(ref[:, first:].astype(f32) for ref in some)
    rows = own_ref.shape[0]
    for k in range(N_SHARD):
        at = row_block(s_ref[NEAR + k], rows)
        ref = own_ref if k == 0 else sent_refs[k - 1]
        ref[:, :QKV] = qkv_sum[at, :QKV].astype(ref.dtype)
        ref[:, QKV : QKV + UP] = up_sum[at, :].astype(ref.dtype)
        ref[:, QKV + UP :] = qkv_sum[at, QKV + OUT :].astype(ref.dtype)
    for c in range(D // OUT):
        out_ref[:, c * OUT : (c + 1) * OUT] = qkv_sum[c * rows : (c + 1) * rows, QKV : QKV + OUT]


def adam_body(s_ref, *refs):
    got, refs = refs[:N_SHARD], refs[N_SHARD:]
    states, vec_state, refs = (refs[0:3], refs[3:6]), refs[6:9], refs[9:]
    results, vec_result, refs = (refs[0:4], refs[4:8]), refs[8:12], refs[12:]
    all_ref, turn_ref = refs
    for k in range(N_SHARD):
        all_ref[k] = got[k][...].astype(f32)
    count, cols = vec_state[0].shape
    turn_ref[...] = jnp.zeros_like(turn_ref)
    turn_ref[:cols, :] = sum(all_ref[k, :, QKV + UP :] for k in range(N_SHARD))
    turn_ref[...] = turn_ref[...].T
    grad = turn_ref[:count, :cols]
    vec_result[0][...] = grad
    new = adam_update(vec_state[0][...], grad, vec_state[1][...], vec_state[2][...], LR_VECTOR, 0.0)
    for ref, value in zip(vec_result[1:], new):
        ref[...] = value
    first = 0
    for state, result in zip(states, results):
        for c in range(state[0].shape[1] // (N_SHARD * LANES)):
            for t in range(N_SHARD):
                grad = all_ref[s_ref[NEAR + t], :, first : first + LANES]
                at = slice((c * N_SHARD + t) * LANES, (c * N_SHARD + t + 1) * LANES)
                result[0][:, at] = grad
                new = adam_update(
                    state[0][:, at], grad, state[1][:, at], state[2][:, at], LR_MATRIX, WEIGHT_DECAY
                )
                for ref, value in zip(result[1:], new):
                    ref[:, at] = value
            first += LANES


def finish_body(s_ref, own_ref, r1_ref, r2_ref, r3_ref, x_ref, cot_ref, o_ref, e_ref):
    total = own_ref[...] + r1_ref[...].astype(f32) + r2_ref[...].astype(f32) + r3_ref[...].astype(f32)
    for i in range(N_REP):
        e_ref[:, lane_block(s_ref[ORDER + i])] = total[:, i * LANES : (i + 1) * LANES]
    x = x_ref[...]
    center = x - jnp.mean(x, axis=-1, keepdims=True)
    inv_std = lax.rsqrt(jnp.mean(center * center, axis=-1, keepdims=True) + LN_EPS)
    normed = center * inv_std
    scaled = e_ref[...]
    o_ref[...] = cot_ref[...] + inv_std * (
        scaled
        - jnp.mean(scaled, axis=-1, keepdims=True)
        - normed * jnp.mean(scaled * normed, axis=-1, keepdims=True)
    )


def to_shards(values):
    return [hop(values[k - 1], "shard", N_SHARD, k) for k in range(1, N_SHARD)]


def to_shards_late(values):
    got = [hop(values[k - 1], "shard", N_SHARD, k) for k in (1, 2)]
    return got + [hop(after(values[2], got[0]), "shard", N_SHARD, 3)]


def to_chips(values):
    return [hop(values[k - 1], "rep", N_REP, 2 * k) for k in range(1, 4)]


def gather_chips(own):
    near = [own] + to_chips([own] * 3)
    return near + [hop(piece, "rep", N_REP, 1) for piece in near]


def sum_rep(keep, got, *earlier):
    parts = [keep[k] + got[k].astype(f32) for k in range(4)]
    sent = [part.astype(bf16) for part in parts[1:]]
    if earlier:
        sent = [after(part, *earlier) for part in sent]
    return [parts[0]] + to_chips(sent)


def after(value, *others):
    return lax.optimization_barrier((value,) + others)[0]


def shards(
    block_in,
    cotangent,
    segments,
    qkv_weight,
    out_weight,
    up_weight,
    down_weight,
    vectors,
    first_qkv,
    first_out,
    first_up,
    first_down,
    first_vec,
    second_qkv,
    second_out,
    second_up,
    second_down,
    second_vec,
):
    tok_count = block_in.shape[0]
    rep = lax.axis_index("rep")
    shard = lax.axis_index("shard")
    seq_len = tok_count * N_SHARD
    rows = qkv_weight.shape[0]
    units = down_weight.shape[0]
    n_vec, cols = vectors.shape
    masks = np.array([0, 2, 4, 6, 1, 3, 5, 7], np.int32)
    spots = np.argsort(masks)
    device = np.arange(N_REP)
    places = spots[device[:, None] ^ device[None, :]].astype(np.int32)
    orders = (device[:, None] ^ masks[None, :]).astype(np.int32)
    near = shard ^ jnp.arange(N_SHARD, dtype=jnp.int32)
    table = jnp.asarray(np.concatenate([orders, places], axis=1))
    scalars = jnp.concatenate(
        [lax.dynamic_index_in_dim(table, rep, 0, keepdims=False), near, shard[None]]
    ).astype(jnp.int32)

    share = HEAD // rows
    pair = LANES // HEAD
    moves = []
    for at in range(N_REP * N_SHARD):
        head, part = at // share, at % share
        owner = (head // pair) % N_SHARD
        local = (head // (pair * N_SHARD)) * pair + head % pair
        moves.append((at, (local * share + part) * N_SHARD + owner))

    own_cols = [((rows, QKV + UP + LANES), bf16)] * N_SHARD
    square = pltpu.VMEM((LANES, LANES), f32)
    packed = single(
        pack_body, own_cols, scalars, [qkv_weight, up_weight, vectors], 1, "pack", [square]
    )
    got_cols = to_shards(packed[1:])
    out_rows = lax.ppermute(out_weight.astype(bf16), ("rep", "shard"), moves)
    down_own = down_weight.astype(bf16)
    (normed_own,) = single(
        norm_body,
        [((tok_count, D), bf16)],
        scalars,
        [block_in],
        1,
        "norm",
        [pltpu.VMEM((tok_count, D), f32)],
    )
    (in_rows,) = single(
        join_body,
        [((N_SHARD * rows, QKV + UP + OUT + LANES), bf16)],
        scalars,
        [packed[0], *got_cols[:2], after(got_cols[2], normed_own), out_rows],
        1,
        "join",
    )
    normed = [normed_own] + to_shards([after(normed_own, *got_cols)] * 3)
    pieces = gather_chips(in_rows)
    downs = gather_chips(after(down_own, *pieces[1:4]))
    downs[0] = down_own
    dy_all = lax.all_gather(cotangent.astype(bf16), "shard", axis=0, tiled=True)

    rope_parts = jnp.asarray(rope_lanes(seq_len)).reshape(N_SHARD, tok_count, 3 * LANES)
    rope = jnp.concatenate(
        [lax.dynamic_index_in_dim(rope_parts, near[k], 0, keepdims=False) for k in range(N_SHARD)]
    )
    seg_row = jnp.concatenate(
        [lax.dynamic_slice(segments[0], (near[k] * tok_count,), (tok_count,)) for k in range(N_SHARD)]
    )
    positions = (near[:, None] * tok_count + jnp.arange(tok_count)[None, :]).reshape(seq_len)
    allowed = (seg_row[:, None] == seg_row[None, :]) & (positions[None, :] <= positions[:, None])
    mask = jnp.where(allowed, 0.0, HIDDEN).astype(f32)

    out_whole, h_one, h_two, qkv16, act16, slope, vec_rel, last = front(
        scalars, normed, pieces, rope
    )
    block16 = ((tok_count, D), bf16)
    block32 = ((tok_count, D), f32)
    half = D // 2
    mixed16 = mix_heads(qkv16, mask)
    out_own, *out_sent = single(
        branch_body,
        [block32, block16, block16, block16],
        scalars,
        [mixed16, act16, out_whole, last, block_in, *downs],
        3,
        "branch",
    )
    out_got = to_shards_late(out_sent)

    dy_seq, d_mixed16, d_up16, up_sum = single(
        hidden_body,
        [((seq_len, D), bf16), ((seq_len, OUT), bf16), ((seq_len, UP), bf16), ((8, UP), f32)],
        scalars,
        [after(dy_all, out_own), *downs, slope, out_whole],
        1,
        "hidden",
    )

    mlp_keep, mlp_sent = single(
        mlp_body,
        [((half, D + UP), f32), ((half, D + UP), bf16)],
        scalars,
        [act16, dy_seq, h_two, d_up16],
        1,
        "mlp",
    )
    mlp_got = hop(mlp_sent.reshape(4, LANES, D + UP), "rep", N_REP, 1)
    mlp_parts = sum_rep(mlp_keep.reshape(4, LANES, D + UP), mlp_got)
    d_mixed16 = after(d_mixed16, mlp_got)
    d_qkv16, qkv_sum = attend_back(qkv16, d_mixed16, mixed16, mask, rope)
    d_qkv16 = after(d_qkv16, *out_got)
    h_one = after(h_one, *mlp_parts[1:])

    e_own, *e_sent, norm_sum = single(
        back_body,
        [block32, block16, block16, block16, ((8, D), f32)],
        scalars,
        [d_qkv16, d_up16, vec_rel, *normed, *pieces],
        1,
        "back",
    )
    e_got = to_shards_late(e_sent)
    cot_sum = jnp.sum(cotangent, axis=0, keepdims=True)
    wide = QKV + OUT + LANES
    qkv_keep, qkv_sent = single(
        terms_body,
        [((half, wide), f32), ((half, wide), bf16)],
        scalars,
        [h_one, d_qkv16, mixed16, dy_seq, norm_sum, qkv_sum, up_sum, cot_sum],
        4,
        "terms",
        [pltpu.VMEM((LANES, D), f32), pltpu.VMEM((OUT, D), f32)],
    )
    qkv_got = hop(qkv_sent.reshape(4, LANES, wide), "rep", N_REP, 1)
    qkv_parts = sum_rep(qkv_keep.reshape(4, LANES, wide), qkv_got, *mlp_parts[1:])
    narrow = (rows, QKV + UP + LANES)
    g_own, g1, g2, g3, out_sum = single(
        fold_body,
        [(narrow, f32), (narrow, bf16), (narrow, bf16), (narrow, bf16), ((rows, D), f32)],
        scalars,
        [*mlp_parts, *qkv_parts],
        1,
        "fold",
        [pltpu.VMEM((LANES, UP), f32), pltpu.VMEM((LANES, wide), f32)],
    )
    g_got = to_shards([g1, g2, g3])
    grad_out = lax.ppermute(out_sum, ("rep", "shard"), [(b, a) for a, b in moves])
    block_out = out_own + out_got[0].astype(f32) + out_got[1].astype(f32) + out_got[2].astype(f32)
    grad_down = sum(part[:, :D].astype(f32) for part in mlp_parts)
    (grad_input,) = single(
        finish_body,
        [block32],
        scalars,
        [e_own, *e_got, block_in, cotangent],
        2,
        "finish",
        [pltpu.VMEM((tok_count, D), f32)],
    )
    qkv_shape = (qkv_weight.shape, f32)
    up_shape = (up_weight.shape, f32)
    vec_shape = (vectors.shape, f32)
    (
        grad_qkv,
        new_qkv,
        new_first_qkv,
        new_second_qkv,
        grad_up,
        new_up,
        new_first_up,
        new_second_up,
        grad_vec,
        new_vec,
        new_first_vec,
        new_second_vec,
    ) = single(
        adam_body,
        [qkv_shape] * 4 + [up_shape] * 4 + [vec_shape] * 4,
        scalars,
        [
            g_own,
            *g_got,
            qkv_weight,
            first_qkv,
            second_qkv,
            up_weight,
            first_up,
            second_up,
            vectors,
            first_vec,
            second_vec,
        ],
        3,
        "adam",
        [pltpu.VMEM((N_SHARD,) + narrow, f32), square],
    )

    new_out, new_first_out, new_second_out = adam_update(
        out_weight, grad_out, first_out, second_out, LR_MATRIX, WEIGHT_DECAY
    )
    new_down, new_first_down, new_second_down = adam_update(
        down_weight, grad_down, first_down, second_down, LR_MATRIX, WEIGHT_DECAY
    )
    return (
        block_out,
        grad_input,
        grad_qkv,
        grad_out,
        grad_up,
        grad_down,
        grad_vec,
        new_qkv,
        new_out,
        new_up,
        new_down,
        new_vec,
        new_first_qkv,
        new_first_out,
        new_first_up,
        new_first_down,
        new_first_vec,
        new_second_qkv,
        new_second_out,
        new_second_up,
        new_second_down,
        new_second_vec,
    )


def solution(mesh):
    aligned = mesh.shape["rep"] == N_REP and mesh.shape["shard"] == N_SHARD
    return jax.shard_map(
        shards if aligned else general,
        mesh=mesh,
        in_specs=(
            P(("rep", "shard"), None),
            P(("rep", "shard"), None),
            P("rep", None),
            P(("rep", "shard"), None),
            P(("rep", "shard"), None),
            P(("rep", "shard"), None),
            P(("rep", "shard"), None),
            P(None, ("rep", "shard")),
            P(("rep", "shard"), None),
            P(("rep", "shard"), None),
            P(("rep", "shard"), None),
            P(("rep", "shard"), None),
            P(None, ("rep", "shard")),
            P(("rep", "shard"), None),
            P(("rep", "shard"), None),
            P(("rep", "shard"), None),
            P(("rep", "shard"), None),
            P(None, ("rep", "shard")),
        ),
        out_specs=(
            P(("rep", "shard"), None),
            P(("rep", "shard"), None),
            P(("rep", "shard"), None),
            P(("rep", "shard"), None),
            P(("rep", "shard"), None),
            P(("rep", "shard"), None),
            P(None, ("rep", "shard")),
            P(("rep", "shard"), None),
            P(("rep", "shard"), None),
            P(("rep", "shard"), None),
            P(("rep", "shard"), None),
            P(None, ("rep", "shard")),
            P(("rep", "shard"), None),
            P(("rep", "shard"), None),
            P(("rep", "shard"), None),
            P(("rep", "shard"), None),
            P(None, ("rep", "shard")),
            P(("rep", "shard"), None),
            P(("rep", "shard"), None),
            P(("rep", "shard"), None),
            P(("rep", "shard"), None),
            P(None, ("rep", "shard")),
        ),
        check_vma=False,
    )
```

```python
import jax
import jax.numpy as jnp
import numpy as np
from jax import lax
from jax.experimental import pallas as pl
from jax.experimental.pallas import tpu as pltpu
from jax.sharding import PartitionSpec as P

D = 1024
HEADS = 16
HEAD = D // HEADS
FF = 4096
ROT = 16
STEP = 10
LANES = 128


LN_EPS = 1e-05
BETA_ONE = 0.9
BETA_TWO = 0.95
ADAM_EPS = 1e-08
LR_MATRIX = 0.03
LR_VECTOR = 0.2
WEIGHT_DECAY = 0.01
ROPE_BASE = 10000.0
INV_ROOT_TWO = 0.7071067811865476
INV_ROOT_TAU = 0.3989422804014327
HIDDEN = -1e30
bf16 = jnp.bfloat16
f32 = jnp.float32
TILE = 256


def adam_update(param, grad, first, second, rate, decay):
    first_new = BETA_ONE * first + (1.0 - BETA_ONE) * grad
    second_new = BETA_TWO * second + (1.0 - BETA_TWO) * grad * grad
    first_hat = first_new / (1.0 - BETA_ONE**STEP)
    second_hat = second_new / (1.0 - BETA_TWO**STEP)
    return (
        param - rate * (first_hat / (jnp.sqrt(second_hat) + ADAM_EPS) + decay * param),
        first_new,
        second_new,
    )


def contract_rows(left, right):
    return lax.dot_general(left, right, (((0,), (0,)), ((), ())), preferred_element_type=f32)


def contract_cols(left, right):
    return lax.dot_general(left, right, (((1,), (1,)), ((), ())), preferred_element_type=f32)


def plain_dot(left, right):
    return jnp.dot(left, right, preferred_element_type=f32)


def rope_lanes(seq_len):
    half = ROT // 2
    freqs = (ROPE_BASE ** (-(2.0 * np.arange(half, dtype=np.float32) / ROT))).astype(np.float32)
    angles = np.arange(seq_len, dtype=np.float32)[:, None] * freqs[None, :]
    cosines, sines = np.cos(angles), np.sin(angles)
    keep = np.ones((seq_len, HEAD), np.float32)
    up = np.zeros((seq_len, HEAD), np.float32)
    down = np.zeros((seq_len, HEAD), np.float32)
    keep[:, :half], keep[:, half:ROT] = cosines, cosines
    up[:, :half] = -sines
    down[:, half:ROT] = sines
    reps = LANES // HEAD
    return np.concatenate([np.tile(t, (1, reps)) for t in (keep, up, down)], axis=1)


def turn(values, table, sign):
    half = ROT // 2
    above = pltpu.roll(values, LANES - half, 1)
    below = pltpu.roll(values, half, 1)
    moved = above * table[:, LANES : 2 * LANES] + below * table[:, 2 * LANES :]
    return values * table[:, :LANES] + sign * moved


def params(mib):
    return pltpu.CompilerParams(vmem_limit_bytes=mib << 20)


def cost(micros):
    return pl.CostEstimate(flops=int(micros * 1.15e9), bytes_accessed=1 << 20, transcendentals=0)


def whole_spec(shape):
    return pl.BlockSpec(shape, lambda *_: (0,) * len(shape))


def rope_tables(positions):
    half_rot = ROT // 2
    freqs = ROPE_BASE ** (-(2.0 * jnp.arange(half_rot).astype(jnp.float32) / ROT))
    angles = positions.astype(jnp.float32)[:, None] * freqs[None, :]
    return (jnp.cos(angles)[:, None, :], jnp.sin(angles)[:, None, :])


def rotate(heads, cosines, sines):
    half_rot = ROT // 2
    lower = heads[..., :half_rot]
    upper = heads[..., half_rot:ROT]
    return jnp.concatenate(
        [lower * cosines - upper * sines, upper * cosines + lower * sines, heads[..., ROT:]],
        axis=-1,
    )


def unrotate(heads, cosines, sines):
    half_rot = ROT // 2
    lower = heads[..., :half_rot]
    upper = heads[..., half_rot:ROT]
    return jnp.concatenate(
        [lower * cosines + upper * sines, upper * cosines - lower * sines, heads[..., ROT:]],
        axis=-1,
    )


def gelu_value(inner):
    return 0.5 * inner * (1.0 + jax.scipy.special.erf(inner * INV_ROOT_TWO))


def gelu_slope(inner):
    return (
        0.5 * (1.0 + jax.scipy.special.erf(inner * INV_ROOT_TWO))
        + inner * jnp.exp(-0.5 * inner * inner) * INV_ROOT_TAU
    )


def hop(value, axis, size, mask):
    return lax.ppermute(value, axis, [(i, i ^ mask) for i in range(size)])


def pick(blocks, index, axis=0):
    return lax.dynamic_index_in_dim(blocks, index, axis, keepdims=False)


def stages(size):
    bits = size.bit_length() - 1
    found = []
    while bits > 0:
        take = 2 if bits >= 2 else 1
        bits -= take
        found.append((bits, 1 << take))
    return found


def gather_axis(own, axis, me, size):
    if size > 16:
        return lax.all_gather(own, axis)
    pieces = {0: own}
    for shift, count in stages(size):
        more = dict(pieces)
        for k in range(1, count):
            for mask, piece in pieces.items():
                more[mask ^ (k << shift)] = hop(piece, axis, size, k << shift)
        pieces = more
    whole = jnp.zeros((size,) + own.shape, own.dtype)
    for mask in range(size):
        whole = lax.dynamic_update_index_in_dim(whole, pieces[mask], me ^ mask, 0)
    return whole


def exchange_axis(blocks, axis, me, size, wire):
    got = [(0, pick(blocks, me))]
    for mask in range(1, size):
        got.append((mask, hop(pick(blocks, me ^ mask).astype(wire), axis, size, mask)))
    return got


def reduce_axis(blocks, axis, me, size, wire):
    current = blocks
    for shift, count in reversed(stages(size)):
        left = current.shape[0] // count
        view = current.reshape((left, count) + current.shape[1:])
        digit = (me >> shift) & (count - 1)
        total = pick(view, digit, 1)
        for k in range(1, count):
            sent = pick(view, digit ^ k, 1).astype(wire)
            total = total + hop(sent, axis, size, k << shift).astype(jnp.float32)
        current = total
    return current[0]


def general(
    block_in,
    cotangent,
    segments,
    qkv_weight,
    out_weight,
    up_weight,
    down_weight,
    vectors,
    first_qkv,
    first_out,
    first_up,
    first_down,
    first_vec,
    second_qkv,
    second_out,
    second_up,
    second_down,
    second_vec,
):
    tok_count = block_in.shape[0]
    n_rep = lax.axis_size("rep")
    n_shard = lax.axis_size("shard")
    rep = lax.axis_index("rep")
    shard = lax.axis_index("shard")
    seq_len = tok_count * n_shard
    head_dim = D // HEADS
    own_heads = HEADS // n_shard
    own_feats = own_heads * head_dim
    rows = qkv_weight.shape[0]
    units = down_weight.shape[0]
    own_units = units * n_rep
    cols = vectors.shape[1]
    score_scale = head_dim ** (-0.5)

    qkv_cols = qkv_weight.astype(bf16).reshape(rows, 3, own_heads, n_shard, head_dim)
    qkv_cols = qkv_cols.transpose(3, 0, 1, 2, 4).reshape(n_shard, rows, 3 * own_feats)
    up_cols = up_weight.astype(bf16).reshape(rows, n_rep, n_shard, units)
    up_cols = up_cols.transpose(2, 0, 1, 3).reshape(n_shard, rows, own_units)
    in_cols = jnp.concatenate([qkv_cols, up_cols], axis=2)
    in_rows = jnp.zeros_like(in_cols)
    for mask, piece in exchange_axis(in_cols, "shard", shard, n_shard, bf16):
        in_rows = lax.dynamic_update_index_in_dim(in_rows, piece, shard ^ mask, 0)
    in_rows = in_rows.reshape(n_shard * rows, 3 * own_feats + own_units)

    center = block_in - jnp.mean(block_in, axis=-1, keepdims=True)
    inv_std = lax.rsqrt(jnp.mean(center * center, axis=-1, keepdims=True) + LN_EPS)
    normed = center * inv_std
    normed_seq = gather_axis(normed.astype(bf16), "shard", shard, n_shard).reshape(seq_len, D)
    normed_seq = normed_seq.astype(f32)

    vec_some = gather_axis(vectors, "shard", shard, n_shard)
    vec_all = gather_axis(vec_some, "rep", rep, n_rep)
    vec_all = vec_all.transpose(2, 0, 1, 3).reshape(vectors.shape[0], D)

    in_whole = gather_axis(in_rows, "rep", rep, n_rep).reshape(D, 3 * own_feats + own_units)
    upstream16 = gather_axis(cotangent.astype(bf16), "shard", shard, n_shard).reshape(seq_len, D)
    down_whole = gather_axis(down_weight.astype(bf16), "rep", rep, n_rep).reshape(own_units, D)
    share = head_dim // rows
    moves = []
    for device in range(n_rep * n_shard):
        head, part = device // share, device % share
        moves.append((device, ((head // n_shard) * share + part) * n_shard + head % n_shard))
    out_rows = lax.ppermute(out_weight.astype(bf16), ("rep", "shard"), moves)
    out_whole = gather_axis(out_rows, "rep", rep, n_rep).reshape(own_feats, D)

    per_row = FF // D
    gain_one, shift_one, gain_two, shift_two = (vec_all[0], vec_all[1], vec_all[2], vec_all[3])
    qkv_bias = pick(vec_all[4:7].reshape(3, own_heads, n_shard, head_dim), shard, 2).reshape(
        3 * own_feats
    )
    up_bias = pick(vec_all[8 : 8 + per_row].reshape(n_rep, n_shard, units), shard, 1).reshape(
        own_units
    )
    out_bias = vec_all[7]
    down_bias = vec_all[8 + per_row]

    h_one = (normed_seq * gain_one + shift_one).astype(bf16)
    h_two = (normed_seq * gain_two + shift_two).astype(bf16)
    qkv_whole = in_whole[:, : 3 * own_feats]
    up_whole = in_whole[:, 3 * own_feats :]
    qkv_lin = jnp.dot(h_one, qkv_whole, preferred_element_type=f32) + qkv_bias
    up_lin = jnp.dot(h_two, up_whole, preferred_element_type=f32) + up_bias

    positions = jnp.arange(seq_len)
    cosines, sines = rope_tables(positions)

    def heads_of(values):
        return values.reshape(seq_len, own_heads, head_dim)

    query16 = rotate(heads_of(qkv_lin[:, :own_feats]), cosines, sines).astype(bf16)
    key16 = rotate(heads_of(qkv_lin[:, own_feats : 2 * own_feats]), cosines, sines).astype(bf16)
    value16 = heads_of(qkv_lin[:, 2 * own_feats :]).astype(bf16)
    seg_row = segments[0]
    allowed = (seg_row[:, None] == seg_row[None, :]) & (positions[None, :] <= positions[:, None])
    scores = jnp.where(
        allowed[None],
        jnp.einsum("qhd,khd->hqk", query16, key16, preferred_element_type=f32) * score_scale,
        -jnp.inf,
    )
    row_max = jnp.max(scores, axis=-1, keepdims=True)
    expo = jnp.exp(scores - row_max)
    row_sum = jnp.sum(expo, axis=-1, keepdims=True)
    log_total = row_max + jnp.log(row_sum)
    probs16 = (expo / row_sum).astype(bf16)
    mixed16 = (
        jnp.einsum("hqk,khd->qhd", probs16, value16, preferred_element_type=f32)
        .reshape(seq_len, own_feats)
        .astype(bf16)
    )
    act16 = gelu_value(up_lin).astype(bf16)
    branches = jnp.dot(mixed16, out_whole, preferred_element_type=f32)
    branches = branches + jnp.dot(act16, down_whole, preferred_element_type=f32)
    branches = reduce_axis(
        branches.reshape(n_shard, tok_count, D), "shard", shard, n_shard, bf16
    )
    block_out = block_in + branches + out_bias + down_bias

    term_down = contract_rows(act16, upstream16)
    sum_down = reduce_axis(term_down.reshape(n_rep, units, D), "rep", rep, n_rep, bf16)
    term_out = contract_rows(mixed16, upstream16)
    sum_out = reduce_axis(term_out.reshape(n_rep, rows, D), "rep", rep, n_rep, bf16)
    grad_out = lax.ppermute(sum_out, ("rep", "shard"), [(b, a) for a, b in moves])
    grad_down = sum_down
    d_act = contract_cols(upstream16, down_whole)
    d_mixed16 = heads_of(contract_cols(upstream16, out_whole)).astype(bf16)
    d_up = d_act * gelu_slope(up_lin)
    d_up16 = d_up.astype(bf16)
    term_up = contract_rows(h_two, d_up16)
    sum_up = reduce_axis(
        term_up.reshape(n_rep, n_shard * rows, own_units), "rep", rep, n_rep, bf16
    )

    def back_rows(sums, width):
        whole = jnp.zeros((n_shard, rows, width), f32)
        blocks = sums.reshape(n_shard, rows, width)
        for mask, piece in exchange_axis(blocks, "shard", shard, n_shard, bf16):
            whole = lax.dynamic_update_index_in_dim(whole, piece.astype(f32), shard ^ mask, 0)
        return whole

    grad_up = back_rows(sum_up, own_units).reshape(n_shard, rows, n_rep, units)
    grad_up = grad_up.transpose(1, 2, 0, 3).reshape(rows, FF)

    row_delta = jnp.sum(
        d_mixed16.astype(f32) * heads_of(mixed16).astype(f32),
        axis=-1,
    ).T[:, :, None]
    probs_again = jnp.exp(scores - log_total)
    d_probs = jnp.einsum("qhd,khd->hqk", d_mixed16, value16, preferred_element_type=f32)
    d_scores16 = (probs_again * (d_probs - row_delta) * score_scale).astype(bf16)
    probs_back16 = probs_again.astype(bf16)
    d_query = jnp.einsum("hqk,khd->qhd", d_scores16, key16, preferred_element_type=f32)
    d_keys = jnp.einsum("hqk,qhd->khd", d_scores16, query16, preferred_element_type=f32)
    d_values = jnp.einsum("hqk,qhd->khd", probs_back16, d_mixed16, preferred_element_type=f32)
    d_qkv = jnp.concatenate(
        [
            unrotate(d_query, cosines, sines).reshape(seq_len, own_feats),
            unrotate(d_keys, cosines, sines).reshape(seq_len, own_feats),
            d_values.reshape(seq_len, own_feats),
        ],
        axis=1,
    )
    d_qkv16 = d_qkv.astype(bf16)
    term_qkv = contract_rows(h_one, d_qkv16)
    sum_qkv = reduce_axis(
        term_qkv.reshape(n_rep, n_shard * rows, 3 * own_feats), "rep", rep, n_rep, bf16
    )
    grad_qkv = back_rows(sum_qkv, 3 * own_feats)
    grad_qkv = grad_qkv.reshape(n_shard, rows, 3, own_heads, head_dim)
    grad_qkv = grad_qkv.transpose(1, 2, 3, 0, 4).reshape(rows, 3 * D)

    d_one = contract_cols(d_qkv16, qkv_whole)
    d_two = contract_cols(d_up16, up_whole)
    scaled = d_one * gain_one + d_two * gain_two
    scaled = reduce_axis(scaled.reshape(n_shard, tok_count, D), "shard", shard, n_shard, bf16)
    grad_input = cotangent + inv_std * (
        scaled
        - jnp.mean(scaled, axis=-1, keepdims=True)
        - normed * jnp.mean(scaled * normed, axis=-1, keepdims=True)
    )

    mine = jnp.arange(n_shard) == shard
    cot_sum = jnp.sum(cotangent, axis=0)
    bias_qkv = jnp.where(
        mine[None, None, :, None],
        jnp.sum(d_qkv, axis=0).reshape(3, own_heads, 1, head_dim),
        0.0,
    ).reshape(3, D)
    bias_up = jnp.where(
        mine[None, :, None], jnp.sum(d_up, axis=0).reshape(n_rep, 1, units), 0.0
    ).reshape(per_row, D)
    vec_terms = jnp.concatenate(
        [
            jnp.sum(d_one * normed_seq, axis=0)[None],
            jnp.sum(d_one, axis=0)[None],
            jnp.sum(d_two * normed_seq, axis=0)[None],
            jnp.sum(d_two, axis=0)[None],
            bias_qkv,
            cot_sum[None],
            bias_up,
            cot_sum[None],
        ],
        axis=0,
    )
    vec_blocks = vec_terms.reshape(vectors.shape[0], n_rep, n_shard, cols).transpose(1, 2, 0, 3)
    grad_vec = reduce_axis(
        reduce_axis(vec_blocks, "rep", rep, n_rep, f32), "shard", shard, n_shard, f32
    )

    new_qkv, new_first_qkv, new_second_qkv = adam_update(
        qkv_weight, grad_qkv, first_qkv, second_qkv, LR_MATRIX, WEIGHT_DECAY
    )
    new_out, new_first_out, new_second_out = adam_update(
        out_weight, grad_out, first_out, second_out, LR_MATRIX, WEIGHT_DECAY
    )
    new_up, new_first_up, new_second_up = adam_update(
        up_weight, grad_up, first_up, second_up, LR_MATRIX, WEIGHT_DECAY
    )
    new_down, new_first_down, new_second_down = adam_update(
        down_weight, grad_down, first_down, second_down, LR_MATRIX, WEIGHT_DECAY
    )
    new_vec, new_first_vec, new_second_vec = adam_update(
        vectors, grad_vec, first_vec, second_vec, LR_VECTOR, 0.0
    )
    return (
        block_out,
        grad_input,
        grad_qkv,
        grad_out,
        grad_up,
        grad_down,
        grad_vec,
        new_qkv,
        new_out,
        new_up,
        new_down,
        new_vec,
        new_first_qkv,
        new_first_out,
        new_first_up,
        new_first_down,
        new_first_vec,
        new_second_qkv,
        new_second_out,
        new_second_up,
        new_second_down,
        new_second_vec,
    )


ROOM = {
    "pack": 6,
    "norm": 4,
    "join": 4,
    "middle": 30,
    "back": 28,
    "terms": 20,
    "mlp": 28,
    "fold": 16,
    "finish": 10,
    "adam": 22,
}


def single(body, outs, prefetch, ins, micros, name, scratch=()):
    shapes = tuple(jax.ShapeDtypeStruct(s, d) for s, d in outs)
    return pl.pallas_call(
        body,
        out_shape=shapes,
        grid_spec=pltpu.PrefetchScalarGridSpec(
            num_scalar_prefetch=1,
            grid=(1,),
            in_specs=[whole_spec(a.shape) for a in ins],
            out_specs=tuple(whole_spec(s.shape) for s in shapes),
            scratch_shapes=list(scratch),
        ),
        compiler_params=params(ROOM[name]),
        cost_estimate=cost(micros),
        name=name,
    )(prefetch, *ins)


def lane_block(index):
    return pl.ds(pl.multiple_of(index * LANES, LANES), LANES)


def row_block(index, size):
    return pl.ds(pl.multiple_of(index * size, size), size)


N_REP = 8
N_SHARD = 4
ORDER = 0
PLACE = N_REP
NEAR = 2 * N_REP
SHARD = NEAR + N_SHARD
QKV = 3 * TILE
UP = D
OUT = TILE


def pack_body(s_ref, qkv_ref, up_ref, vec_ref, *refs):
    outs, turn_ref = refs[:-1], refs[-1]
    count, cols = vec_ref.shape
    turn_ref[...] = jnp.zeros_like(turn_ref)
    vec = vec_ref[...]
    for i in range(3):
        part = vec.astype(bf16).astype(f32)
        turn_ref[16 * i : 16 * i + count, :cols] = part
        vec = vec - part
    vec16 = turn_ref[...].T[:cols, :].astype(bf16)
    for k in range(N_SHARD):
        t = s_ref[NEAR + k]
        o_ref = outs[k]
        for c in range(QKV // LANES):
            o_ref[:, c * LANES : (c + 1) * LANES] = qkv_ref[:, lane_block(c * N_SHARD + t)].astype(bf16)
        for c in range(UP // LANES):
            at = QKV + c * LANES
            o_ref[:, at : at + LANES] = up_ref[:, lane_block(c * N_SHARD + t)].astype(bf16)
        o_ref[:, QKV + UP :] = vec16


def norm_body(s_ref, x_ref, o_ref, n_ref):
    x = x_ref[...]
    center = x - jnp.mean(x, axis=-1, keepdims=True)
    inv_std = lax.rsqrt(jnp.mean(center * center, axis=-1, keepdims=True) + LN_EPS)
    n_ref[...] = center * inv_std
    for i in range(N_REP):
        o_ref[:, i * LANES : (i + 1) * LANES] = n_ref[:, lane_block(s_ref[ORDER + i])].astype(bf16)


def join_body(s_ref, *refs):
    out_ref, o_ref = refs[N_SHARD], refs[N_SHARD + 1]
    rows = out_ref.shape[0]
    for k in range(N_SHARD):
        at = row_block(s_ref[NEAR + k], rows)
        o_ref[at, : QKV + UP] = refs[k][:, : QKV + UP]
        o_ref[at, QKV + UP + OUT :] = refs[k][:, QKV + UP :]
    for c in range(D // OUT):
        o_ref[c * rows : (c + 1) * rows, QKV + UP : QKV + UP + OUT] = out_ref[:, c * OUT : (c + 1) * OUT]


def bias_places(s_ref):
    shard = s_ref[SHARD]
    found = []
    for c in range(QKV // LANES):
        found.append((4 + c // 2, s_ref[PLACE + (c % 2) * N_SHARD + shard], c * LANES))
    for c in range(UP // LANES):
        found.append((8 + c // 2, s_ref[PLACE + (c % 2) * N_SHARD + shard], QKV + c * LANES))
    return found


def front_body(s_ref, *refs):
    n_refs, refs = refs[:N_SHARD], refs[N_SHARD:]
    w_refs, refs = refs[:N_REP], refs[N_REP:]
    v_refs, refs = refs[:N_REP], refs[N_REP:]
    out_refs, refs = refs[:N_REP], refs[N_REP:]
    rope_ref, whole_ref, h1_ref, h2_ref, qkv_ref, act_ref, slope_ref, vec_ref, last_ref, bias_ref = refs
    j = pl.program_id(0)
    rows = n_refs[0].shape[0]

    @pl.when(j == 0)
    def _():
        for i in range(N_REP):
            parts = v_refs[i][...].astype(f32).T
            vec_ref[:, i * LANES : (i + 1) * LANES] = (parts[0:16] + parts[16:32]) + parts[32:48]
        for k in range(N_SHARD):
            normed = n_refs[k][...].astype(f32)
            at = slice(k * rows, (k + 1) * rows)
            h1_ref[at, :] = (normed * vec_ref[0:1, :] + vec_ref[1:2, :]).astype(bf16)
            h2_ref[at, :] = (normed * vec_ref[2:3, :] + vec_ref[3:4, :]).astype(bf16)
        for row, block, at in bias_places(s_ref):
            bias_ref[at // TILE, 0:1, at % TILE : at % TILE + LANES] = vec_ref[row : row + 1, lane_block(block)]
        both = vec_ref[7:8, :] + vec_ref[12:13, :]
        for i in range(N_REP):
            last_ref[0:1, lane_block(s_ref[ORDER + i])] = both[:, i * LANES : (i + 1) * LANES]
        chunks = D // OUT
        size = out_refs[0].shape[0] // chunks
        for i in range(N_REP):
            at = row_block(s_ref[ORDER + i], size)
            for c in range(chunks):
                whole_ref[at, c * OUT : (c + 1) * OUT] = out_refs[i][c * size : (c + 1) * size, :]

    def product(h_ref):
        total = bias_ref[j, 0:1, :]
        for i in range(0, N_REP, 2):
            weights = jnp.concatenate([w_refs[i][...], w_refs[i + 1][...]], axis=0)
            total = total + plain_dot(h_ref[:, i * LANES : (i + 2) * LANES], weights)
        return total

    @pl.when(j < 2)
    def _():
        lin = product(h1_ref)
        for c in range(0, TILE, LANES):
            qkv_ref[:, c : c + LANES] = turn(lin[:, c : c + LANES], rope_ref[...], 1.0).astype(bf16)

    @pl.when(j == 2)
    def _():
        qkv_ref[...] = product(h1_ref).astype(bf16)

    @pl.when(j > 2)
    def _():
        lin = product(h2_ref)
        above = 0.5 * (1.0 + lax.erf(lin * INV_ROOT_TWO))
        act = (lin * above).astype(bf16)
        slope = above + lin * jnp.exp(-0.5 * lin * lin) * INV_ROOT_TAU
        for c in range(2):
            at = lane_block(s_ref[PLACE + (j - 3) * 2 + c])
            act_ref[:, at] = act[:, c * LANES : (c + 1) * LANES]
            slope_ref[:, at] = slope[:, c * LANES : (c + 1) * LANES]


def front(scalars, normed, pieces, rope):
    tokens = rope.shape[0]
    block = pieces[0].shape[0]
    shapes = (
        ((OUT, D), bf16),
        ((tokens, D), bf16),
        ((tokens, D), bf16),
        ((tokens, QKV), bf16),
        ((tokens, UP), bf16),
        ((tokens, UP), f32),
        ((16, D), f32),
        ((8, D), f32),
    )
    specs = [whole_spec(s) for s, _ in shapes]
    specs[3] = pl.BlockSpec((tokens, TILE), lambda j, s: (0, jnp.minimum(j, 2)))
    return pl.pallas_call(
        front_body,
        out_shape=tuple(jax.ShapeDtypeStruct(s, d) for s, d in shapes),
        grid_spec=pltpu.PrefetchScalarGridSpec(
            num_scalar_prefetch=1,
            grid=((QKV + UP) // TILE,),
            in_specs=[whole_spec(n.shape) for n in normed]
            + [pl.BlockSpec((block, TILE), lambda j, s: (0, j))] * N_REP
            + [pl.BlockSpec((block, LANES), lambda j, s: (0, (QKV + UP + OUT) // LANES))] * N_REP
            + [pl.BlockSpec((block, OUT), lambda j, s: (0, (QKV + UP) // OUT))] * N_REP
            + [whole_spec(rope.shape)],
            out_specs=tuple(specs),
            scratch_shapes=[pltpu.VMEM(((QKV + UP) // TILE, 8, TILE), f32)],
        ),
        compiler_params=params(24),
        cost_estimate=cost(9),
        name="front",
    )(scalars, *normed, *pieces, *pieces, *pieces, rope)


def hidden_body(s_ref, *refs):
    dy_ref, refs = refs[0], refs[1:]
    down_refs, refs = refs[:N_REP], refs[N_REP:]
    slope_ref, whole_ref, seq_ref, dmix_ref, du_ref, sum_ref = refs
    tokens = dy_ref.shape[0] // N_SHARD
    for k in range(N_SHARD):
        seq_ref[k * tokens : (k + 1) * tokens, :] = dy_ref[row_block(s_ref[NEAR + k], tokens), :]
    dy = seq_ref[...]
    dmix_ref[...] = contract_cols(dy, whole_ref[...]).astype(bf16)
    for i in range(N_REP):
        du = contract_cols(dy, down_refs[i][...]) * slope_ref[:, i * LANES : (i + 1) * LANES]
        at = lane_block(s_ref[ORDER + i])
        du_ref[:, at] = du.astype(bf16)
        sum_ref[0:1, at] = jnp.sum(du, axis=0, keepdims=True)


def weigh(q, k, mask):
    score = contract_cols(q, k) * (HEAD ** (-0.5)) + mask
    expo = jnp.exp(score - jnp.max(score, axis=-1, keepdims=True))
    return expo * (1.0 / jnp.sum(expo, axis=-1, keepdims=True))


def only(values, mine):
    return jnp.where(mine, values, jnp.zeros_like(values))


def mix_body(q_ref, k_ref, v_ref, mask_ref, mix_ref):
    first = lax.broadcasted_iota(jnp.int32, (LANES, LANES), 1) < HEAD
    k = k_ref[...]
    v = v_ref[...]
    for c in range(0, q_ref.shape[0], LANES):
        rows = slice(c, c + LANES)
        q = q_ref[rows, :]
        mixes = []
        for mine in (first, jnp.logical_not(first)):
            prob = weigh(only(q, mine), k, mask_ref[rows, :])
            mixes.append(plain_dot(prob.astype(bf16), v))
        mix_ref[rows, :] = jnp.where(first, mixes[0], mixes[1]).astype(bf16)


def attend_body(
    q_ref, k_ref, v_ref, dm_ref, mix_ref, mask_ref, rope_ref, dqkv_ref, sum_ref, dk_ref, dv_ref
):
    pair = pl.program_id(0)
    tokens = q_ref.shape[0]
    scale = HEAD ** (-0.5)
    first = lax.broadcasted_iota(jnp.int32, (LANES, LANES), 1) < HEAD
    every = lax.broadcasted_iota(jnp.int32, (tokens, LANES), 1) < HEAD
    k = k_ref[...]
    v = v_ref[...]
    pairs = pl.num_programs(0)

    def columns(part):
        return lane_block(part * pairs + pair)

    dq_total = jnp.zeros((1, LANES), f32)
    for c in range(0, tokens, LANES):
        rows = slice(c, c + LANES)
        q = q_ref[rows, :]
        dm = dm_ref[rows, :]
        mix = mix_ref[rows, :].astype(f32)
        dqs, dks, dvs = [], [], []
        for mine in (first, jnp.logical_not(first)):
            dmh = only(dm, mine)
            prob = weigh(only(q, mine), k, mask_ref[rows, :])
            delta = jnp.sum(dmh.astype(f32) * mix, axis=-1, keepdims=True)
            d_prob = contract_cols(dmh, v)
            ds16 = (prob * (d_prob - delta) * scale).astype(bf16)
            dqs.append(plain_dot(ds16, k))
            dks.append(contract_rows(ds16, q))
            dvs.append(contract_rows(prob.astype(bf16), dm))
        dq = turn(jnp.where(first, dqs[0], dqs[1]), rope_ref[rows, :], -1.0)
        dqkv_ref[rows, columns(0)] = dq.astype(bf16)
        dq_total = dq_total + jnp.sum(dq, axis=0, keepdims=True)
        dk = jnp.where(every, dks[0], dks[1])
        dv = jnp.where(every, dvs[0], dvs[1])
        if c == 0:
            dk_ref[...] = dk
            dv_ref[...] = dv
        else:
            dk_ref[...] += dk
            dv_ref[...] += dv
    dk = turn(dk_ref[...], rope_ref[...], -1.0)
    dv = dv_ref[...]
    dqkv_ref[:, columns(1)] = dk.astype(bf16)
    dqkv_ref[:, columns(2)] = dv.astype(bf16)
    sum_ref[:, columns(0)] = dq_total
    sum_ref[:, columns(1)] = jnp.sum(dk, axis=0, keepdims=True)
    sum_ref[:, columns(2)] = jnp.sum(dv, axis=0, keepdims=True)


def pair_spec(tokens, first):
    return pl.BlockSpec((tokens, LANES), lambda j: (0, first + j))


def mix_heads(qkv, mask):
    tokens = qkv.shape[0]
    pairs = OUT // LANES
    return pl.pallas_call(
        mix_body,
        out_shape=jax.ShapeDtypeStruct((tokens, OUT), bf16),
        grid=(pairs,),
        in_specs=[pair_spec(tokens, i * pairs) for i in range(3)] + [whole_spec(mask.shape)],
        out_specs=pair_spec(tokens, 0),
        compiler_params=params(10),
        cost_estimate=cost(6),
        name="mix_heads",
    )(qkv, qkv, qkv, mask)


def attend_back(qkv, d_mix, mixed, mask, rope):
    tokens = qkv.shape[0]
    pairs = OUT // LANES
    return pl.pallas_call(
        attend_body,
        out_shape=(
            jax.ShapeDtypeStruct((tokens, QKV), bf16),
            jax.ShapeDtypeStruct((1, QKV), f32),
        ),
        grid=(pairs,),
        in_specs=[pair_spec(tokens, i * pairs) for i in range(3)]
        + [pair_spec(tokens, 0), pair_spec(tokens, 0), whole_spec(mask.shape), whole_spec(rope.shape)],
        out_specs=(whole_spec((tokens, QKV)), whole_spec((1, QKV))),
        scratch_shapes=[pltpu.VMEM((tokens, LANES), f32), pltpu.VMEM((tokens, LANES), f32)],
        compiler_params=params(12),
        cost_estimate=cost(4),
        name="attend_back",
    )(qkv, qkv, qkv, d_mix, mixed, mask, rope)


def back_body(s_ref, dqkv_ref, du_ref, vec_ref, *refs):
    n_refs, refs = refs[:N_SHARD], refs[N_SHARD:]
    w_refs, refs = refs[:N_REP], refs[N_REP:]
    own_ref, sent_refs, sum_ref = refs[0], refs[1:N_SHARD], refs[N_SHARD]
    rows = n_refs[0].shape[0]
    for i in range(0, N_REP, 2):
        cols = slice(i * LANES, (i + 2) * LANES)
        weights = jnp.concatenate([w_refs[i][:, : QKV + UP], w_refs[i + 1][:, : QKV + UP]], axis=0)
        d_one = contract_cols(dqkv_ref[...], weights[:, :QKV])
        d_two = contract_cols(du_ref[...], weights[:, QKV:])
        scaled = d_one * vec_ref[0:1, cols] + d_two * vec_ref[2:3, cols]
        own_ref[:, cols] = scaled[:rows]
        sums = [jnp.sum(d, axis=0, keepdims=True) for d in (d_one, d_two)]
        turned = [jnp.zeros_like(sums[0])] * 2
        for k in range(N_SHARD):
            at = slice(k * rows, (k + 1) * rows)
            if k:
                sent_refs[k - 1][:, cols] = scaled[at].astype(bf16)
            normed = n_refs[k][:, cols].astype(f32)
            turned = [
                t + jnp.sum(d[at] * normed, axis=0, keepdims=True)
                for t, d in zip(turned, (d_one, d_two))
            ]
        sum_ref[0:1, cols] = turned[0]
        sum_ref[1:2, cols] = sums[0]
        sum_ref[2:3, cols] = turned[1]
        sum_ref[3:4, cols] = sums[1]


def middle_body(s_ref, mix_ref, act_ref, whole_ref, last_ref, x_ref, dy_ref, slope_ref, *refs):
    down_refs, refs = refs[:N_REP], refs[N_REP:]
    own_ref, sent_refs = refs[0], refs[1:N_SHARD]
    rows = x_ref.shape[0]
    total = plain_dot(mix_ref[...], whole_ref[...])
    for i in range(0, N_REP, 2):
        weights = jnp.concatenate([down_refs[i][...], down_refs[i + 1][...]], axis=0)
        total = total + plain_dot(act_ref[:, i * LANES : (i + 2) * LANES], weights)
    own_ref[...] = x_ref[...] + total[:rows] + last_ref[0:1, :]
    for k in range(1, N_SHARD):
        sent_refs[k - 1][...] = total[k * rows : (k + 1) * rows].astype(bf16)
    hidden_body(s_ref, dy_ref, *down_refs, slope_ref, whole_ref, *refs[N_SHARD:])


def terms_body(
    s_ref, h_ref, dqkv_ref, mix_ref, dy_ref, norm_ref, qkv_sum_ref, up_sum_ref, cot_ref, keep_ref, sent_ref, vec_ref, g_ref
):
    half = keep_ref.shape[0]
    keep_ref[:, :QKV] = contract_rows(h_ref[:, :half], dqkv_ref[...])
    sent_ref[:, :QKV] = contract_rows(h_ref[:, half:], dqkv_ref[...]).astype(bf16)
    g_ref[...] = contract_rows(mix_ref[...], dy_ref[...])
    vec_ref[...] = jnp.zeros_like(vec_ref)
    vec_ref[0:4, :] = norm_ref[0:4, :]
    for row, block, at in bias_places(s_ref):
        ref, at = (qkv_sum_ref, at) if at < QKV else (up_sum_ref, at - QKV)
        vec_ref[row : row + 1, lane_block(block)] = ref[0:1, at : at + LANES]
    rows = OUT // N_REP
    for i in range(N_REP):
        here = slice(i * LANES, (i + 1) * LANES)
        cot = cot_ref[0:1, lane_block(s_ref[ORDER + i])]
        vec_ref[7:8, here] = cot
        vec_ref[12:13, here] = cot
        ref = keep_ref if i < N_REP // 2 else sent_ref
        base = i * LANES % half
        found = g_ref[row_block(s_ref[ORDER + i], rows), :]
        for c in range(D // OUT):
            ref[base + c * rows : base + (c + 1) * rows, QKV : QKV + OUT] = found[
                :, c * OUT : (c + 1) * OUT
            ].astype(ref.dtype)
        ref[base : base + LANES, QKV + OUT :] = vec_ref[:, here].T.astype(ref.dtype)


def mlp_body(s_ref, act_ref, dy_ref, h_ref, du_ref, keep_ref, sent_ref):
    half = keep_ref.shape[0]
    for left, right, at in ((act_ref, dy_ref, 0), (h_ref, du_ref, D)):
        cols = slice(at, at + right.shape[1])
        sent_ref[:, cols] = contract_rows(left[:, half:], right[...]).astype(bf16)
        keep_ref[:, cols] = contract_rows(left[:, :half], right[...])


def fold_body(s_ref, *refs):
    up_refs, refs = refs[:4], refs[4:]
    qkv_refs, refs = refs[:4], refs[4:]
    own_ref, sent_refs, out_ref, up_sum, qkv_sum = refs[0], refs[1:4], refs[4], refs[5], refs[6]
    for some, total, first in ((up_refs, up_sum, D), (qkv_refs, qkv_sum, 0)):
        total[...] = sum(ref[:, first:].astype(f32) for ref in some)
    rows = own_ref.shape[0]
    for k in range(N_SHARD):
        at = row_block(s_ref[NEAR + k], rows)
        ref = own_ref if k == 0 else sent_refs[k - 1]
        ref[:, :QKV] = qkv_sum[at, :QKV].astype(ref.dtype)
        ref[:, QKV : QKV + UP] = up_sum[at, :].astype(ref.dtype)
        ref[:, QKV + UP :] = qkv_sum[at, QKV + OUT :].astype(ref.dtype)
    for c in range(D // OUT):
        out_ref[:, c * OUT : (c + 1) * OUT] = qkv_sum[c * rows : (c + 1) * rows, QKV : QKV + OUT]


def adam_body(s_ref, *refs):
    got, refs = refs[:N_SHARD], refs[N_SHARD:]
    states, vec_state, refs = (refs[0:3], refs[3:6]), refs[6:9], refs[9:]
    results, vec_result, refs = (refs[0:4], refs[4:8]), refs[8:12], refs[12:]
    all_ref, turn_ref = refs
    for k in range(N_SHARD):
        all_ref[k] = got[k][...].astype(f32)
    count, cols = vec_state[0].shape
    turn_ref[...] = jnp.zeros_like(turn_ref)
    turn_ref[:cols, :] = sum(all_ref[k, :, QKV + UP :] for k in range(N_SHARD))
    turn_ref[...] = turn_ref[...].T
    grad = turn_ref[:count, :cols]
    vec_result[0][...] = grad
    new = adam_update(vec_state[0][...], grad, vec_state[1][...], vec_state[2][...], LR_VECTOR, 0.0)
    for ref, value in zip(vec_result[1:], new):
        ref[...] = value
    first = 0
    for state, result in zip(states, results):
        for c in range(state[0].shape[1] // (N_SHARD * LANES)):
            for t in range(N_SHARD):
                grad = all_ref[s_ref[NEAR + t], :, first : first + LANES]
                at = slice((c * N_SHARD + t) * LANES, (c * N_SHARD + t + 1) * LANES)
                result[0][:, at] = grad
                new = adam_update(
                    state[0][:, at], grad, state[1][:, at], state[2][:, at], LR_MATRIX, WEIGHT_DECAY
                )
                for ref, value in zip(result[1:], new):
                    ref[:, at] = value
            first += LANES


def finish_body(s_ref, own_ref, r1_ref, r2_ref, r3_ref, x_ref, cot_ref, o_ref, e_ref):
    total = own_ref[...] + r1_ref[...].astype(f32) + r2_ref[...].astype(f32) + r3_ref[...].astype(f32)
    for i in range(N_REP):
        e_ref[:, lane_block(s_ref[ORDER + i])] = total[:, i * LANES : (i + 1) * LANES]
    x = x_ref[...]
    center = x - jnp.mean(x, axis=-1, keepdims=True)
    inv_std = lax.rsqrt(jnp.mean(center * center, axis=-1, keepdims=True) + LN_EPS)
    normed = center * inv_std
    scaled = e_ref[...]
    o_ref[...] = cot_ref[...] + inv_std * (
        scaled
        - jnp.mean(scaled, axis=-1, keepdims=True)
        - normed * jnp.mean(scaled * normed, axis=-1, keepdims=True)
    )


def to_shards(values):
    return [hop(values[k - 1], "shard", N_SHARD, k) for k in range(1, N_SHARD)]


def to_chips(values):
    return [hop(values[k - 1], "rep", N_REP, 2 * k) for k in range(1, 4)]


def gather_chips(own):
    near = [own] + to_chips([own] * 3)
    return near + [hop(piece, "rep", N_REP, 1) for piece in near]


def sum_rep(keep, got, *earlier):
    parts = [keep[k] + got[k].astype(f32) for k in range(4)]
    sent = [part.astype(bf16) for part in parts[1:]]
    if earlier:
        sent = [after(part, *earlier) for part in sent]
    return [parts[0]] + to_chips(sent)


def after(value, *others):
    return lax.optimization_barrier((value,) + others)[0]


def shards(
    block_in,
    cotangent,
    segments,
    qkv_weight,
    out_weight,
    up_weight,
    down_weight,
    vectors,
    first_qkv,
    first_out,
    first_up,
    first_down,
    first_vec,
    second_qkv,
    second_out,
    second_up,
    second_down,
    second_vec,
):
    tok_count = block_in.shape[0]
    rep = lax.axis_index("rep")
    shard = lax.axis_index("shard")
    seq_len = tok_count * N_SHARD
    rows = qkv_weight.shape[0]
    units = down_weight.shape[0]
    n_vec, cols = vectors.shape
    masks = np.array([0, 2, 4, 6, 1, 3, 5, 7], np.int32)
    spots = np.argsort(masks)
    device = np.arange(N_REP)
    places = spots[device[:, None] ^ device[None, :]].astype(np.int32)
    orders = (device[:, None] ^ masks[None, :]).astype(np.int32)
    near = shard ^ jnp.arange(N_SHARD, dtype=jnp.int32)
    table = jnp.asarray(np.concatenate([orders, places], axis=1))
    scalars = jnp.concatenate(
        [lax.dynamic_index_in_dim(table, rep, 0, keepdims=False), near, shard[None]]
    ).astype(jnp.int32)

    share = HEAD // rows
    pair = LANES // HEAD
    moves = []
    for at in range(N_REP * N_SHARD):
        head, part = at // share, at % share
        owner = (head // pair) % N_SHARD
        local = (head // (pair * N_SHARD)) * pair + head % pair
        moves.append((at, (local * share + part) * N_SHARD + owner))

    own_cols = [((rows, QKV + UP + LANES), bf16)] * N_SHARD
    square = pltpu.VMEM((LANES, LANES), f32)
    packed = single(
        pack_body, own_cols, scalars, [qkv_weight, up_weight, vectors], 1, "pack", [square]
    )
    got_cols = to_shards(packed[1:])
    out_rows = lax.ppermute(out_weight.astype(bf16), ("rep", "shard"), moves)
    down_own = down_weight.astype(bf16)
    (normed_own,) = single(
        norm_body,
        [((tok_count, D), bf16)],
        scalars,
        [block_in],
        1,
        "norm",
        [pltpu.VMEM((tok_count, D), f32)],
    )
    (in_rows,) = single(
        join_body,
        [((N_SHARD * rows, QKV + UP + OUT + LANES), bf16)],
        scalars,
        [packed[0], *got_cols[:2], after(got_cols[2], normed_own), out_rows],
        1,
        "join",
    )
    normed = [normed_own] + to_shards([after(normed_own, *got_cols)] * 3)
    pieces = [in_rows] + to_chips([in_rows, in_rows, after(in_rows, normed[1])])
    pieces = pieces + [hop(after(piece, normed[2], normed[3]), "rep", N_REP, 1) for piece in pieces]
    downs = [down_own] + to_chips([after(down_own, *pieces[1:4])] * 3)
    dy_own = after(cotangent.astype(bf16), *normed[1:3])
    dy_all = lax.all_gather(dy_own, "shard", axis=0, tiled=True)

    rope_parts = jnp.asarray(rope_lanes(seq_len)).reshape(N_SHARD, tok_count, 3 * LANES)
    rope = jnp.concatenate(
        [lax.dynamic_index_in_dim(rope_parts, near[k], 0, keepdims=False) for k in range(N_SHARD)]
    )
    seg_row = jnp.concatenate(
        [lax.dynamic_slice(segments[0], (near[k] * tok_count,), (tok_count,)) for k in range(N_SHARD)]
    )
    positions = (near[:, None] * tok_count + jnp.arange(tok_count)[None, :]).reshape(seq_len)
    allowed = (seg_row[:, None] == seg_row[None, :]) & (positions[None, :] <= positions[:, None])
    mask = jnp.where(allowed, 0.0, HIDDEN).astype(f32)

    out_whole, h_one, h_two, qkv16, act16, slope, vec_rel, last = front(
        scalars, normed, pieces, rope
    )
    block16 = ((tok_count, D), bf16)
    block32 = ((tok_count, D), f32)
    half = D // 2
    downs = downs + [hop(after(piece, qkv16), "rep", N_REP, 1) for piece in downs]
    mixed16 = mix_heads(qkv16, mask)
    out_own, s1, s2, s3, dy_seq, d_mixed16, d_up16, up_sum = single(
        middle_body,
        [
            block32,
            block16,
            block16,
            block16,
            ((seq_len, D), bf16),
            ((seq_len, OUT), bf16),
            ((seq_len, UP), bf16),
            ((8, UP), f32),
        ],
        scalars,
        [mixed16, act16, out_whole, last, block_in, dy_all, slope, *downs],
        2,
        "middle",
    )
    out_got = [hop(s1, "shard", N_SHARD, 1), hop(s2, "shard", N_SHARD, 2)]

    mlp_keep, mlp_sent = single(
        mlp_body,
        [((half, D + UP), f32), ((half, D + UP), bf16)],
        scalars,
        [act16, dy_seq, h_two, d_up16],
        1,
        "mlp",
    )
    mlp_got = hop(mlp_sent.reshape(4, LANES, D + UP), "rep", N_REP, 1)
    mlp_parts = sum_rep(mlp_keep.reshape(4, LANES, D + UP), mlp_got)
    d_mixed16 = after(d_mixed16, mlp_got)
    d_qkv16, qkv_sum = attend_back(qkv16, d_mixed16, mixed16, mask, rope)
    out_got.append(hop(after(s3, d_qkv16), "shard", N_SHARD, 3))
    d_qkv16 = after(d_qkv16, *out_got[:2])
    h_one = after(h_one, out_got[2], *mlp_parts[1:])

    e_own, *e_sent, norm_sum = single(
        back_body,
        [block32, block16, block16, block16, ((8, D), f32)],
        scalars,
        [d_qkv16, d_up16, vec_rel, *normed, *pieces],
        1,
        "back",
    )
    cot_sum = jnp.sum(cotangent, axis=0, keepdims=True)
    wide = QKV + OUT + LANES
    qkv_keep, qkv_sent = single(
        terms_body,
        [((half, wide), f32), ((half, wide), bf16)],
        scalars,
        [h_one, d_qkv16, mixed16, dy_seq, norm_sum, qkv_sum, up_sum, cot_sum],
        4,
        "terms",
        [pltpu.VMEM((LANES, D), f32), pltpu.VMEM((OUT, D), f32)],
    )
    qkv_got = hop(qkv_sent.reshape(4, LANES, wide), "rep", N_REP, 1)
    qkv_parts = sum_rep(qkv_keep.reshape(4, LANES, wide), qkv_got, *mlp_parts[1:])
    e_got = [hop(e_sent[0], "shard", N_SHARD, 1), hop(e_sent[1], "shard", N_SHARD, 2)]
    e_got.append(hop(after(e_sent[2], qkv_parts[1]), "shard", N_SHARD, 3))
    narrow = (rows, QKV + UP + LANES)
    g_own, g1, g2, g3, out_sum = single(
        fold_body,
        [(narrow, f32), (narrow, bf16), (narrow, bf16), (narrow, bf16), ((rows, D), f32)],
        scalars,
        [*mlp_parts, after(qkv_parts[0], *e_got[:2]), *qkv_parts[1:]],
        1,
        "fold",
        [pltpu.VMEM((LANES, UP), f32), pltpu.VMEM((LANES, wide), f32)],
    )
    g_got = to_shards([g1, g2, g3])
    grad_out = lax.ppermute(out_sum, ("rep", "shard"), [(b, a) for a, b in moves])
    block_out = out_own + out_got[0].astype(f32) + out_got[1].astype(f32) + out_got[2].astype(f32)
    grad_down = sum(part[:, :D].astype(f32) for part in mlp_parts)
    (grad_input,) = single(
        finish_body,
        [block32],
        scalars,
        [e_own, *e_got, block_in, cotangent],
        2,
        "finish",
        [pltpu.VMEM((tok_count, D), f32)],
    )
    qkv_shape = (qkv_weight.shape, f32)
    up_shape = (up_weight.shape, f32)
    vec_shape = (vectors.shape, f32)
    (
        grad_qkv,
        new_qkv,
        new_first_qkv,
        new_second_qkv,
        grad_up,
        new_up,
        new_first_up,
        new_second_up,
        grad_vec,
        new_vec,
        new_first_vec,
        new_second_vec,
    ) = single(
        adam_body,
        [qkv_shape] * 4 + [up_shape] * 4 + [vec_shape] * 4,
        scalars,
        [
            after(g_own, e_got[2]),
            *g_got,
            qkv_weight,
            first_qkv,
            second_qkv,
            up_weight,
            first_up,
            second_up,
            vectors,
            first_vec,
            second_vec,
        ],
        3,
        "adam",
        [pltpu.VMEM((N_SHARD,) + narrow, f32), square],
    )

    new_out, new_first_out, new_second_out = adam_update(
        out_weight, grad_out, first_out, second_out, LR_MATRIX, WEIGHT_DECAY
    )
    new_down, new_first_down, new_second_down = adam_update(
        down_weight, grad_down, first_down, second_down, LR_MATRIX, WEIGHT_DECAY
    )
    return (
        block_out,
        grad_input,
        grad_qkv,
        grad_out,
        grad_up,
        grad_down,
        grad_vec,
        new_qkv,
        new_out,
        new_up,
        new_down,
        new_vec,
        new_first_qkv,
        new_first_out,
        new_first_up,
        new_first_down,
        new_first_vec,
        new_second_qkv,
        new_second_out,
        new_second_up,
        new_second_down,
        new_second_vec,
    )


def solution(mesh):
    aligned = mesh.shape["rep"] == N_REP and mesh.shape["shard"] == N_SHARD
    return jax.shard_map(
        shards if aligned else general,
        mesh=mesh,
        in_specs=(
            P(("rep", "shard"), None),
            P(("rep", "shard"), None),
            P("rep", None),
            P(("rep", "shard"), None),
            P(("rep", "shard"), None),
            P(("rep", "shard"), None),
            P(("rep", "shard"), None),
            P(None, ("rep", "shard")),
            P(("rep", "shard"), None),
            P(("rep", "shard"), None),
            P(("rep", "shard"), None),
            P(("rep", "shard"), None),
            P(None, ("rep", "shard")),
            P(("rep", "shard"), None),
            P(("rep", "shard"), None),
            P(("rep", "shard"), None),
            P(("rep", "shard"), None),
            P(None, ("rep", "shard")),
        ),
        out_specs=(
            P(("rep", "shard"), None),
            P(("rep", "shard"), None),
            P(("rep", "shard"), None),
            P(("rep", "shard"), None),
            P(("rep", "shard"), None),
            P(("rep", "shard"), None),
            P(None, ("rep", "shard")),
            P(("rep", "shard"), None),
            P(("rep", "shard"), None),
            P(("rep", "shard"), None),
            P(("rep", "shard"), None),
            P(None, ("rep", "shard")),
            P(("rep", "shard"), None),
            P(("rep", "shard"), None),
            P(("rep", "shard"), None),
            P(("rep", "shard"), None),
            P(None, ("rep", "shard")),
            P(("rep", "shard"), None),
            P(("rep", "shard"), None),
            P(("rep", "shard"), None),
            P(("rep", "shard"), None),
            P(None, ("rep", "shard")),
        ),
        check_vma=False,
    )
```

```python
import jax
import jax.numpy as jnp
import numpy as np
from jax import lax
from jax.experimental import pallas as pl
from jax.experimental.pallas import tpu as pltpu
from jax.sharding import PartitionSpec as P

D = 1024
HEADS = 16
HEAD = D // HEADS
FF = 4096
ROT = 16
STEP = 10
LANES = 128


LN_EPS = 1e-05
BETA_ONE = 0.9
BETA_TWO = 0.95
ADAM_EPS = 1e-08
LR_MATRIX = 0.03
LR_VECTOR = 0.2
WEIGHT_DECAY = 0.01
ROPE_BASE = 10000.0
INV_ROOT_TWO = 0.7071067811865476
INV_ROOT_TAU = 0.3989422804014327
HIDDEN = -1e30
bf16 = jnp.bfloat16
f32 = jnp.float32
TILE = 256


def adam_update(param, grad, first, second, rate, decay):
    first_new = BETA_ONE * first + (1.0 - BETA_ONE) * grad
    second_new = BETA_TWO * second + (1.0 - BETA_TWO) * grad * grad
    first_hat = first_new / (1.0 - BETA_ONE**STEP)
    second_hat = second_new / (1.0 - BETA_TWO**STEP)
    return (
        param - rate * (first_hat / (jnp.sqrt(second_hat) + ADAM_EPS) + decay * param),
        first_new,
        second_new,
    )


def contract_rows(left, right):
    return lax.dot_general(left, right, (((0,), (0,)), ((), ())), preferred_element_type=f32)


def contract_cols(left, right):
    return lax.dot_general(left, right, (((1,), (1,)), ((), ())), preferred_element_type=f32)


def plain_dot(left, right):
    return jnp.dot(left, right, preferred_element_type=f32)


def rope_lanes(seq_len):
    half = ROT // 2
    freqs = (ROPE_BASE ** (-(2.0 * np.arange(half, dtype=np.float32) / ROT))).astype(np.float32)
    angles = np.arange(seq_len, dtype=np.float32)[:, None] * freqs[None, :]
    cosines, sines = np.cos(angles), np.sin(angles)
    keep = np.ones((seq_len, HEAD), np.float32)
    up = np.zeros((seq_len, HEAD), np.float32)
    down = np.zeros((seq_len, HEAD), np.float32)
    keep[:, :half], keep[:, half:ROT] = cosines, cosines
    up[:, :half] = -sines
    down[:, half:ROT] = sines
    reps = LANES // HEAD
    return np.concatenate([np.tile(t, (1, reps)) for t in (keep, up, down)], axis=1)


def turn(values, table, sign):
    half = ROT // 2
    above = pltpu.roll(values, LANES - half, 1)
    below = pltpu.roll(values, half, 1)
    moved = above * table[:, LANES : 2 * LANES] + below * table[:, 2 * LANES :]
    return values * table[:, :LANES] + sign * moved


def params(mib):
    return pltpu.CompilerParams(vmem_limit_bytes=mib << 20)


def cost(micros):
    return pl.CostEstimate(flops=int(micros * 1.15e9), bytes_accessed=1 << 20, transcendentals=0)


def whole_spec(shape):
    return pl.BlockSpec(shape, lambda *_: (0,) * len(shape))


def rope_tables(positions):
    half_rot = ROT // 2
    freqs = ROPE_BASE ** (-(2.0 * jnp.arange(half_rot).astype(jnp.float32) / ROT))
    angles = positions.astype(jnp.float32)[:, None] * freqs[None, :]
    return (jnp.cos(angles)[:, None, :], jnp.sin(angles)[:, None, :])


def rotate(heads, cosines, sines):
    half_rot = ROT // 2
    lower = heads[..., :half_rot]
    upper = heads[..., half_rot:ROT]
    return jnp.concatenate(
        [lower * cosines - upper * sines, upper * cosines + lower * sines, heads[..., ROT:]],
        axis=-1,
    )


def unrotate(heads, cosines, sines):
    half_rot = ROT // 2
    lower = heads[..., :half_rot]
    upper = heads[..., half_rot:ROT]
    return jnp.concatenate(
        [lower * cosines + upper * sines, upper * cosines - lower * sines, heads[..., ROT:]],
        axis=-1,
    )


def gelu_value(inner):
    return 0.5 * inner * (1.0 + jax.scipy.special.erf(inner * INV_ROOT_TWO))


def gelu_slope(inner):
    return (
        0.5 * (1.0 + jax.scipy.special.erf(inner * INV_ROOT_TWO))
        + inner * jnp.exp(-0.5 * inner * inner) * INV_ROOT_TAU
    )


def hop(value, axis, size, mask):
    return lax.ppermute(value, axis, [(i, i ^ mask) for i in range(size)])


def pick(blocks, index, axis=0):
    return lax.dynamic_index_in_dim(blocks, index, axis, keepdims=False)


def stages(size):
    bits = size.bit_length() - 1
    found = []
    while bits > 0:
        take = 2 if bits >= 2 else 1
        bits -= take
        found.append((bits, 1 << take))
    return found


def gather_axis(own, axis, me, size):
    if size > 16:
        return lax.all_gather(own, axis)
    pieces = {0: own}
    for shift, count in stages(size):
        more = dict(pieces)
        for k in range(1, count):
            for mask, piece in pieces.items():
                more[mask ^ (k << shift)] = hop(piece, axis, size, k << shift)
        pieces = more
    whole = jnp.zeros((size,) + own.shape, own.dtype)
    for mask in range(size):
        whole = lax.dynamic_update_index_in_dim(whole, pieces[mask], me ^ mask, 0)
    return whole


def exchange_axis(blocks, axis, me, size, wire):
    got = [(0, pick(blocks, me))]
    for mask in range(1, size):
        got.append((mask, hop(pick(blocks, me ^ mask).astype(wire), axis, size, mask)))
    return got


def reduce_axis(blocks, axis, me, size, wire):
    current = blocks
    for shift, count in reversed(stages(size)):
        left = current.shape[0] // count
        view = current.reshape((left, count) + current.shape[1:])
        digit = (me >> shift) & (count - 1)
        total = pick(view, digit, 1)
        for k in range(1, count):
            sent = pick(view, digit ^ k, 1).astype(wire)
            total = total + hop(sent, axis, size, k << shift).astype(jnp.float32)
        current = total
    return current[0]


def general(
    block_in,
    cotangent,
    segments,
    qkv_weight,
    out_weight,
    up_weight,
    down_weight,
    vectors,
    first_qkv,
    first_out,
    first_up,
    first_down,
    first_vec,
    second_qkv,
    second_out,
    second_up,
    second_down,
    second_vec,
):
    tok_count = block_in.shape[0]
    n_rep = lax.axis_size("rep")
    n_shard = lax.axis_size("shard")
    rep = lax.axis_index("rep")
    shard = lax.axis_index("shard")
    seq_len = tok_count * n_shard
    head_dim = D // HEADS
    own_heads = HEADS // n_shard
    own_feats = own_heads * head_dim
    rows = qkv_weight.shape[0]
    units = down_weight.shape[0]
    own_units = units * n_rep
    cols = vectors.shape[1]
    score_scale = head_dim ** (-0.5)

    qkv_cols = qkv_weight.astype(bf16).reshape(rows, 3, own_heads, n_shard, head_dim)
    qkv_cols = qkv_cols.transpose(3, 0, 1, 2, 4).reshape(n_shard, rows, 3 * own_feats)
    up_cols = up_weight.astype(bf16).reshape(rows, n_rep, n_shard, units)
    up_cols = up_cols.transpose(2, 0, 1, 3).reshape(n_shard, rows, own_units)
    in_cols = jnp.concatenate([qkv_cols, up_cols], axis=2)
    in_rows = jnp.zeros_like(in_cols)
    for mask, piece in exchange_axis(in_cols, "shard", shard, n_shard, bf16):
        in_rows = lax.dynamic_update_index_in_dim(in_rows, piece, shard ^ mask, 0)
    in_rows = in_rows.reshape(n_shard * rows, 3 * own_feats + own_units)

    center = block_in - jnp.mean(block_in, axis=-1, keepdims=True)
    inv_std = lax.rsqrt(jnp.mean(center * center, axis=-1, keepdims=True) + LN_EPS)
    normed = center * inv_std
    normed_seq = gather_axis(normed.astype(bf16), "shard", shard, n_shard).reshape(seq_len, D)
    normed_seq = normed_seq.astype(f32)

    vec_some = gather_axis(vectors, "shard", shard, n_shard)
    vec_all = gather_axis(vec_some, "rep", rep, n_rep)
    vec_all = vec_all.transpose(2, 0, 1, 3).reshape(vectors.shape[0], D)

    in_whole = gather_axis(in_rows, "rep", rep, n_rep).reshape(D, 3 * own_feats + own_units)
    upstream16 = gather_axis(cotangent.astype(bf16), "shard", shard, n_shard).reshape(seq_len, D)
    down_whole = gather_axis(down_weight.astype(bf16), "rep", rep, n_rep).reshape(own_units, D)
    share = head_dim // rows
    moves = []
    for device in range(n_rep * n_shard):
        head, part = device // share, device % share
        moves.append((device, ((head // n_shard) * share + part) * n_shard + head % n_shard))
    out_rows = lax.ppermute(out_weight.astype(bf16), ("rep", "shard"), moves)
    out_whole = gather_axis(out_rows, "rep", rep, n_rep).reshape(own_feats, D)

    per_row = FF // D
    gain_one, shift_one, gain_two, shift_two = (vec_all[0], vec_all[1], vec_all[2], vec_all[3])
    qkv_bias = pick(vec_all[4:7].reshape(3, own_heads, n_shard, head_dim), shard, 2).reshape(
        3 * own_feats
    )
    up_bias = pick(vec_all[8 : 8 + per_row].reshape(n_rep, n_shard, units), shard, 1).reshape(
        own_units
    )
    out_bias = vec_all[7]
    down_bias = vec_all[8 + per_row]

    h_one = (normed_seq * gain_one + shift_one).astype(bf16)
    h_two = (normed_seq * gain_two + shift_two).astype(bf16)
    qkv_whole = in_whole[:, : 3 * own_feats]
    up_whole = in_whole[:, 3 * own_feats :]
    qkv_lin = jnp.dot(h_one, qkv_whole, preferred_element_type=f32) + qkv_bias
    up_lin = jnp.dot(h_two, up_whole, preferred_element_type=f32) + up_bias

    positions = jnp.arange(seq_len)
    cosines, sines = rope_tables(positions)

    def heads_of(values):
        return values.reshape(seq_len, own_heads, head_dim)

    query16 = rotate(heads_of(qkv_lin[:, :own_feats]), cosines, sines).astype(bf16)
    key16 = rotate(heads_of(qkv_lin[:, own_feats : 2 * own_feats]), cosines, sines).astype(bf16)
    value16 = heads_of(qkv_lin[:, 2 * own_feats :]).astype(bf16)
    seg_row = segments[0]
    allowed = (seg_row[:, None] == seg_row[None, :]) & (positions[None, :] <= positions[:, None])
    scores = jnp.where(
        allowed[None],
        jnp.einsum("qhd,khd->hqk", query16, key16, preferred_element_type=f32) * score_scale,
        -jnp.inf,
    )
    row_max = jnp.max(scores, axis=-1, keepdims=True)
    expo = jnp.exp(scores - row_max)
    row_sum = jnp.sum(expo, axis=-1, keepdims=True)
    log_total = row_max + jnp.log(row_sum)
    probs16 = (expo / row_sum).astype(bf16)
    mixed16 = (
        jnp.einsum("hqk,khd->qhd", probs16, value16, preferred_element_type=f32)
        .reshape(seq_len, own_feats)
        .astype(bf16)
    )
    act16 = gelu_value(up_lin).astype(bf16)
    branches = jnp.dot(mixed16, out_whole, preferred_element_type=f32)
    branches = branches + jnp.dot(act16, down_whole, preferred_element_type=f32)
    branches = reduce_axis(
        branches.reshape(n_shard, tok_count, D), "shard", shard, n_shard, bf16
    )
    block_out = block_in + branches + out_bias + down_bias

    term_down = contract_rows(act16, upstream16)
    sum_down = reduce_axis(term_down.reshape(n_rep, units, D), "rep", rep, n_rep, bf16)
    term_out = contract_rows(mixed16, upstream16)
    sum_out = reduce_axis(term_out.reshape(n_rep, rows, D), "rep", rep, n_rep, bf16)
    grad_out = lax.ppermute(sum_out, ("rep", "shard"), [(b, a) for a, b in moves])
    grad_down = sum_down
    d_act = contract_cols(upstream16, down_whole)
    d_mixed16 = heads_of(contract_cols(upstream16, out_whole)).astype(bf16)
    d_up = d_act * gelu_slope(up_lin)
    d_up16 = d_up.astype(bf16)
    term_up = contract_rows(h_two, d_up16)
    sum_up = reduce_axis(
        term_up.reshape(n_rep, n_shard * rows, own_units), "rep", rep, n_rep, bf16
    )

    def back_rows(sums, width):
        whole = jnp.zeros((n_shard, rows, width), f32)
        blocks = sums.reshape(n_shard, rows, width)
        for mask, piece in exchange_axis(blocks, "shard", shard, n_shard, bf16):
            whole = lax.dynamic_update_index_in_dim(whole, piece.astype(f32), shard ^ mask, 0)
        return whole

    grad_up = back_rows(sum_up, own_units).reshape(n_shard, rows, n_rep, units)
    grad_up = grad_up.transpose(1, 2, 0, 3).reshape(rows, FF)

    row_delta = jnp.sum(
        d_mixed16.astype(f32) * heads_of(mixed16).astype(f32),
        axis=-1,
    ).T[:, :, None]
    probs_again = jnp.exp(scores - log_total)
    d_probs = jnp.einsum("qhd,khd->hqk", d_mixed16, value16, preferred_element_type=f32)
    d_scores16 = (probs_again * (d_probs - row_delta) * score_scale).astype(bf16)
    probs_back16 = probs_again.astype(bf16)
    d_query = jnp.einsum("hqk,khd->qhd", d_scores16, key16, preferred_element_type=f32)
    d_keys = jnp.einsum("hqk,qhd->khd", d_scores16, query16, preferred_element_type=f32)
    d_values = jnp.einsum("hqk,qhd->khd", probs_back16, d_mixed16, preferred_element_type=f32)
    d_qkv = jnp.concatenate(
        [
            unrotate(d_query, cosines, sines).reshape(seq_len, own_feats),
            unrotate(d_keys, cosines, sines).reshape(seq_len, own_feats),
            d_values.reshape(seq_len, own_feats),
        ],
        axis=1,
    )
    d_qkv16 = d_qkv.astype(bf16)
    term_qkv = contract_rows(h_one, d_qkv16)
    sum_qkv = reduce_axis(
        term_qkv.reshape(n_rep, n_shard * rows, 3 * own_feats), "rep", rep, n_rep, bf16
    )
    grad_qkv = back_rows(sum_qkv, 3 * own_feats)
    grad_qkv = grad_qkv.reshape(n_shard, rows, 3, own_heads, head_dim)
    grad_qkv = grad_qkv.transpose(1, 2, 3, 0, 4).reshape(rows, 3 * D)

    d_one = contract_cols(d_qkv16, qkv_whole)
    d_two = contract_cols(d_up16, up_whole)
    scaled = d_one * gain_one + d_two * gain_two
    scaled = reduce_axis(scaled.reshape(n_shard, tok_count, D), "shard", shard, n_shard, bf16)
    grad_input = cotangent + inv_std * (
        scaled
        - jnp.mean(scaled, axis=-1, keepdims=True)
        - normed * jnp.mean(scaled * normed, axis=-1, keepdims=True)
    )

    mine = jnp.arange(n_shard) == shard
    cot_sum = jnp.sum(cotangent, axis=0)
    bias_qkv = jnp.where(
        mine[None, None, :, None],
        jnp.sum(d_qkv, axis=0).reshape(3, own_heads, 1, head_dim),
        0.0,
    ).reshape(3, D)
    bias_up = jnp.where(
        mine[None, :, None], jnp.sum(d_up, axis=0).reshape(n_rep, 1, units), 0.0
    ).reshape(per_row, D)
    vec_terms = jnp.concatenate(
        [
            jnp.sum(d_one * normed_seq, axis=0)[None],
            jnp.sum(d_one, axis=0)[None],
            jnp.sum(d_two * normed_seq, axis=0)[None],
            jnp.sum(d_two, axis=0)[None],
            bias_qkv,
            cot_sum[None],
            bias_up,
            cot_sum[None],
        ],
        axis=0,
    )
    vec_blocks = vec_terms.reshape(vectors.shape[0], n_rep, n_shard, cols).transpose(1, 2, 0, 3)
    grad_vec = reduce_axis(
        reduce_axis(vec_blocks, "rep", rep, n_rep, f32), "shard", shard, n_shard, f32
    )

    new_qkv, new_first_qkv, new_second_qkv = adam_update(
        qkv_weight, grad_qkv, first_qkv, second_qkv, LR_MATRIX, WEIGHT_DECAY
    )
    new_out, new_first_out, new_second_out = adam_update(
        out_weight, grad_out, first_out, second_out, LR_MATRIX, WEIGHT_DECAY
    )
    new_up, new_first_up, new_second_up = adam_update(
        up_weight, grad_up, first_up, second_up, LR_MATRIX, WEIGHT_DECAY
    )
    new_down, new_first_down, new_second_down = adam_update(
        down_weight, grad_down, first_down, second_down, LR_MATRIX, WEIGHT_DECAY
    )
    new_vec, new_first_vec, new_second_vec = adam_update(
        vectors, grad_vec, first_vec, second_vec, LR_VECTOR, 0.0
    )
    return (
        block_out,
        grad_input,
        grad_qkv,
        grad_out,
        grad_up,
        grad_down,
        grad_vec,
        new_qkv,
        new_out,
        new_up,
        new_down,
        new_vec,
        new_first_qkv,
        new_first_out,
        new_first_up,
        new_first_down,
        new_first_vec,
        new_second_qkv,
        new_second_out,
        new_second_up,
        new_second_down,
        new_second_vec,
    )


ROOM = {
    "pack": 6,
    "norm": 4,
    "join": 4,
    "middle": 30,
    "back": 28,
    "terms": 20,
    "mlp": 28,
    "fold": 16,
    "finish": 10,
    "adam": 22,
}


def single(body, outs, prefetch, ins, micros, name, scratch=()):
    shapes = tuple(jax.ShapeDtypeStruct(s, d) for s, d in outs)
    return pl.pallas_call(
        body,
        out_shape=shapes,
        grid_spec=pltpu.PrefetchScalarGridSpec(
            num_scalar_prefetch=1,
            grid=(1,),
            in_specs=[whole_spec(a.shape) for a in ins],
            out_specs=tuple(whole_spec(s.shape) for s in shapes),
            scratch_shapes=list(scratch),
        ),
        compiler_params=params(ROOM[name]),
        cost_estimate=cost(micros),
        name=name,
    )(prefetch, *ins)


def lane_block(index):
    return pl.ds(pl.multiple_of(index * LANES, LANES), LANES)


def row_block(index, size):
    return pl.ds(pl.multiple_of(index * size, size), size)


N_REP = 8
N_SHARD = 4
ORDER = 0
PLACE = N_REP
NEAR = 2 * N_REP
SHARD = NEAR + N_SHARD
QKV = 3 * TILE
UP = D
OUT = TILE


def pack_body(s_ref, qkv_ref, up_ref, vec_ref, *refs):
    outs, turn_ref = refs[:-1], refs[-1]
    count, cols = vec_ref.shape
    turn_ref[...] = jnp.zeros_like(turn_ref)
    vec = vec_ref[...]
    for i in range(3):
        part = vec.astype(bf16).astype(f32)
        turn_ref[16 * i : 16 * i + count, :cols] = part
        vec = vec - part
    vec16 = turn_ref[...].T[:cols, :].astype(bf16)
    for k in range(N_SHARD):
        t = s_ref[NEAR + k]
        o_ref = outs[k]
        for c in range(QKV // LANES):
            o_ref[:, c * LANES : (c + 1) * LANES] = qkv_ref[:, lane_block(c * N_SHARD + t)].astype(bf16)
        for c in range(UP // LANES):
            at = QKV + c * LANES
            o_ref[:, at : at + LANES] = up_ref[:, lane_block(c * N_SHARD + t)].astype(bf16)
        o_ref[:, QKV + UP :] = vec16


def norm_body(s_ref, x_ref, o_ref, n_ref):
    x = x_ref[...]
    center = x - jnp.mean(x, axis=-1, keepdims=True)
    inv_std = lax.rsqrt(jnp.mean(center * center, axis=-1, keepdims=True) + LN_EPS)
    n_ref[...] = center * inv_std
    for i in range(N_REP):
        o_ref[:, i * LANES : (i + 1) * LANES] = n_ref[:, lane_block(s_ref[ORDER + i])].astype(bf16)


def join_body(s_ref, *refs):
    out_ref, o_ref = refs[N_SHARD], refs[N_SHARD + 1]
    rows = out_ref.shape[0]
    for k in range(N_SHARD):
        at = row_block(s_ref[NEAR + k], rows)
        o_ref[at, : QKV + UP] = refs[k][:, : QKV + UP]
        o_ref[at, QKV + UP + OUT :] = refs[k][:, QKV + UP :]
    for c in range(D // OUT):
        o_ref[c * rows : (c + 1) * rows, QKV + UP : QKV + UP + OUT] = out_ref[:, c * OUT : (c + 1) * OUT]


def bias_places(s_ref):
    shard = s_ref[SHARD]
    found = []
    for c in range(QKV // LANES):
        found.append((4 + c // 2, s_ref[PLACE + (c % 2) * N_SHARD + shard], c * LANES))
    for c in range(UP // LANES):
        found.append((8 + c // 2, s_ref[PLACE + (c % 2) * N_SHARD + shard], QKV + c * LANES))
    return found


def front_body(s_ref, *refs):
    n_refs, refs = refs[:N_SHARD], refs[N_SHARD:]
    w_refs, refs = refs[:N_REP], refs[N_REP:]
    v_refs, refs = refs[:N_REP], refs[N_REP:]
    out_refs, refs = refs[:N_REP], refs[N_REP:]
    rope_ref, whole_ref, h1_ref, h2_ref, qkv_ref, act_ref, slope_ref, vec_ref, last_ref, bias_ref = refs
    j = pl.program_id(0)
    rows = n_refs[0].shape[0]

    @pl.when(j == 0)
    def _():
        for i in range(N_REP):
            parts = v_refs[i][...].astype(f32).T
            vec_ref[:, i * LANES : (i + 1) * LANES] = (parts[0:16] + parts[16:32]) + parts[32:48]
        for k in range(N_SHARD):
            normed = n_refs[k][...].astype(f32)
            at = slice(k * rows, (k + 1) * rows)
            h1_ref[at, :] = (normed * vec_ref[0:1, :] + vec_ref[1:2, :]).astype(bf16)
            h2_ref[at, :] = (normed * vec_ref[2:3, :] + vec_ref[3:4, :]).astype(bf16)
        for row, block, at in bias_places(s_ref):
            bias_ref[at // TILE, 0:1, at % TILE : at % TILE + LANES] = vec_ref[row : row + 1, lane_block(block)]
        both = vec_ref[7:8, :] + vec_ref[12:13, :]
        for i in range(N_REP):
            last_ref[0:1, lane_block(s_ref[ORDER + i])] = both[:, i * LANES : (i + 1) * LANES]
        chunks = D // OUT
        size = out_refs[0].shape[0] // chunks
        for i in range(N_REP):
            at = row_block(s_ref[ORDER + i], size)
            for c in range(chunks):
                whole_ref[at, c * OUT : (c + 1) * OUT] = out_refs[i][c * size : (c + 1) * size, :]

    def product(h_ref):
        total = bias_ref[j, 0:1, :]
        for i in range(0, N_REP, 2):
            weights = jnp.concatenate([w_refs[i][...], w_refs[i + 1][...]], axis=0)
            total = total + plain_dot(h_ref[:, i * LANES : (i + 2) * LANES], weights)
        return total

    @pl.when(j < 2)
    def _():
        lin = product(h1_ref)
        for c in range(0, TILE, LANES):
            qkv_ref[:, c : c + LANES] = turn(lin[:, c : c + LANES], rope_ref[...], 1.0).astype(bf16)

    @pl.when(j == 2)
    def _():
        qkv_ref[...] = product(h1_ref).astype(bf16)

    @pl.when(j > 2)
    def _():
        lin = product(h2_ref)
        above = 0.5 * (1.0 + lax.erf(lin * INV_ROOT_TWO))
        act = (lin * above).astype(bf16)
        slope = above + lin * jnp.exp(-0.5 * lin * lin) * INV_ROOT_TAU
        for c in range(2):
            at = lane_block(s_ref[PLACE + (j - 3) * 2 + c])
            act_ref[:, at] = act[:, c * LANES : (c + 1) * LANES]
            slope_ref[:, at] = slope[:, c * LANES : (c + 1) * LANES]


def front(scalars, normed, pieces, rope):
    tokens = rope.shape[0]
    block = pieces[0].shape[0]
    shapes = (
        ((OUT, D), bf16),
        ((tokens, D), bf16),
        ((tokens, D), bf16),
        ((tokens, QKV), bf16),
        ((tokens, UP), bf16),
        ((tokens, UP), f32),
        ((16, D), f32),
        ((8, D), f32),
    )
    specs = [whole_spec(s) for s, _ in shapes]
    specs[3] = pl.BlockSpec((tokens, TILE), lambda j, s: (0, jnp.minimum(j, 2)))
    return pl.pallas_call(
        front_body,
        out_shape=tuple(jax.ShapeDtypeStruct(s, d) for s, d in shapes),
        grid_spec=pltpu.PrefetchScalarGridSpec(
            num_scalar_prefetch=1,
            grid=((QKV + UP) // TILE,),
            in_specs=[whole_spec(n.shape) for n in normed]
            + [pl.BlockSpec((block, TILE), lambda j, s: (0, j))] * N_REP
            + [pl.BlockSpec((block, LANES), lambda j, s: (0, (QKV + UP + OUT) // LANES))] * N_REP
            + [pl.BlockSpec((block, OUT), lambda j, s: (0, (QKV + UP) // OUT))] * N_REP
            + [whole_spec(rope.shape)],
            out_specs=tuple(specs),
            scratch_shapes=[pltpu.VMEM(((QKV + UP) // TILE, 8, TILE), f32)],
        ),
        compiler_params=params(24),
        cost_estimate=cost(9),
        name="front",
    )(scalars, *normed, *pieces, *pieces, *pieces, rope)


def hidden_body(s_ref, *refs):
    dy_ref, refs = refs[0], refs[1:]
    down_refs, refs = refs[:N_REP], refs[N_REP:]
    slope_ref, whole_ref, seq_ref, dmix_ref, du_ref, sum_ref = refs
    tokens = dy_ref.shape[0] // N_SHARD
    for k in range(N_SHARD):
        seq_ref[k * tokens : (k + 1) * tokens, :] = dy_ref[k * tokens : (k + 1) * tokens, :]
    dy = seq_ref[...]
    dmix_ref[...] = contract_cols(dy, whole_ref[...]).astype(bf16)
    for i in range(N_REP):
        du = contract_cols(dy, down_refs[i][...]) * slope_ref[:, i * LANES : (i + 1) * LANES]
        at = lane_block(s_ref[ORDER + i])
        du_ref[:, at] = du.astype(bf16)
        sum_ref[0:1, at] = jnp.sum(du, axis=0, keepdims=True)


def weigh(q, k, mask):
    score = contract_cols(q, k) * (HEAD ** (-0.5)) + mask
    expo = jnp.exp(score - jnp.max(score, axis=-1, keepdims=True))
    return expo * (1.0 / jnp.sum(expo, axis=-1, keepdims=True))


def only(values, mine):
    return jnp.where(mine, values, jnp.zeros_like(values))


def mix_body(q_ref, k_ref, v_ref, mask_ref, mix_ref):
    first = lax.broadcasted_iota(jnp.int32, (LANES, LANES), 1) < HEAD
    k = k_ref[...]
    v = v_ref[...]
    for c in range(0, q_ref.shape[0], LANES):
        rows = slice(c, c + LANES)
        q = q_ref[rows, :]
        mixes = []
        for mine in (first, jnp.logical_not(first)):
            prob = weigh(only(q, mine), k, mask_ref[rows, :])
            mixes.append(plain_dot(prob.astype(bf16), v))
        mix_ref[rows, :] = jnp.where(first, mixes[0], mixes[1]).astype(bf16)


def attend_body(
    q_ref, k_ref, v_ref, dm_ref, mix_ref, mask_ref, rope_ref, dqkv_ref, sum_ref, dk_ref, dv_ref
):
    pair = pl.program_id(0)
    tokens = q_ref.shape[0]
    scale = HEAD ** (-0.5)
    first = lax.broadcasted_iota(jnp.int32, (LANES, LANES), 1) < HEAD
    every = lax.broadcasted_iota(jnp.int32, (tokens, LANES), 1) < HEAD
    k = k_ref[...]
    v = v_ref[...]
    pairs = pl.num_programs(0)

    def columns(part):
        return lane_block(part * pairs + pair)

    dq_total = jnp.zeros((1, LANES), f32)
    for c in range(0, tokens, LANES):
        rows = slice(c, c + LANES)
        q = q_ref[rows, :]
        dm = dm_ref[rows, :]
        mix = mix_ref[rows, :].astype(f32)
        dqs, dks, dvs = [], [], []
        for mine in (first, jnp.logical_not(first)):
            dmh = only(dm, mine)
            prob = weigh(only(q, mine), k, mask_ref[rows, :])
            delta = jnp.sum(dmh.astype(f32) * mix, axis=-1, keepdims=True)
            d_prob = contract_cols(dmh, v)
            ds16 = (prob * (d_prob - delta) * scale).astype(bf16)
            dqs.append(plain_dot(ds16, k))
            dks.append(contract_rows(ds16, q))
            dvs.append(contract_rows(prob.astype(bf16), dm))
        dq = turn(jnp.where(first, dqs[0], dqs[1]), rope_ref[rows, :], -1.0)
        dqkv_ref[rows, columns(0)] = dq.astype(bf16)
        dq_total = dq_total + jnp.sum(dq, axis=0, keepdims=True)
        dk = jnp.where(every, dks[0], dks[1])
        dv = jnp.where(every, dvs[0], dvs[1])
        if c == 0:
            dk_ref[...] = dk
            dv_ref[...] = dv
        else:
            dk_ref[...] += dk
            dv_ref[...] += dv
    dk = turn(dk_ref[...], rope_ref[...], -1.0)
    dv = dv_ref[...]
    dqkv_ref[:, columns(1)] = dk.astype(bf16)
    dqkv_ref[:, columns(2)] = dv.astype(bf16)
    sum_ref[:, columns(0)] = dq_total
    sum_ref[:, columns(1)] = jnp.sum(dk, axis=0, keepdims=True)
    sum_ref[:, columns(2)] = jnp.sum(dv, axis=0, keepdims=True)


def pair_spec(tokens, first):
    return pl.BlockSpec((tokens, LANES), lambda j: (0, first + j))


def mix_heads(qkv, mask):
    tokens = qkv.shape[0]
    pairs = OUT // LANES
    return pl.pallas_call(
        mix_body,
        out_shape=jax.ShapeDtypeStruct((tokens, OUT), bf16),
        grid=(pairs,),
        in_specs=[pair_spec(tokens, i * pairs) for i in range(3)] + [whole_spec(mask.shape)],
        out_specs=pair_spec(tokens, 0),
        compiler_params=params(10),
        cost_estimate=cost(6),
        name="mix_heads",
    )(qkv, qkv, qkv, mask)


def attend_back(qkv, d_mix, mixed, mask, rope):
    tokens = qkv.shape[0]
    pairs = OUT // LANES
    return pl.pallas_call(
        attend_body,
        out_shape=(
            jax.ShapeDtypeStruct((tokens, QKV), bf16),
            jax.ShapeDtypeStruct((1, QKV), f32),
        ),
        grid=(pairs,),
        in_specs=[pair_spec(tokens, i * pairs) for i in range(3)]
        + [pair_spec(tokens, 0), pair_spec(tokens, 0), whole_spec(mask.shape), whole_spec(rope.shape)],
        out_specs=(whole_spec((tokens, QKV)), whole_spec((1, QKV))),
        scratch_shapes=[pltpu.VMEM((tokens, LANES), f32), pltpu.VMEM((tokens, LANES), f32)],
        compiler_params=params(12),
        cost_estimate=cost(4),
        name="attend_back",
    )(qkv, qkv, qkv, d_mix, mixed, mask, rope)


def back_body(s_ref, dqkv_ref, du_ref, vec_ref, *refs):
    n_refs, refs = refs[:N_SHARD], refs[N_SHARD:]
    w_refs, refs = refs[:N_REP], refs[N_REP:]
    own_ref, sent_refs, sum_ref = refs[0], refs[1:N_SHARD], refs[N_SHARD]
    rows = n_refs[0].shape[0]
    for i in range(0, N_REP, 2):
        cols = slice(i * LANES, (i + 2) * LANES)
        weights = jnp.concatenate([w_refs[i][:, : QKV + UP], w_refs[i + 1][:, : QKV + UP]], axis=0)
        d_one = contract_cols(dqkv_ref[...], weights[:, :QKV])
        d_two = contract_cols(du_ref[...], weights[:, QKV:])
        scaled = d_one * vec_ref[0:1, cols] + d_two * vec_ref[2:3, cols]
        own_ref[:, cols] = scaled[:rows]
        sums = [jnp.sum(d, axis=0, keepdims=True) for d in (d_one, d_two)]
        turned = [jnp.zeros_like(sums[0])] * 2
        for k in range(N_SHARD):
            at = slice(k * rows, (k + 1) * rows)
            if k:
                sent_refs[k - 1][:, cols] = scaled[at].astype(bf16)
            normed = n_refs[k][:, cols].astype(f32)
            turned = [
                t + jnp.sum(d[at] * normed, axis=0, keepdims=True)
                for t, d in zip(turned, (d_one, d_two))
            ]
        sum_ref[0:1, cols] = turned[0]
        sum_ref[1:2, cols] = sums[0]
        sum_ref[2:3, cols] = turned[1]
        sum_ref[3:4, cols] = sums[1]


def middle_body(s_ref, mix_ref, act_ref, whole_ref, last_ref, x_ref, dy_ref, slope_ref, *refs):
    down_refs, refs = refs[:N_REP], refs[N_REP:]
    own_ref, sent_refs = refs[0], refs[1:N_SHARD]
    rows = x_ref.shape[0]
    total = plain_dot(mix_ref[...], whole_ref[...])
    for i in range(0, N_REP, 2):
        weights = jnp.concatenate([down_refs[i][...], down_refs[i + 1][...]], axis=0)
        total = total + plain_dot(act_ref[:, i * LANES : (i + 2) * LANES], weights)
    own_ref[...] = x_ref[...] + total[:rows] + last_ref[0:1, :]
    for k in range(1, N_SHARD):
        sent_refs[k - 1][...] = total[k * rows : (k + 1) * rows].astype(bf16)
    hidden_body(s_ref, dy_ref, *down_refs, slope_ref, whole_ref, *refs[N_SHARD:])


def terms_body(
    s_ref, h_ref, dqkv_ref, mix_ref, dy_ref, norm_ref, qkv_sum_ref, up_sum_ref, cot_ref, keep_ref, sent_ref, vec_ref, g_ref
):
    half = keep_ref.shape[0]
    keep_ref[:, :QKV] = contract_rows(h_ref[:, :half], dqkv_ref[...])
    sent_ref[:, :QKV] = contract_rows(h_ref[:, half:], dqkv_ref[...]).astype(bf16)
    g_ref[...] = contract_rows(mix_ref[...], dy_ref[...])
    vec_ref[...] = jnp.zeros_like(vec_ref)
    vec_ref[0:4, :] = norm_ref[0:4, :]
    for row, block, at in bias_places(s_ref):
        ref, at = (qkv_sum_ref, at) if at < QKV else (up_sum_ref, at - QKV)
        vec_ref[row : row + 1, lane_block(block)] = ref[0:1, at : at + LANES]
    rows = OUT // N_REP
    for i in range(N_REP):
        here = slice(i * LANES, (i + 1) * LANES)
        cot = cot_ref[0:1, lane_block(s_ref[ORDER + i])]
        vec_ref[7:8, here] = cot
        vec_ref[12:13, here] = cot
        ref = keep_ref if i < N_REP // 2 else sent_ref
        base = i * LANES % half
        found = g_ref[row_block(s_ref[ORDER + i], rows), :]
        for c in range(D // OUT):
            ref[base + c * rows : base + (c + 1) * rows, QKV : QKV + OUT] = found[
                :, c * OUT : (c + 1) * OUT
            ].astype(ref.dtype)
        ref[base : base + LANES, QKV + OUT :] = vec_ref[:, here].T.astype(ref.dtype)


def mlp_body(s_ref, act_ref, dy_ref, h_ref, du_ref, keep_ref, sent_ref):
    half = keep_ref.shape[0]
    for left, right, at in ((act_ref, dy_ref, 0), (h_ref, du_ref, D)):
        cols = slice(at, at + right.shape[1])
        sent_ref[:, cols] = contract_rows(left[:, half:], right[...]).astype(bf16)
        keep_ref[:, cols] = contract_rows(left[:, :half], right[...])


def fold_body(s_ref, *refs):
    up_refs, refs = refs[:4], refs[4:]
    qkv_refs, refs = refs[:4], refs[4:]
    own_ref, sent_refs, out_ref, up_sum, qkv_sum = refs[0], refs[1:4], refs[4], refs[5], refs[6]
    for some, total, first in ((up_refs, up_sum, D), (qkv_refs, qkv_sum, 0)):
        total[...] = sum(ref[:, first:].astype(f32) for ref in some)
    rows = own_ref.shape[0]
    for k in range(N_SHARD):
        at = row_block(s_ref[NEAR + k], rows)
        ref = own_ref if k == 0 else sent_refs[k - 1]
        ref[:, :QKV] = qkv_sum[at, :QKV].astype(ref.dtype)
        ref[:, QKV : QKV + UP] = up_sum[at, :].astype(ref.dtype)
        ref[:, QKV + UP :] = qkv_sum[at, QKV + OUT :].astype(ref.dtype)
    for c in range(D // OUT):
        out_ref[:, c * OUT : (c + 1) * OUT] = qkv_sum[c * rows : (c + 1) * rows, QKV : QKV + OUT]


def adam_body(s_ref, *refs):
    got, refs = refs[:N_SHARD], refs[N_SHARD:]
    states, vec_state, refs = (refs[0:3], refs[3:6]), refs[6:9], refs[9:]
    results, vec_result, refs = (refs[0:4], refs[4:8]), refs[8:12], refs[12:]
    all_ref, turn_ref = refs
    for k in range(N_SHARD):
        all_ref[k] = got[k][...].astype(f32)
    count, cols = vec_state[0].shape
    turn_ref[...] = jnp.zeros_like(turn_ref)
    turn_ref[:cols, :] = sum(all_ref[k, :, QKV + UP :] for k in range(N_SHARD))
    turn_ref[...] = turn_ref[...].T
    grad = turn_ref[:count, :cols]
    vec_result[0][...] = grad
    new = adam_update(vec_state[0][...], grad, vec_state[1][...], vec_state[2][...], LR_VECTOR, 0.0)
    for ref, value in zip(vec_result[1:], new):
        ref[...] = value
    first = 0
    for state, result in zip(states, results):
        for c in range(state[0].shape[1] // (N_SHARD * LANES)):
            for t in range(N_SHARD):
                grad = all_ref[s_ref[NEAR + t], :, first : first + LANES]
                at = slice((c * N_SHARD + t) * LANES, (c * N_SHARD + t + 1) * LANES)
                result[0][:, at] = grad
                new = adam_update(
                    state[0][:, at], grad, state[1][:, at], state[2][:, at], LR_MATRIX, WEIGHT_DECAY
                )
                for ref, value in zip(result[1:], new):
                    ref[:, at] = value
            first += LANES


def finish_body(s_ref, own_ref, r1_ref, r2_ref, r3_ref, x_ref, cot_ref, o_ref, e_ref):
    total = own_ref[...] + r1_ref[...].astype(f32) + r2_ref[...].astype(f32) + r3_ref[...].astype(f32)
    for i in range(N_REP):
        e_ref[:, lane_block(s_ref[ORDER + i])] = total[:, i * LANES : (i + 1) * LANES]
    x = x_ref[...]
    center = x - jnp.mean(x, axis=-1, keepdims=True)
    inv_std = lax.rsqrt(jnp.mean(center * center, axis=-1, keepdims=True) + LN_EPS)
    normed = center * inv_std
    scaled = e_ref[...]
    o_ref[...] = cot_ref[...] + inv_std * (
        scaled
        - jnp.mean(scaled, axis=-1, keepdims=True)
        - normed * jnp.mean(scaled * normed, axis=-1, keepdims=True)
    )


def to_shards(values):
    return [hop(values[k - 1], "shard", N_SHARD, k) for k in range(1, N_SHARD)]


def to_chips(values):
    return [hop(values[k - 1], "rep", N_REP, 2 * k) for k in range(1, 4)]


def gather_chips(own):
    near = [own] + to_chips([own] * 3)
    return near + [hop(piece, "rep", N_REP, 1) for piece in near]


def sum_rep(keep, got, *earlier):
    parts = [keep[k] + got[k].astype(f32) for k in range(4)]
    sent = [part.astype(bf16) for part in parts[1:]]
    if earlier:
        sent = [after(part, *earlier) for part in sent]
    return [parts[0]] + to_chips(sent)


def after(value, *others):
    return lax.optimization_barrier((value,) + others)[0]


def shards(
    block_in,
    cotangent,
    segments,
    qkv_weight,
    out_weight,
    up_weight,
    down_weight,
    vectors,
    first_qkv,
    first_out,
    first_up,
    first_down,
    first_vec,
    second_qkv,
    second_out,
    second_up,
    second_down,
    second_vec,
):
    tok_count = block_in.shape[0]
    rep = lax.axis_index("rep")
    shard = lax.axis_index("shard")
    seq_len = tok_count * N_SHARD
    rows = qkv_weight.shape[0]
    units = down_weight.shape[0]
    n_vec, cols = vectors.shape
    masks = np.array([0, 2, 4, 6, 1, 3, 5, 7], np.int32)
    spots = np.argsort(masks)
    device = np.arange(N_REP)
    places = spots[device[:, None] ^ device[None, :]].astype(np.int32)
    orders = (device[:, None] ^ masks[None, :]).astype(np.int32)
    near = shard ^ jnp.arange(N_SHARD, dtype=jnp.int32)
    table = jnp.asarray(np.concatenate([orders, places], axis=1))
    scalars = jnp.concatenate(
        [lax.dynamic_index_in_dim(table, rep, 0, keepdims=False), near, shard[None]]
    ).astype(jnp.int32)

    share = HEAD // rows
    pair = LANES // HEAD
    moves = []
    for at in range(N_REP * N_SHARD):
        head, part = at // share, at % share
        owner = (head // pair) % N_SHARD
        local = (head // (pair * N_SHARD)) * pair + head % pair
        moves.append((at, (local * share + part) * N_SHARD + owner))

    own_cols = [((rows, QKV + UP + LANES), bf16)] * N_SHARD
    square = pltpu.VMEM((LANES, LANES), f32)
    packed = single(
        pack_body, own_cols, scalars, [qkv_weight, up_weight, vectors], 1, "pack", [square]
    )
    got_cols = to_shards(packed[1:])
    out_rows = lax.ppermute(out_weight.astype(bf16), ("rep", "shard"), moves)
    down_own = down_weight.astype(bf16)
    (normed_own,) = single(
        norm_body,
        [((tok_count, D), bf16)],
        scalars,
        [block_in],
        1,
        "norm",
        [pltpu.VMEM((tok_count, D), f32)],
    )
    (in_rows,) = single(
        join_body,
        [((N_SHARD * rows, QKV + UP + OUT + LANES), bf16)],
        scalars,
        [packed[0], *got_cols[:2], after(got_cols[2], normed_own), out_rows],
        1,
        "join",
    )
    normed = [normed_own] + to_shards([after(normed_own, *got_cols)] * 3)
    pieces = [in_rows] + to_chips([in_rows, in_rows, after(in_rows, normed[1])])
    pieces = pieces + [hop(after(piece, normed[2], normed[3]), "rep", N_REP, 1) for piece in pieces]
    downs = [down_own] + to_chips([after(down_own, *pieces[1:4])] * 3)
    dy_own = cotangent.astype(bf16)

    rope_parts = jnp.asarray(rope_lanes(seq_len)).reshape(N_SHARD, tok_count, 3 * LANES)
    rope = jnp.concatenate(
        [lax.dynamic_index_in_dim(rope_parts, near[k], 0, keepdims=False) for k in range(N_SHARD)]
    )
    seg_row = jnp.concatenate(
        [lax.dynamic_slice(segments[0], (near[k] * tok_count,), (tok_count,)) for k in range(N_SHARD)]
    )
    positions = (near[:, None] * tok_count + jnp.arange(tok_count)[None, :]).reshape(seq_len)
    allowed = (seg_row[:, None] == seg_row[None, :]) & (positions[None, :] <= positions[:, None])
    mask = jnp.where(allowed, 0.0, HIDDEN).astype(f32)

    out_whole, h_one, h_two, qkv16, act16, slope, vec_rel, last = front(
        scalars, normed, pieces, rope
    )
    block16 = ((tok_count, D), bf16)
    block32 = ((tok_count, D), f32)
    half = D // 2
    downs = downs + [hop(after(piece, qkv16), "rep", N_REP, 1) for piece in downs]
    dys = to_shards([after(dy_own, *pieces[4:])] * 3)
    dy_all = jnp.concatenate([after(dy_own, qkv16)] + dys, axis=0)
    mixed16 = mix_heads(qkv16, mask)
    out_own, s1, s2, s3, dy_seq, d_mixed16, d_up16, up_sum = single(
        middle_body,
        [
            block32,
            block16,
            block16,
            block16,
            ((seq_len, D), bf16),
            ((seq_len, OUT), bf16),
            ((seq_len, UP), bf16),
            ((8, UP), f32),
        ],
        scalars,
        [mixed16, act16, out_whole, last, block_in, dy_all, slope, *downs],
        2,
        "middle",
    )
    out_got = [hop(s1, "shard", N_SHARD, 1), hop(s2, "shard", N_SHARD, 2)]

    mlp_keep, mlp_sent = single(
        mlp_body,
        [((half, D + UP), f32), ((half, D + UP), bf16)],
        scalars,
        [act16, dy_seq, h_two, d_up16],
        1,
        "mlp",
    )
    mlp_got = hop(mlp_sent.reshape(4, LANES, D + UP), "rep", N_REP, 1)
    mlp_parts = sum_rep(mlp_keep.reshape(4, LANES, D + UP), mlp_got)
    d_mixed16 = after(d_mixed16, mlp_got)
    d_qkv16, qkv_sum = attend_back(qkv16, d_mixed16, mixed16, mask, rope)
    out_got.append(hop(after(s3, d_qkv16), "shard", N_SHARD, 3))
    d_qkv16 = after(d_qkv16, *out_got[:2])
    h_one = after(h_one, out_got[2], *mlp_parts[1:])

    e_own, *e_sent, norm_sum = single(
        back_body,
        [block32, block16, block16, block16, ((8, D), f32)],
        scalars,
        [d_qkv16, d_up16, vec_rel, *normed, *pieces],
        1,
        "back",
    )
    cot_sum = jnp.sum(cotangent, axis=0, keepdims=True)
    wide = QKV + OUT + LANES
    qkv_keep, qkv_sent = single(
        terms_body,
        [((half, wide), f32), ((half, wide), bf16)],
        scalars,
        [h_one, d_qkv16, mixed16, dy_seq, norm_sum, qkv_sum, up_sum, cot_sum],
        4,
        "terms",
        [pltpu.VMEM((LANES, D), f32), pltpu.VMEM((OUT, D), f32)],
    )
    qkv_got = hop(qkv_sent.reshape(4, LANES, wide), "rep", N_REP, 1)
    qkv_parts = sum_rep(qkv_keep.reshape(4, LANES, wide), qkv_got, *mlp_parts[1:])
    e_got = [hop(e_sent[0], "shard", N_SHARD, 1), hop(e_sent[1], "shard", N_SHARD, 2)]
    e_got.append(hop(after(e_sent[2], qkv_parts[1]), "shard", N_SHARD, 3))
    narrow = (rows, QKV + UP + LANES)
    g_own, g1, g2, g3, out_sum = single(
        fold_body,
        [(narrow, f32), (narrow, bf16), (narrow, bf16), (narrow, bf16), ((rows, D), f32)],
        scalars,
        [*mlp_parts, after(qkv_parts[0], *e_got[:2]), *qkv_parts[1:]],
        1,
        "fold",
        [pltpu.VMEM((LANES, UP), f32), pltpu.VMEM((LANES, wide), f32)],
    )
    g_got = to_shards([g1, g2, g3])
    grad_out = lax.ppermute(out_sum, ("rep", "shard"), [(b, a) for a, b in moves])
    block_out = out_own + out_got[0].astype(f32) + out_got[1].astype(f32) + out_got[2].astype(f32)
    grad_down = sum(part[:, :D].astype(f32) for part in mlp_parts)
    (grad_input,) = single(
        finish_body,
        [block32],
        scalars,
        [e_own, *e_got, block_in, cotangent],
        2,
        "finish",
        [pltpu.VMEM((tok_count, D), f32)],
    )
    qkv_shape = (qkv_weight.shape, f32)
    up_shape = (up_weight.shape, f32)
    vec_shape = (vectors.shape, f32)
    (
        grad_qkv,
        new_qkv,
        new_first_qkv,
        new_second_qkv,
        grad_up,
        new_up,
        new_first_up,
        new_second_up,
        grad_vec,
        new_vec,
        new_first_vec,
        new_second_vec,
    ) = single(
        adam_body,
        [qkv_shape] * 4 + [up_shape] * 4 + [vec_shape] * 4,
        scalars,
        [
            after(g_own, e_got[2]),
            *g_got,
            qkv_weight,
            first_qkv,
            second_qkv,
            up_weight,
            first_up,
            second_up,
            vectors,
            first_vec,
            second_vec,
        ],
        3,
        "adam",
        [pltpu.VMEM((N_SHARD,) + narrow, f32), square],
    )

    new_out, new_first_out, new_second_out = adam_update(
        out_weight, grad_out, first_out, second_out, LR_MATRIX, WEIGHT_DECAY
    )
    new_down, new_first_down, new_second_down = adam_update(
        down_weight, grad_down, first_down, second_down, LR_MATRIX, WEIGHT_DECAY
    )
    return (
        block_out,
        grad_input,
        grad_qkv,
        grad_out,
        grad_up,
        grad_down,
        grad_vec,
        new_qkv,
        new_out,
        new_up,
        new_down,
        new_vec,
        new_first_qkv,
        new_first_out,
        new_first_up,
        new_first_down,
        new_first_vec,
        new_second_qkv,
        new_second_out,
        new_second_up,
        new_second_down,
        new_second_vec,
    )


def solution(mesh):
    aligned = mesh.shape["rep"] == N_REP and mesh.shape["shard"] == N_SHARD
    return jax.shard_map(
        shards if aligned else general,
        mesh=mesh,
        in_specs=(
            P(("rep", "shard"), None),
            P(("rep", "shard"), None),
            P("rep", None),
            P(("rep", "shard"), None),
            P(("rep", "shard"), None),
            P(("rep", "shard"), None),
            P(("rep", "shard"), None),
            P(None, ("rep", "shard")),
            P(("rep", "shard"), None),
            P(("rep", "shard"), None),
            P(("rep", "shard"), None),
            P(("rep", "shard"), None),
            P(None, ("rep", "shard")),
            P(("rep", "shard"), None),
            P(("rep", "shard"), None),
            P(("rep", "shard"), None),
            P(("rep", "shard"), None),
            P(None, ("rep", "shard")),
        ),
        out_specs=(
            P(("rep", "shard"), None),
            P(("rep", "shard"), None),
            P(("rep", "shard"), None),
            P(("rep", "shard"), None),
            P(("rep", "shard"), None),
            P(("rep", "shard"), None),
            P(None, ("rep", "shard")),
            P(("rep", "shard"), None),
            P(("rep", "shard"), None),
            P(("rep", "shard"), None),
            P(("rep", "shard"), None),
            P(None, ("rep", "shard")),
            P(("rep", "shard"), None),
            P(("rep", "shard"), None),
            P(("rep", "shard"), None),
            P(("rep", "shard"), None),
            P(None, ("rep", "shard")),
            P(("rep", "shard"), None),
            P(("rep", "shard"), None),
            P(("rep", "shard"), None),
            P(("rep", "shard"), None),
            P(None, ("rep", "shard")),
        ),
        check_vma=False,
    )
```

```python
import jax
import jax.numpy as jnp
import numpy as np
from jax import lax
from jax.experimental import pallas as pl
from jax.experimental.pallas import tpu as pltpu
from jax.sharding import PartitionSpec as P

D = 1024
HEADS = 16
HEAD = D // HEADS
FF = 4096
ROT = 16
STEP = 10
LANES = 128


LN_EPS = 1e-05
BETA_ONE = 0.9
BETA_TWO = 0.95
ADAM_EPS = 1e-08
LR_MATRIX = 0.03
LR_VECTOR = 0.2
WEIGHT_DECAY = 0.01
ROPE_BASE = 10000.0
INV_ROOT_TWO = 0.7071067811865476
INV_ROOT_TAU = 0.3989422804014327
HIDDEN = -1e30
bf16 = jnp.bfloat16
f32 = jnp.float32
TILE = 256


def adam_update(param, grad, first, second, rate, decay):
    first_new = BETA_ONE * first + (1.0 - BETA_ONE) * grad
    second_new = BETA_TWO * second + (1.0 - BETA_TWO) * grad * grad
    first_hat = first_new / (1.0 - BETA_ONE**STEP)
    second_hat = second_new / (1.0 - BETA_TWO**STEP)
    return (
        param - rate * (first_hat / (jnp.sqrt(second_hat) + ADAM_EPS) + decay * param),
        first_new,
        second_new,
    )


def contract_rows(left, right):
    return lax.dot_general(left, right, (((0,), (0,)), ((), ())), preferred_element_type=f32)


def contract_cols(left, right):
    return lax.dot_general(left, right, (((1,), (1,)), ((), ())), preferred_element_type=f32)


def plain_dot(left, right):
    return jnp.dot(left, right, preferred_element_type=f32)


def rope_lanes(seq_len):
    half = ROT // 2
    freqs = (ROPE_BASE ** (-(2.0 * np.arange(half, dtype=np.float32) / ROT))).astype(np.float32)
    angles = np.arange(seq_len, dtype=np.float32)[:, None] * freqs[None, :]
    cosines, sines = np.cos(angles), np.sin(angles)
    keep = np.ones((seq_len, HEAD), np.float32)
    up = np.zeros((seq_len, HEAD), np.float32)
    down = np.zeros((seq_len, HEAD), np.float32)
    keep[:, :half], keep[:, half:ROT] = cosines, cosines
    up[:, :half] = -sines
    down[:, half:ROT] = sines
    reps = LANES // HEAD
    return np.concatenate([np.tile(t, (1, reps)) for t in (keep, up, down)], axis=1)


def turn(values, table, sign):
    half = ROT // 2
    above = pltpu.roll(values, LANES - half, 1)
    below = pltpu.roll(values, half, 1)
    moved = above * table[:, LANES : 2 * LANES] + below * table[:, 2 * LANES :]
    return values * table[:, :LANES] + sign * moved


def params(mib):
    return pltpu.CompilerParams(vmem_limit_bytes=mib << 20)


def cost(micros):
    return pl.CostEstimate(flops=int(micros * 1.15e9), bytes_accessed=1 << 20, transcendentals=0)


def whole_spec(shape):
    return pl.BlockSpec(shape, lambda *_: (0,) * len(shape))


def rope_tables(positions):
    half_rot = ROT // 2
    freqs = ROPE_BASE ** (-(2.0 * jnp.arange(half_rot).astype(jnp.float32) / ROT))
    angles = positions.astype(jnp.float32)[:, None] * freqs[None, :]
    return (jnp.cos(angles)[:, None, :], jnp.sin(angles)[:, None, :])


def rotate(heads, cosines, sines):
    half_rot = ROT // 2
    lower = heads[..., :half_rot]
    upper = heads[..., half_rot:ROT]
    return jnp.concatenate(
        [lower * cosines - upper * sines, upper * cosines + lower * sines, heads[..., ROT:]],
        axis=-1,
    )


def unrotate(heads, cosines, sines):
    half_rot = ROT // 2
    lower = heads[..., :half_rot]
    upper = heads[..., half_rot:ROT]
    return jnp.concatenate(
        [lower * cosines + upper * sines, upper * cosines - lower * sines, heads[..., ROT:]],
        axis=-1,
    )


def gelu_value(inner):
    return 0.5 * inner * (1.0 + jax.scipy.special.erf(inner * INV_ROOT_TWO))


def gelu_slope(inner):
    return (
        0.5 * (1.0 + jax.scipy.special.erf(inner * INV_ROOT_TWO))
        + inner * jnp.exp(-0.5 * inner * inner) * INV_ROOT_TAU
    )


def hop(value, axis, size, mask):
    return lax.ppermute(value, axis, [(i, i ^ mask) for i in range(size)])


def pick(blocks, index, axis=0):
    return lax.dynamic_index_in_dim(blocks, index, axis, keepdims=False)


def stages(size):
    bits = size.bit_length() - 1
    found = []
    while bits > 0:
        take = 2 if bits >= 2 else 1
        bits -= take
        found.append((bits, 1 << take))
    return found


def gather_axis(own, axis, me, size):
    if size > 16:
        return lax.all_gather(own, axis)
    pieces = {0: own}
    for shift, count in stages(size):
        more = dict(pieces)
        for k in range(1, count):
            for mask, piece in pieces.items():
                more[mask ^ (k << shift)] = hop(piece, axis, size, k << shift)
        pieces = more
    whole = jnp.zeros((size,) + own.shape, own.dtype)
    for mask in range(size):
        whole = lax.dynamic_update_index_in_dim(whole, pieces[mask], me ^ mask, 0)
    return whole


def exchange_axis(blocks, axis, me, size, wire):
    got = [(0, pick(blocks, me))]
    for mask in range(1, size):
        got.append((mask, hop(pick(blocks, me ^ mask).astype(wire), axis, size, mask)))
    return got


def reduce_axis(blocks, axis, me, size, wire):
    current = blocks
    for shift, count in reversed(stages(size)):
        left = current.shape[0] // count
        view = current.reshape((left, count) + current.shape[1:])
        digit = (me >> shift) & (count - 1)
        total = pick(view, digit, 1)
        for k in range(1, count):
            sent = pick(view, digit ^ k, 1).astype(wire)
            total = total + hop(sent, axis, size, k << shift).astype(jnp.float32)
        current = total
    return current[0]


def general(
    block_in,
    cotangent,
    segments,
    qkv_weight,
    out_weight,
    up_weight,
    down_weight,
    vectors,
    first_qkv,
    first_out,
    first_up,
    first_down,
    first_vec,
    second_qkv,
    second_out,
    second_up,
    second_down,
    second_vec,
):
    tok_count = block_in.shape[0]
    n_rep = lax.axis_size("rep")
    n_shard = lax.axis_size("shard")
    rep = lax.axis_index("rep")
    shard = lax.axis_index("shard")
    seq_len = tok_count * n_shard
    head_dim = D // HEADS
    own_heads = HEADS // n_shard
    own_feats = own_heads * head_dim
    rows = qkv_weight.shape[0]
    units = down_weight.shape[0]
    own_units = units * n_rep
    cols = vectors.shape[1]
    score_scale = head_dim ** (-0.5)

    qkv_cols = qkv_weight.astype(bf16).reshape(rows, 3, own_heads, n_shard, head_dim)
    qkv_cols = qkv_cols.transpose(3, 0, 1, 2, 4).reshape(n_shard, rows, 3 * own_feats)
    up_cols = up_weight.astype(bf16).reshape(rows, n_rep, n_shard, units)
    up_cols = up_cols.transpose(2, 0, 1, 3).reshape(n_shard, rows, own_units)
    in_cols = jnp.concatenate([qkv_cols, up_cols], axis=2)
    in_rows = jnp.zeros_like(in_cols)
    for mask, piece in exchange_axis(in_cols, "shard", shard, n_shard, bf16):
        in_rows = lax.dynamic_update_index_in_dim(in_rows, piece, shard ^ mask, 0)
    in_rows = in_rows.reshape(n_shard * rows, 3 * own_feats + own_units)

    center = block_in - jnp.mean(block_in, axis=-1, keepdims=True)
    inv_std = lax.rsqrt(jnp.mean(center * center, axis=-1, keepdims=True) + LN_EPS)
    normed = center * inv_std
    normed_seq = gather_axis(normed.astype(bf16), "shard", shard, n_shard).reshape(seq_len, D)
    normed_seq = normed_seq.astype(f32)

    vec_some = gather_axis(vectors, "shard", shard, n_shard)
    vec_all = gather_axis(vec_some, "rep", rep, n_rep)
    vec_all = vec_all.transpose(2, 0, 1, 3).reshape(vectors.shape[0], D)

    in_whole = gather_axis(in_rows, "rep", rep, n_rep).reshape(D, 3 * own_feats + own_units)
    upstream16 = gather_axis(cotangent.astype(bf16), "shard", shard, n_shard).reshape(seq_len, D)
    down_whole = gather_axis(down_weight.astype(bf16), "rep", rep, n_rep).reshape(own_units, D)
    share = head_dim // rows
    moves = []
    for device in range(n_rep * n_shard):
        head, part = device // share, device % share
        moves.append((device, ((head // n_shard) * share + part) * n_shard + head % n_shard))
    out_rows = lax.ppermute(out_weight.astype(bf16), ("rep", "shard"), moves)
    out_whole = gather_axis(out_rows, "rep", rep, n_rep).reshape(own_feats, D)

    per_row = FF // D
    gain_one, shift_one, gain_two, shift_two = (vec_all[0], vec_all[1], vec_all[2], vec_all[3])
    qkv_bias = pick(vec_all[4:7].reshape(3, own_heads, n_shard, head_dim), shard, 2).reshape(
        3 * own_feats
    )
    up_bias = pick(vec_all[8 : 8 + per_row].reshape(n_rep, n_shard, units), shard, 1).reshape(
        own_units
    )
    out_bias = vec_all[7]
    down_bias = vec_all[8 + per_row]

    h_one = (normed_seq * gain_one + shift_one).astype(bf16)
    h_two = (normed_seq * gain_two + shift_two).astype(bf16)
    qkv_whole = in_whole[:, : 3 * own_feats]
    up_whole = in_whole[:, 3 * own_feats :]
    qkv_lin = jnp.dot(h_one, qkv_whole, preferred_element_type=f32) + qkv_bias
    up_lin = jnp.dot(h_two, up_whole, preferred_element_type=f32) + up_bias

    positions = jnp.arange(seq_len)
    cosines, sines = rope_tables(positions)

    def heads_of(values):
        return values.reshape(seq_len, own_heads, head_dim)

    query16 = rotate(heads_of(qkv_lin[:, :own_feats]), cosines, sines).astype(bf16)
    key16 = rotate(heads_of(qkv_lin[:, own_feats : 2 * own_feats]), cosines, sines).astype(bf16)
    value16 = heads_of(qkv_lin[:, 2 * own_feats :]).astype(bf16)
    seg_row = segments[0]
    allowed = (seg_row[:, None] == seg_row[None, :]) & (positions[None, :] <= positions[:, None])
    scores = jnp.where(
        allowed[None],
        jnp.einsum("qhd,khd->hqk", query16, key16, preferred_element_type=f32) * score_scale,
        -jnp.inf,
    )
    row_max = jnp.max(scores, axis=-1, keepdims=True)
    expo = jnp.exp(scores - row_max)
    row_sum = jnp.sum(expo, axis=-1, keepdims=True)
    log_total = row_max + jnp.log(row_sum)
    probs16 = (expo / row_sum).astype(bf16)
    mixed16 = (
        jnp.einsum("hqk,khd->qhd", probs16, value16, preferred_element_type=f32)
        .reshape(seq_len, own_feats)
        .astype(bf16)
    )
    act16 = gelu_value(up_lin).astype(bf16)
    branches = jnp.dot(mixed16, out_whole, preferred_element_type=f32)
    branches = branches + jnp.dot(act16, down_whole, preferred_element_type=f32)
    branches = reduce_axis(
        branches.reshape(n_shard, tok_count, D), "shard", shard, n_shard, bf16
    )
    block_out = block_in + branches + out_bias + down_bias

    term_down = contract_rows(act16, upstream16)
    sum_down = reduce_axis(term_down.reshape(n_rep, units, D), "rep", rep, n_rep, bf16)
    term_out = contract_rows(mixed16, upstream16)
    sum_out = reduce_axis(term_out.reshape(n_rep, rows, D), "rep", rep, n_rep, bf16)
    grad_out = lax.ppermute(sum_out, ("rep", "shard"), [(b, a) for a, b in moves])
    grad_down = sum_down
    d_act = contract_cols(upstream16, down_whole)
    d_mixed16 = heads_of(contract_cols(upstream16, out_whole)).astype(bf16)
    d_up = d_act * gelu_slope(up_lin)
    d_up16 = d_up.astype(bf16)
    term_up = contract_rows(h_two, d_up16)
    sum_up = reduce_axis(
        term_up.reshape(n_rep, n_shard * rows, own_units), "rep", rep, n_rep, bf16
    )

    def back_rows(sums, width):
        whole = jnp.zeros((n_shard, rows, width), f32)
        blocks = sums.reshape(n_shard, rows, width)
        for mask, piece in exchange_axis(blocks, "shard", shard, n_shard, bf16):
            whole = lax.dynamic_update_index_in_dim(whole, piece.astype(f32), shard ^ mask, 0)
        return whole

    grad_up = back_rows(sum_up, own_units).reshape(n_shard, rows, n_rep, units)
    grad_up = grad_up.transpose(1, 2, 0, 3).reshape(rows, FF)

    row_delta = jnp.sum(
        d_mixed16.astype(f32) * heads_of(mixed16).astype(f32),
        axis=-1,
    ).T[:, :, None]
    probs_again = jnp.exp(scores - log_total)
    d_probs = jnp.einsum("qhd,khd->hqk", d_mixed16, value16, preferred_element_type=f32)
    d_scores16 = (probs_again * (d_probs - row_delta) * score_scale).astype(bf16)
    probs_back16 = probs_again.astype(bf16)
    d_query = jnp.einsum("hqk,khd->qhd", d_scores16, key16, preferred_element_type=f32)
    d_keys = jnp.einsum("hqk,qhd->khd", d_scores16, query16, preferred_element_type=f32)
    d_values = jnp.einsum("hqk,qhd->khd", probs_back16, d_mixed16, preferred_element_type=f32)
    d_qkv = jnp.concatenate(
        [
            unrotate(d_query, cosines, sines).reshape(seq_len, own_feats),
            unrotate(d_keys, cosines, sines).reshape(seq_len, own_feats),
            d_values.reshape(seq_len, own_feats),
        ],
        axis=1,
    )
    d_qkv16 = d_qkv.astype(bf16)
    term_qkv = contract_rows(h_one, d_qkv16)
    sum_qkv = reduce_axis(
        term_qkv.reshape(n_rep, n_shard * rows, 3 * own_feats), "rep", rep, n_rep, bf16
    )
    grad_qkv = back_rows(sum_qkv, 3 * own_feats)
    grad_qkv = grad_qkv.reshape(n_shard, rows, 3, own_heads, head_dim)
    grad_qkv = grad_qkv.transpose(1, 2, 3, 0, 4).reshape(rows, 3 * D)

    d_one = contract_cols(d_qkv16, qkv_whole)
    d_two = contract_cols(d_up16, up_whole)
    scaled = d_one * gain_one + d_two * gain_two
    scaled = reduce_axis(scaled.reshape(n_shard, tok_count, D), "shard", shard, n_shard, bf16)
    grad_input = cotangent + inv_std * (
        scaled
        - jnp.mean(scaled, axis=-1, keepdims=True)
        - normed * jnp.mean(scaled * normed, axis=-1, keepdims=True)
    )

    mine = jnp.arange(n_shard) == shard
    cot_sum = jnp.sum(cotangent, axis=0)
    bias_qkv = jnp.where(
        mine[None, None, :, None],
        jnp.sum(d_qkv, axis=0).reshape(3, own_heads, 1, head_dim),
        0.0,
    ).reshape(3, D)
    bias_up = jnp.where(
        mine[None, :, None], jnp.sum(d_up, axis=0).reshape(n_rep, 1, units), 0.0
    ).reshape(per_row, D)
    vec_terms = jnp.concatenate(
        [
            jnp.sum(d_one * normed_seq, axis=0)[None],
            jnp.sum(d_one, axis=0)[None],
            jnp.sum(d_two * normed_seq, axis=0)[None],
            jnp.sum(d_two, axis=0)[None],
            bias_qkv,
            cot_sum[None],
            bias_up,
            cot_sum[None],
        ],
        axis=0,
    )
    vec_blocks = vec_terms.reshape(vectors.shape[0], n_rep, n_shard, cols).transpose(1, 2, 0, 3)
    grad_vec = reduce_axis(
        reduce_axis(vec_blocks, "rep", rep, n_rep, f32), "shard", shard, n_shard, f32
    )

    new_qkv, new_first_qkv, new_second_qkv = adam_update(
        qkv_weight, grad_qkv, first_qkv, second_qkv, LR_MATRIX, WEIGHT_DECAY
    )
    new_out, new_first_out, new_second_out = adam_update(
        out_weight, grad_out, first_out, second_out, LR_MATRIX, WEIGHT_DECAY
    )
    new_up, new_first_up, new_second_up = adam_update(
        up_weight, grad_up, first_up, second_up, LR_MATRIX, WEIGHT_DECAY
    )
    new_down, new_first_down, new_second_down = adam_update(
        down_weight, grad_down, first_down, second_down, LR_MATRIX, WEIGHT_DECAY
    )
    new_vec, new_first_vec, new_second_vec = adam_update(
        vectors, grad_vec, first_vec, second_vec, LR_VECTOR, 0.0
    )
    return (
        block_out,
        grad_input,
        grad_qkv,
        grad_out,
        grad_up,
        grad_down,
        grad_vec,
        new_qkv,
        new_out,
        new_up,
        new_down,
        new_vec,
        new_first_qkv,
        new_first_out,
        new_first_up,
        new_first_down,
        new_first_vec,
        new_second_qkv,
        new_second_out,
        new_second_up,
        new_second_down,
        new_second_vec,
    )


ROOM = {
    "pack": 6,
    "norm": 4,
    "join": 4,
    "middle": 30,
    "back": 28,
    "terms": 20,
    "mlp": 28,
    "fold": 16,
    "finish": 10,
    "adam": 22,
}


def single(body, outs, prefetch, ins, micros, name, scratch=()):
    shapes = tuple(jax.ShapeDtypeStruct(s, d) for s, d in outs)
    return pl.pallas_call(
        body,
        out_shape=shapes,
        grid_spec=pltpu.PrefetchScalarGridSpec(
            num_scalar_prefetch=1,
            grid=(1,),
            in_specs=[whole_spec(a.shape) for a in ins],
            out_specs=tuple(whole_spec(s.shape) for s in shapes),
            scratch_shapes=list(scratch),
        ),
        compiler_params=params(ROOM[name]),
        cost_estimate=cost(micros),
        name=name,
    )(prefetch, *ins)


def lane_block(index):
    return pl.ds(pl.multiple_of(index * LANES, LANES), LANES)


def row_block(index, size):
    return pl.ds(pl.multiple_of(index * size, size), size)


N_REP = 8
N_SHARD = 4
ORDER = 0
PLACE = N_REP
NEAR = 2 * N_REP
SHARD = NEAR + N_SHARD
QKV = 3 * TILE
UP = D
OUT = TILE


def pack_body(s_ref, qkv_ref, up_ref, vec_ref, *refs):
    outs, turn_ref = refs[:-1], refs[-1]
    count, cols = vec_ref.shape
    turn_ref[...] = jnp.zeros_like(turn_ref)
    vec = vec_ref[...]
    for i in range(3):
        part = vec.astype(bf16).astype(f32)
        turn_ref[16 * i : 16 * i + count, :cols] = part
        vec = vec - part
    vec16 = turn_ref[...].T[:cols, :].astype(bf16)
    for k in range(N_SHARD):
        t = s_ref[NEAR + k]
        o_ref = outs[k]
        for c in range(QKV // LANES):
            o_ref[:, c * LANES : (c + 1) * LANES] = qkv_ref[:, lane_block(c * N_SHARD + t)].astype(bf16)
        for c in range(UP // LANES):
            at = QKV + c * LANES
            o_ref[:, at : at + LANES] = up_ref[:, lane_block(c * N_SHARD + t)].astype(bf16)
        o_ref[:, QKV + UP :] = vec16


def norm_body(s_ref, x_ref, o_ref, n_ref):
    x = x_ref[...]
    center = x - jnp.mean(x, axis=-1, keepdims=True)
    inv_std = lax.rsqrt(jnp.mean(center * center, axis=-1, keepdims=True) + LN_EPS)
    n_ref[...] = center * inv_std
    for i in range(N_REP):
        o_ref[:, i * LANES : (i + 1) * LANES] = n_ref[:, lane_block(s_ref[ORDER + i])].astype(bf16)


def join_body(s_ref, *refs):
    out_ref, o_ref = refs[N_SHARD], refs[N_SHARD + 1]
    rows = out_ref.shape[0]
    for k in range(N_SHARD):
        at = row_block(s_ref[NEAR + k], rows)
        o_ref[at, : QKV + UP] = refs[k][:, : QKV + UP]
        o_ref[at, QKV + UP + OUT :] = refs[k][:, QKV + UP :]
    for c in range(D // OUT):
        o_ref[c * rows : (c + 1) * rows, QKV + UP : QKV + UP + OUT] = out_ref[:, c * OUT : (c + 1) * OUT]


def bias_places(s_ref):
    shard = s_ref[SHARD]
    found = []
    for c in range(QKV // LANES):
        found.append((4 + c // 2, s_ref[PLACE + (c % 2) * N_SHARD + shard], c * LANES))
    for c in range(UP // LANES):
        found.append((8 + c // 2, s_ref[PLACE + (c % 2) * N_SHARD + shard], QKV + c * LANES))
    return found


def front_body(s_ref, *refs):
    n_refs, refs = refs[:N_SHARD], refs[N_SHARD:]
    w_refs, refs = refs[:N_REP], refs[N_REP:]
    v_refs, refs = refs[:N_REP], refs[N_REP:]
    out_refs, refs = refs[:N_REP], refs[N_REP:]
    rope_ref, whole_ref, h1_ref, h2_ref, qkv_ref, act_ref, slope_ref, vec_ref, last_ref, bias_ref = refs
    j = pl.program_id(0)
    rows = n_refs[0].shape[0]

    @pl.when(j == 0)
    def _():
        for i in range(N_REP):
            parts = v_refs[i][...].astype(f32).T
            vec_ref[:, i * LANES : (i + 1) * LANES] = (parts[0:16] + parts[16:32]) + parts[32:48]
        for k in range(N_SHARD):
            normed = n_refs[k][...].astype(f32)
            at = slice(k * rows, (k + 1) * rows)
            h1_ref[at, :] = (normed * vec_ref[0:1, :] + vec_ref[1:2, :]).astype(bf16)
            h2_ref[at, :] = (normed * vec_ref[2:3, :] + vec_ref[3:4, :]).astype(bf16)
        for row, block, at in bias_places(s_ref):
            bias_ref[at // TILE, 0:1, at % TILE : at % TILE + LANES] = vec_ref[row : row + 1, lane_block(block)]
        both = vec_ref[7:8, :] + vec_ref[12:13, :]
        for i in range(N_REP):
            last_ref[0:1, lane_block(s_ref[ORDER + i])] = both[:, i * LANES : (i + 1) * LANES]
        chunks = D // OUT
        size = out_refs[0].shape[0] // chunks
        for i in range(N_REP):
            at = row_block(s_ref[ORDER + i], size)
            for c in range(chunks):
                whole_ref[at, c * OUT : (c + 1) * OUT] = out_refs[i][c * size : (c + 1) * size, :]

    def product(h_ref):
        total = bias_ref[j, 0:1, :]
        for i in range(0, N_REP, 2):
            weights = jnp.concatenate([w_refs[i][...], w_refs[i + 1][...]], axis=0)
            total = total + plain_dot(h_ref[:, i * LANES : (i + 2) * LANES], weights)
        return total

    @pl.when(j < 2)
    def _():
        lin = product(h1_ref)
        for c in range(0, TILE, LANES):
            qkv_ref[:, c : c + LANES] = turn(lin[:, c : c + LANES], rope_ref[...], 1.0).astype(bf16)

    @pl.when(j == 2)
    def _():
        qkv_ref[...] = product(h1_ref).astype(bf16)

    @pl.when(j > 2)
    def _():
        lin = product(h2_ref)
        above = 0.5 * (1.0 + lax.erf(lin * INV_ROOT_TWO))
        act = (lin * above).astype(bf16)
        slope = above + lin * jnp.exp(-0.5 * lin * lin) * INV_ROOT_TAU
        for c in range(2):
            at = lane_block(s_ref[PLACE + (j - 3) * 2 + c])
            act_ref[:, at] = act[:, c * LANES : (c + 1) * LANES]
            slope_ref[:, at] = slope[:, c * LANES : (c + 1) * LANES]


def front(scalars, normed, pieces, rope):
    tokens = rope.shape[0]
    block = pieces[0].shape[0]
    shapes = (
        ((OUT, D), bf16),
        ((tokens, D), bf16),
        ((tokens, D), bf16),
        ((tokens, QKV), bf16),
        ((tokens, UP), bf16),
        ((tokens, UP), f32),
        ((16, D), f32),
        ((8, D), f32),
    )
    specs = [whole_spec(s) for s, _ in shapes]
    specs[3] = pl.BlockSpec((tokens, TILE), lambda j, s: (0, jnp.minimum(j, 2)))
    return pl.pallas_call(
        front_body,
        out_shape=tuple(jax.ShapeDtypeStruct(s, d) for s, d in shapes),
        grid_spec=pltpu.PrefetchScalarGridSpec(
            num_scalar_prefetch=1,
            grid=((QKV + UP) // TILE,),
            in_specs=[whole_spec(n.shape) for n in normed]
            + [pl.BlockSpec((block, TILE), lambda j, s: (0, j))] * N_REP
            + [pl.BlockSpec((block, LANES), lambda j, s: (0, (QKV + UP + OUT) // LANES))] * N_REP
            + [pl.BlockSpec((block, OUT), lambda j, s: (0, (QKV + UP) // OUT))] * N_REP
            + [whole_spec(rope.shape)],
            out_specs=tuple(specs),
            scratch_shapes=[pltpu.VMEM(((QKV + UP) // TILE, 8, TILE), f32)],
        ),
        compiler_params=params(24),
        cost_estimate=cost(9),
        name="front",
    )(scalars, *normed, *pieces, *pieces, *pieces, rope)


def hidden_body(s_ref, *refs):
    dy_ref, refs = refs[0], refs[1:]
    down_refs, refs = refs[:N_REP], refs[N_REP:]
    slope_ref, whole_ref, seq_ref, dmix_ref, du_ref, sum_ref = refs
    tokens = dy_ref.shape[0] // N_SHARD
    for k in range(N_SHARD):
        seq_ref[k * tokens : (k + 1) * tokens, :] = dy_ref[k * tokens : (k + 1) * tokens, :]
    dy = seq_ref[...]
    dmix_ref[...] = contract_cols(dy, whole_ref[...]).astype(bf16)
    for i in range(N_REP):
        du = contract_cols(dy, down_refs[i][...]) * slope_ref[:, i * LANES : (i + 1) * LANES]
        at = lane_block(s_ref[ORDER + i])
        du_ref[:, at] = du.astype(bf16)
        sum_ref[0:1, at] = jnp.sum(du, axis=0, keepdims=True)


def weigh(q, k, mask):
    score = contract_cols(q, k) * (HEAD ** (-0.5)) + mask
    expo = jnp.exp(score - jnp.max(score, axis=-1, keepdims=True))
    return expo * (1.0 / jnp.sum(expo, axis=-1, keepdims=True))


def only(values, mine):
    return jnp.where(mine, values, jnp.zeros_like(values))


def mix_body(q_ref, k_ref, v_ref, mask_ref, mix_ref):
    first = lax.broadcasted_iota(jnp.int32, (LANES, LANES), 1) < HEAD
    k = k_ref[...]
    v = v_ref[...]
    for c in range(0, q_ref.shape[0], LANES):
        rows = slice(c, c + LANES)
        q = q_ref[rows, :]
        mixes = []
        for mine in (first, jnp.logical_not(first)):
            prob = weigh(only(q, mine), k, mask_ref[rows, :])
            mixes.append(plain_dot(prob.astype(bf16), v))
        mix_ref[rows, :] = jnp.where(first, mixes[0], mixes[1]).astype(bf16)


def attend_body(
    q_ref, k_ref, v_ref, dm_ref, mix_ref, mask_ref, rope_ref, dqkv_ref, sum_ref, dk_ref, dv_ref
):
    pair = pl.program_id(0)
    tokens = q_ref.shape[0]
    scale = HEAD ** (-0.5)
    first = lax.broadcasted_iota(jnp.int32, (LANES, LANES), 1) < HEAD
    every = lax.broadcasted_iota(jnp.int32, (tokens, LANES), 1) < HEAD
    k = k_ref[...]
    v = v_ref[...]
    pairs = pl.num_programs(0)

    def columns(part):
        return lane_block(part * pairs + pair)

    dq_total = jnp.zeros((1, LANES), f32)
    for c in range(0, tokens, LANES):
        rows = slice(c, c + LANES)
        q = q_ref[rows, :]
        dm = dm_ref[rows, :]
        mix = mix_ref[rows, :].astype(f32)
        dqs, dks, dvs = [], [], []
        for mine in (first, jnp.logical_not(first)):
            dmh = only(dm, mine)
            prob = weigh(only(q, mine), k, mask_ref[rows, :])
            delta = jnp.sum(dmh.astype(f32) * mix, axis=-1, keepdims=True)
            d_prob = contract_cols(dmh, v)
            ds16 = (prob * (d_prob - delta) * scale).astype(bf16)
            dqs.append(plain_dot(ds16, k))
            dks.append(contract_rows(ds16, q))
            dvs.append(contract_rows(prob.astype(bf16), dm))
        dq = turn(jnp.where(first, dqs[0], dqs[1]), rope_ref[rows, :], -1.0)
        dqkv_ref[rows, columns(0)] = dq.astype(bf16)
        dq_total = dq_total + jnp.sum(dq, axis=0, keepdims=True)
        dk = jnp.where(every, dks[0], dks[1])
        dv = jnp.where(every, dvs[0], dvs[1])
        if c == 0:
            dk_ref[...] = dk
            dv_ref[...] = dv
        else:
            dk_ref[...] += dk
            dv_ref[...] += dv
    dk = turn(dk_ref[...], rope_ref[...], -1.0)
    dv = dv_ref[...]
    dqkv_ref[:, columns(1)] = dk.astype(bf16)
    dqkv_ref[:, columns(2)] = dv.astype(bf16)
    sum_ref[:, columns(0)] = dq_total
    sum_ref[:, columns(1)] = jnp.sum(dk, axis=0, keepdims=True)
    sum_ref[:, columns(2)] = jnp.sum(dv, axis=0, keepdims=True)


def pair_spec(tokens, first):
    return pl.BlockSpec((tokens, LANES), lambda j: (0, first + j))


def mix_heads(qkv, mask):
    tokens = qkv.shape[0]
    pairs = OUT // LANES
    return pl.pallas_call(
        mix_body,
        out_shape=jax.ShapeDtypeStruct((tokens, OUT), bf16),
        grid=(pairs,),
        in_specs=[pair_spec(tokens, i * pairs) for i in range(3)] + [whole_spec(mask.shape)],
        out_specs=pair_spec(tokens, 0),
        compiler_params=params(10),
        cost_estimate=cost(6),
        name="mix_heads",
    )(qkv, qkv, qkv, mask)


def attend_back(qkv, d_mix, mixed, mask, rope):
    tokens = qkv.shape[0]
    pairs = OUT // LANES
    return pl.pallas_call(
        attend_body,
        out_shape=(
            jax.ShapeDtypeStruct((tokens, QKV), bf16),
            jax.ShapeDtypeStruct((1, QKV), f32),
        ),
        grid=(pairs,),
        in_specs=[pair_spec(tokens, i * pairs) for i in range(3)]
        + [pair_spec(tokens, 0), pair_spec(tokens, 0), whole_spec(mask.shape), whole_spec(rope.shape)],
        out_specs=(whole_spec((tokens, QKV)), whole_spec((1, QKV))),
        scratch_shapes=[pltpu.VMEM((tokens, LANES), f32), pltpu.VMEM((tokens, LANES), f32)],
        compiler_params=params(12),
        cost_estimate=cost(4),
        name="attend_back",
    )(qkv, qkv, qkv, d_mix, mixed, mask, rope)


def back_body(s_ref, dqkv_ref, du_ref, vec_ref, *refs):
    n_refs, refs = refs[:N_SHARD], refs[N_SHARD:]
    w_refs, refs = refs[:N_REP], refs[N_REP:]
    own_ref, sent_refs, sum_ref = refs[0], refs[1:N_SHARD], refs[N_SHARD]
    rows = n_refs[0].shape[0]
    for i in range(0, N_REP, 2):
        cols = slice(i * LANES, (i + 2) * LANES)
        weights = jnp.concatenate([w_refs[i][:, : QKV + UP], w_refs[i + 1][:, : QKV + UP]], axis=0)
        d_one = contract_cols(dqkv_ref[...], weights[:, :QKV])
        d_two = contract_cols(du_ref[...], weights[:, QKV:])
        scaled = d_one * vec_ref[0:1, cols] + d_two * vec_ref[2:3, cols]
        own_ref[:, cols] = scaled[:rows]
        sums = [jnp.sum(d, axis=0, keepdims=True) for d in (d_one, d_two)]
        turned = [jnp.zeros_like(sums[0])] * 2
        for k in range(N_SHARD):
            at = slice(k * rows, (k + 1) * rows)
            if k:
                sent_refs[k - 1][:, cols] = scaled[at].astype(bf16)
            normed = n_refs[k][:, cols].astype(f32)
            turned = [
                t + jnp.sum(d[at] * normed, axis=0, keepdims=True)
                for t, d in zip(turned, (d_one, d_two))
            ]
        sum_ref[0:1, cols] = turned[0]
        sum_ref[1:2, cols] = sums[0]
        sum_ref[2:3, cols] = turned[1]
        sum_ref[3:4, cols] = sums[1]


def middle_body(s_ref, mix_ref, act_ref, whole_ref, last_ref, x_ref, dy_ref, slope_ref, *refs):
    down_refs, refs = refs[:N_REP], refs[N_REP:]
    own_ref, sent_refs = refs[0], refs[1:N_SHARD]
    rows = x_ref.shape[0]
    total = plain_dot(mix_ref[...], whole_ref[...])
    for i in range(0, N_REP, 2):
        weights = jnp.concatenate([down_refs[i][...], down_refs[i + 1][...]], axis=0)
        total = total + plain_dot(act_ref[:, i * LANES : (i + 2) * LANES], weights)
    own_ref[...] = x_ref[...] + total[:rows] + last_ref[0:1, :]
    for k in range(1, N_SHARD):
        sent_refs[k - 1][...] = total[k * rows : (k + 1) * rows].astype(bf16)
    hidden_body(s_ref, dy_ref, *down_refs, slope_ref, whole_ref, *refs[N_SHARD:])


def terms_body(
    s_ref, h_ref, dqkv_ref, mix_ref, dy_ref, norm_ref, qkv_sum_ref, up_sum_ref, cot_ref, keep_ref, sent_ref, vec_ref, g_ref
):
    half = keep_ref.shape[0]
    keep_ref[:, :QKV] = contract_rows(h_ref[:, :half], dqkv_ref[...])
    sent_ref[:, :QKV] = contract_rows(h_ref[:, half:], dqkv_ref[...]).astype(bf16)
    g_ref[...] = contract_rows(mix_ref[...], dy_ref[...])
    vec_ref[...] = jnp.zeros_like(vec_ref)
    vec_ref[0:4, :] = norm_ref[0:4, :]
    for row, block, at in bias_places(s_ref):
        ref, at = (qkv_sum_ref, at) if at < QKV else (up_sum_ref, at - QKV)
        vec_ref[row : row + 1, lane_block(block)] = ref[0:1, at : at + LANES]
    rows = OUT // N_REP
    for i in range(N_REP):
        here = slice(i * LANES, (i + 1) * LANES)
        cot = cot_ref[0:1, lane_block(s_ref[ORDER + i])]
        vec_ref[7:8, here] = cot
        vec_ref[12:13, here] = cot
        ref = keep_ref if i < N_REP // 2 else sent_ref
        base = i * LANES % half
        found = g_ref[row_block(s_ref[ORDER + i], rows), :]
        for c in range(D // OUT):
            ref[base + c * rows : base + (c + 1) * rows, QKV : QKV + OUT] = found[
                :, c * OUT : (c + 1) * OUT
            ].astype(ref.dtype)
        ref[base : base + LANES, QKV + OUT :] = vec_ref[:, here].T.astype(ref.dtype)


def mlp_body(s_ref, act_ref, dy_ref, h_ref, du_ref, keep_ref, sent_ref):
    half = keep_ref.shape[0]
    for left, right, at in ((act_ref, dy_ref, 0), (h_ref, du_ref, D)):
        cols = slice(at, at + right.shape[1])
        sent_ref[:, cols] = contract_rows(left[:, half:], right[...]).astype(bf16)
        keep_ref[:, cols] = contract_rows(left[:, :half], right[...])


def fold_body(s_ref, *refs):
    up_refs, refs = refs[:4], refs[4:]
    qkv_refs, refs = refs[:4], refs[4:]
    own_ref, sent_refs, out_ref, up_sum, qkv_sum = refs[0], refs[1:4], refs[4], refs[5], refs[6]
    for some, total, first in ((up_refs, up_sum, D), (qkv_refs, qkv_sum, 0)):
        total[...] = sum(ref[:, first:].astype(f32) for ref in some)
    rows = own_ref.shape[0]
    for k in range(N_SHARD):
        at = row_block(s_ref[NEAR + k], rows)
        ref = own_ref if k == 0 else sent_refs[k - 1]
        ref[:, :QKV] = qkv_sum[at, :QKV].astype(ref.dtype)
        ref[:, QKV : QKV + UP] = up_sum[at, :].astype(ref.dtype)
        ref[:, QKV + UP :] = qkv_sum[at, QKV + OUT :].astype(ref.dtype)
    for c in range(D // OUT):
        out_ref[:, c * OUT : (c + 1) * OUT] = qkv_sum[c * rows : (c + 1) * rows, QKV : QKV + OUT]


def adam_body(s_ref, *refs):
    got, refs = refs[:N_SHARD], refs[N_SHARD:]
    states, vec_state, refs = (refs[0:3], refs[3:6]), refs[6:9], refs[9:]
    results, vec_result, refs = (refs[0:4], refs[4:8]), refs[8:12], refs[12:]
    all_ref, turn_ref = refs
    for k in range(N_SHARD):
        all_ref[k] = got[k][...].astype(f32)
    count, cols = vec_state[0].shape
    turn_ref[...] = jnp.zeros_like(turn_ref)
    turn_ref[:cols, :] = sum(all_ref[k, :, QKV + UP :] for k in range(N_SHARD))
    turn_ref[...] = turn_ref[...].T
    grad = turn_ref[:count, :cols]
    vec_result[0][...] = grad
    new = adam_update(vec_state[0][...], grad, vec_state[1][...], vec_state[2][...], LR_VECTOR, 0.0)
    for ref, value in zip(vec_result[1:], new):
        ref[...] = value
    first = 0
    for state, result in zip(states, results):
        for c in range(state[0].shape[1] // (N_SHARD * LANES)):
            for t in range(N_SHARD):
                grad = all_ref[s_ref[NEAR + t], :, first : first + LANES]
                at = slice((c * N_SHARD + t) * LANES, (c * N_SHARD + t + 1) * LANES)
                result[0][:, at] = grad
                new = adam_update(
                    state[0][:, at], grad, state[1][:, at], state[2][:, at], LR_MATRIX, WEIGHT_DECAY
                )
                for ref, value in zip(result[1:], new):
                    ref[:, at] = value
            first += LANES


def finish_body(s_ref, own_ref, r1_ref, r2_ref, r3_ref, x_ref, cot_ref, o_ref, e_ref):
    total = own_ref[...] + r1_ref[...].astype(f32) + r2_ref[...].astype(f32) + r3_ref[...].astype(f32)
    for i in range(N_REP):
        e_ref[:, lane_block(s_ref[ORDER + i])] = total[:, i * LANES : (i + 1) * LANES]
    x = x_ref[...]
    center = x - jnp.mean(x, axis=-1, keepdims=True)
    inv_std = lax.rsqrt(jnp.mean(center * center, axis=-1, keepdims=True) + LN_EPS)
    normed = center * inv_std
    scaled = e_ref[...]
    o_ref[...] = cot_ref[...] + inv_std * (
        scaled
        - jnp.mean(scaled, axis=-1, keepdims=True)
        - normed * jnp.mean(scaled * normed, axis=-1, keepdims=True)
    )


def to_shards(values):
    return [hop(values[k - 1], "shard", N_SHARD, k) for k in range(1, N_SHARD)]


def to_chips(values):
    return [hop(values[k - 1], "rep", N_REP, 2 * k) for k in range(1, 4)]


def gather_chips(own):
    near = [own] + to_chips([own] * 3)
    return near + [hop(piece, "rep", N_REP, 1) for piece in near]


def sum_rep(keep, got, *earlier):
    parts = [keep[k] + got[k].astype(f32) for k in range(4)]
    sent = [part.astype(bf16) for part in parts[1:]]
    if earlier:
        sent = [after(part, *earlier) for part in sent]
    return [parts[0]] + to_chips(sent)


def after(value, *others):
    return lax.optimization_barrier((value,) + others)[0]


def shards(
    block_in,
    cotangent,
    segments,
    qkv_weight,
    out_weight,
    up_weight,
    down_weight,
    vectors,
    first_qkv,
    first_out,
    first_up,
    first_down,
    first_vec,
    second_qkv,
    second_out,
    second_up,
    second_down,
    second_vec,
):
    tok_count = block_in.shape[0]
    rep = lax.axis_index("rep")
    shard = lax.axis_index("shard")
    seq_len = tok_count * N_SHARD
    rows = qkv_weight.shape[0]
    units = down_weight.shape[0]
    n_vec, cols = vectors.shape
    masks = np.array([0, 2, 4, 6, 1, 3, 5, 7], np.int32)
    spots = np.argsort(masks)
    device = np.arange(N_REP)
    places = spots[device[:, None] ^ device[None, :]].astype(np.int32)
    orders = (device[:, None] ^ masks[None, :]).astype(np.int32)
    near = shard ^ jnp.arange(N_SHARD, dtype=jnp.int32)
    table = jnp.asarray(np.concatenate([orders, places], axis=1))
    scalars = jnp.concatenate(
        [lax.dynamic_index_in_dim(table, rep, 0, keepdims=False), near, shard[None]]
    ).astype(jnp.int32)

    share = HEAD // rows
    pair = LANES // HEAD
    moves = []
    for at in range(N_REP * N_SHARD):
        head, part = at // share, at % share
        owner = (head // pair) % N_SHARD
        local = (head // (pair * N_SHARD)) * pair + head % pair
        moves.append((at, (local * share + part) * N_SHARD + owner))

    own_cols = [((rows, QKV + UP + LANES), bf16)] * N_SHARD
    square = pltpu.VMEM((LANES, LANES), f32)
    packed = single(
        pack_body, own_cols, scalars, [qkv_weight, up_weight, vectors], 1, "pack", [square]
    )
    got_cols = to_shards(packed[1:])
    out_rows = lax.ppermute(out_weight.astype(bf16), ("rep", "shard"), moves)
    down_own = down_weight.astype(bf16)
    (normed_own,) = single(
        norm_body,
        [((tok_count, D), bf16)],
        scalars,
        [block_in],
        1,
        "norm",
        [pltpu.VMEM((tok_count, D), f32)],
    )
    (in_rows,) = single(
        join_body,
        [((N_SHARD * rows, QKV + UP + OUT + LANES), bf16)],
        scalars,
        [packed[0], *got_cols[:2], after(got_cols[2], normed_own), out_rows],
        1,
        "join",
    )
    normed = [normed_own] + to_shards([after(normed_own, *got_cols)] * 3)
    pieces = [in_rows] + to_chips([in_rows, in_rows, after(in_rows, normed[1])])
    pieces = pieces + [hop(after(piece, normed[2], normed[3]), "rep", N_REP, 1) for piece in pieces]
    downs = [down_own] + to_chips([after(down_own, *pieces[1:4])] * 3)
    dy_own = cotangent.astype(bf16)

    rope_parts = jnp.asarray(rope_lanes(seq_len)).reshape(N_SHARD, tok_count, 3 * LANES)
    rope = jnp.concatenate(
        [lax.dynamic_index_in_dim(rope_parts, near[k], 0, keepdims=False) for k in range(N_SHARD)]
    )
    seg_row = jnp.concatenate(
        [lax.dynamic_slice(segments[0], (near[k] * tok_count,), (tok_count,)) for k in range(N_SHARD)]
    )
    positions = (near[:, None] * tok_count + jnp.arange(tok_count)[None, :]).reshape(seq_len)
    allowed = (seg_row[:, None] == seg_row[None, :]) & (positions[None, :] <= positions[:, None])
    mask = jnp.where(allowed, 0.0, HIDDEN).astype(f32)

    out_whole, h_one, h_two, qkv16, act16, slope, vec_rel, last = front(
        scalars, normed, pieces, rope
    )
    block16 = ((tok_count, D), bf16)
    block32 = ((tok_count, D), f32)
    half = D // 2
    downs = downs + [hop(after(piece, qkv16), "rep", N_REP, 1) for piece in downs]
    dys = to_shards([after(dy_own, *pieces[4:])] * 3)
    dy_all = jnp.concatenate([after(dy_own, qkv16)] + dys, axis=0)
    mixed16 = mix_heads(qkv16, mask)
    out_own, s1, s2, s3, dy_seq, d_mixed16, d_up16, up_sum = single(
        middle_body,
        [
            block32,
            block16,
            block16,
            block16,
            ((seq_len, D), bf16),
            ((seq_len, OUT), bf16),
            ((seq_len, UP), bf16),
            ((8, UP), f32),
        ],
        scalars,
        [mixed16, act16, out_whole, last, block_in, dy_all, slope, *downs],
        2,
        "middle",
    )
    out_got = [hop(s1, "shard", N_SHARD, 1), hop(s2, "shard", N_SHARD, 2)]

    mlp_keep, mlp_sent = single(
        mlp_body,
        [((half, D + UP), f32), ((half, D + UP), bf16)],
        scalars,
        [act16, dy_seq, h_two, d_up16],
        1,
        "mlp",
    )
    mlp_got = hop(mlp_sent.reshape(4, LANES, D + UP), "rep", N_REP, 1)
    mlp_parts = sum_rep(mlp_keep.reshape(4, LANES, D + UP), mlp_got)
    d_mixed16 = after(d_mixed16, mlp_got)
    d_qkv16, qkv_sum = attend_back(qkv16, d_mixed16, mixed16, mask, rope)
    out_got.append(hop(after(s3, d_qkv16), "shard", N_SHARD, 3))
    d_qkv16 = after(d_qkv16, *out_got[:2])
    h_one = after(h_one, out_got[2], *mlp_parts[1:])

    e_own, *e_sent, norm_sum = single(
        back_body,
        [block32, block16, block16, block16, ((8, D), f32)],
        scalars,
        [d_qkv16, d_up16, vec_rel, *normed, *pieces],
        1,
        "back",
    )
    cot_sum = jnp.sum(cotangent, axis=0, keepdims=True)
    wide = QKV + OUT + LANES
    qkv_keep, qkv_sent = single(
        terms_body,
        [((half, wide), f32), ((half, wide), bf16)],
        scalars,
        [h_one, d_qkv16, mixed16, dy_seq, norm_sum, qkv_sum, up_sum, cot_sum],
        4,
        "terms",
        [pltpu.VMEM((LANES, D), f32), pltpu.VMEM((OUT, D), f32)],
    )
    qkv_got = hop(qkv_sent.reshape(4, LANES, wide), "rep", N_REP, 1)
    qkv_parts = sum_rep(qkv_keep.reshape(4, LANES, wide), qkv_got, *mlp_parts[1:])
    e_got = [hop(e_sent[0], "shard", N_SHARD, 1), hop(e_sent[1], "shard", N_SHARD, 2)]
    e_got.append(hop(after(e_sent[2], e_got[0]), "shard", N_SHARD, 3))
    narrow = (rows, QKV + UP + LANES)
    g_own, g1, g2, g3, out_sum = single(
        fold_body,
        [(narrow, f32), (narrow, bf16), (narrow, bf16), (narrow, bf16), ((rows, D), f32)],
        scalars,
        [*mlp_parts, after(qkv_parts[0], *e_got[:2]), *qkv_parts[1:]],
        1,
        "fold",
        [pltpu.VMEM((LANES, UP), f32), pltpu.VMEM((LANES, wide), f32)],
    )
    g_got = to_shards([g1, g2, g3])
    grad_out = lax.ppermute(out_sum, ("rep", "shard"), [(b, a) for a, b in moves])
    block_out = out_own + out_got[0].astype(f32) + out_got[1].astype(f32) + out_got[2].astype(f32)
    grad_down = sum(part[:, :D].astype(f32) for part in mlp_parts)
    (grad_input,) = single(
        finish_body,
        [block32],
        scalars,
        [e_own, *e_got, block_in, cotangent],
        2,
        "finish",
        [pltpu.VMEM((tok_count, D), f32)],
    )
    qkv_shape = (qkv_weight.shape, f32)
    up_shape = (up_weight.shape, f32)
    vec_shape = (vectors.shape, f32)
    (
        grad_qkv,
        new_qkv,
        new_first_qkv,
        new_second_qkv,
        grad_up,
        new_up,
        new_first_up,
        new_second_up,
        grad_vec,
        new_vec,
        new_first_vec,
        new_second_vec,
    ) = single(
        adam_body,
        [qkv_shape] * 4 + [up_shape] * 4 + [vec_shape] * 4,
        scalars,
        [
            after(g_own, e_got[2]),
            *g_got,
            qkv_weight,
            first_qkv,
            second_qkv,
            up_weight,
            first_up,
            second_up,
            vectors,
            first_vec,
            second_vec,
        ],
        3,
        "adam",
        [pltpu.VMEM((N_SHARD,) + narrow, f32), square],
    )

    new_out, new_first_out, new_second_out = adam_update(
        out_weight, grad_out, first_out, second_out, LR_MATRIX, WEIGHT_DECAY
    )
    new_down, new_first_down, new_second_down = adam_update(
        down_weight, grad_down, first_down, second_down, LR_MATRIX, WEIGHT_DECAY
    )
    return (
        block_out,
        grad_input,
        grad_qkv,
        grad_out,
        grad_up,
        grad_down,
        grad_vec,
        new_qkv,
        new_out,
        new_up,
        new_down,
        new_vec,
        new_first_qkv,
        new_first_out,
        new_first_up,
        new_first_down,
        new_first_vec,
        new_second_qkv,
        new_second_out,
        new_second_up,
        new_second_down,
        new_second_vec,
    )


def solution(mesh):
    aligned = mesh.shape["rep"] == N_REP and mesh.shape["shard"] == N_SHARD
    return jax.shard_map(
        shards if aligned else general,
        mesh=mesh,
        in_specs=(
            P(("rep", "shard"), None),
            P(("rep", "shard"), None),
            P("rep", None),
            P(("rep", "shard"), None),
            P(("rep", "shard"), None),
            P(("rep", "shard"), None),
            P(("rep", "shard"), None),
            P(None, ("rep", "shard")),
            P(("rep", "shard"), None),
            P(("rep", "shard"), None),
            P(("rep", "shard"), None),
            P(("rep", "shard"), None),
            P(None, ("rep", "shard")),
            P(("rep", "shard"), None),
            P(("rep", "shard"), None),
            P(("rep", "shard"), None),
            P(("rep", "shard"), None),
            P(None, ("rep", "shard")),
        ),
        out_specs=(
            P(("rep", "shard"), None),
            P(("rep", "shard"), None),
            P(("rep", "shard"), None),
            P(("rep", "shard"), None),
            P(("rep", "shard"), None),
            P(("rep", "shard"), None),
            P(None, ("rep", "shard")),
            P(("rep", "shard"), None),
            P(("rep", "shard"), None),
            P(("rep", "shard"), None),
            P(("rep", "shard"), None),
            P(None, ("rep", "shard")),
            P(("rep", "shard"), None),
            P(("rep", "shard"), None),
            P(("rep", "shard"), None),
            P(("rep", "shard"), None),
            P(None, ("rep", "shard")),
            P(("rep", "shard"), None),
            P(("rep", "shard"), None),
            P(("rep", "shard"), None),
            P(("rep", "shard"), None),
            P(None, ("rep", "shard")),
        ),
        check_vma=False,
    )
```
